256 devices in a mesh: gx: 16 (over z_hi, y), gy: 16 (over x, z_lo, core).
Axes of the slice: x: 4, y: 4, z: 8 (z_hi: 4, z_lo: 2; z = z_hi * 2 + z_lo), core: 2. Of those that a mesh axis runs over, the one named last changes fastest.
Arguments:
- prec_pops: float32 [27, 64, 128, 256], P(None, 'gx', 'gy'), may hold values from 0 to 1, as said below
- main_pops: float32 [27, 128, 256, 256], P(None, 'gx', 'gy'), may hold values from 0 to 1, as said below
- cell_type: int32 [128, 256, 256], P('gx', 'gy'), may hold values from 0 to 2, as said below
- rates: float32 [27], replicated, may hold values from 0.7 to 1.8
Outputs:
- prec_next: float32 [27, 64, 128, 256], P(None, 'gx', 'gy')
- main_next: float32 [27, 128, 256, 256], P(None, 'gx', 'gy')
The draws below stay inside these ranges and needn't reach their ends.
Inputs may be any that keep to these rules, and one draw needn't show every extreme that they name: `prec_pops`: every population is positive; the populations of a cell sum to between 0.6 and 1.5. `main_pops`: every population is positive; the populations of a cell sum to between 0.6 and 1.5. `cell_type`: the lowest one to three cells of every column are solid (1); above them cells are fluid (0) or turbine disk (2).
All inputs are finite; a program needn't handle non-finite values.
Results may differ from the reference program's by a relative error of at most 0.000076.
Values sent between devices are 32-bit elements; how exact they have to be, the bound alone decides.
A program may use at most 128 MiB of HBM per device.

```python
import math
import jax
import jax.numpy as jnp
import numpy as np
from jax import lax

NZ = 256
NXP = 64
NYP = 128
NXM = 128
NYM = 256


def draw_populations(key, extent_x, extent_y, depth):
    keys = jax.random.split(key, 5)
    shape = (extent_x, extent_y, depth)
    density = jax.random.uniform(keys[0], shape, jnp.float32, 0.9, 1.1)
    flow_x = jax.random.uniform(keys[1], shape, jnp.float32, -0.08, 0.08)
    flow_y = jax.random.uniform(keys[2], shape, jnp.float32, -0.08, 0.08)
    flow_z = jax.random.uniform(keys[3], shape, jnp.float32, -0.08, 0.08)
    speeds = jnp.asarray(np.array([[step_x, step_y, step_z] for step_x in (-1, 0, 1) for step_y in (-1, 0, 1) for step_z in (-1, 0, 1)]), jnp.float32)
    weights = jnp.prod(jnp.where(speeds == 0, 2.0 / 3.0, 1.0 / 6.0), axis=1)
    projected = speeds[:, 0, None, None, None] * flow_x[None] + speeds[:, 1, None, None, None] * flow_y[None] + speeds[:, 2, None, None, None] * flow_z[None]
    square = flow_x * flow_x + flow_y * flow_y + flow_z * flow_z
    equilibrium = weights[:, None, None, None] * density[None] * (1.0 + 3.0 * projected + 4.5 * projected * projected - 1.5 * square[None])
    noise = jax.random.uniform(keys[4], (27,) + shape, jnp.float32, -1.0, 1.0)
    return (equilibrium * (1.0 + 0.3 * noise)).astype(jnp.float32)


def draw_prec_pops(key, part):
    return draw_populations(jax.random.fold_in(key, 11), NXP, NYP, NZ)


def draw_main_pops(key, part):
    return draw_populations(jax.random.fold_in(key, 23), NXM, NYM, NZ)


def draw_cell_type(key, part):
    keys = jax.random.split(jax.random.fold_in(key, 37), 2)
    terrain = jax.random.randint(keys[0], (NXM, NYM, 1), 1, 4)
    height = lax.broadcasted_iota(jnp.int32, (NXM, NYM, NZ), 2)
    solid = height < terrain
    disk = jax.random.randint(keys[1], (NXM, NYM, NZ), 0, 12) == 0
    return jnp.where(solid, 1, jnp.where(disk, 2, 0)).astype(jnp.int32)


def setup_inputs(seed: int = 0) -> dict:
    key_of = jax.random.split(jax.random.key(seed), 5)
    prec_pops = draw_prec_pops(jax.random.fold_in(key_of[4], 71), 0)
    main_pops = draw_main_pops(jax.random.fold_in(key_of[4], 71), 0)
    cell_type = draw_cell_type(jax.random.fold_in(key_of[4], 71), 0)
    rates = jnp.clip(jnp.exp(jax.random.uniform(key_of[3], (27,), jnp.float32, math.log(0.7), math.log(1.8))), 0.7, 1.8)
    return dict(prec_pops=prec_pops, main_pops=main_pops, cell_type=cell_type, rates=rates)


thrust_coef = 0.75
highest = lax.Precision.HIGHEST


def lattice_speeds():
    return np.array([[step_x, step_y, step_z] for step_x in (-1, 0, 1) for step_y in (-1, 0, 1) for step_z in (-1, 0, 1)])


def lattice_weights():
    speeds = lattice_speeds()
    return np.prod(np.where(speeds == 0, 2.0 / 3.0, 1.0 / 6.0), axis=1)


def relax_matrix(rates):
    single = np.array([[1.0, 1.0, 1.0], [-1.0, 0.0, 1.0], [1.0, 0.0, 1.0]])
    inverse = np.array([[0.0, -0.5, 0.5], [1.0, 0.0, -1.0], [0.0, 0.5, 0.5]])
    moments = jnp.asarray(np.kron(np.kron(single, single), single), jnp.float32)
    inverse_full = jnp.asarray(np.kron(np.kron(inverse, inverse), inverse), jnp.float32)
    return jnp.dot(inverse_full * rates[None, :], moments, precision=highest)


def collide(populations, relaxer):
    cell_count = populations.shape[1] * populations.shape[2] * populations.shape[3]
    flattened = populations.reshape(27, cell_count)
    speeds = jnp.asarray(lattice_speeds().T, jnp.float32)
    weights = jnp.asarray(lattice_weights(), jnp.float32)
    density = jnp.sum(flattened, axis=0)
    velocity = jnp.dot(speeds, flattened, precision=highest) / density[None, :]
    projected = jnp.dot(speeds.T, velocity, precision=highest)
    square = jnp.sum(velocity * velocity, axis=0)
    equilibrium = weights[:, None] * density[None, :] * (1.0 + 3.0 * projected + 4.5 * projected * projected - 1.5 * square[None, :])
    relaxed = flattened - jnp.dot(relaxer, flattened - equilibrium, precision=highest)
    return flattened, relaxed, density, velocity


def apply_cells(flattened, relaxed, density, velocity, cell_type):
    flags = cell_type.reshape(-1)[None, :]
    speeds_x = jnp.asarray(lattice_speeds()[:, 0], jnp.float32)
    weights = jnp.asarray(lattice_weights(), jnp.float32)
    drag = -0.5 * thrust_coef * density * velocity[0] * jnp.abs(velocity[0])
    relaxed = relaxed + jnp.where(flags == 2, 3.0 * (weights * speeds_x)[:, None] * drag[None, :], 0.0)
    return jnp.where(flags == 1, flattened[::-1], relaxed)


def stream_pull(extended, relaxed):
    extent_x = relaxed.shape[1]
    extent_y = relaxed.shape[2]
    pulled = []
    for direction in range(27):
        step_x = direction // 9 - 1
        step_y = (direction // 3) % 3 - 1
        step_z = direction % 3 - 1
        shifted = extended[direction, 1 - step_x:1 - step_x + extent_x, 1 - step_y:1 - step_y + extent_y]
        if step_z == 1:
            shifted = jnp.concatenate([relaxed[26 - direction, :, :, :1], shifted[:, :, :-1]], axis=2)
        elif step_z == -1:
            shifted = jnp.concatenate([shifted[:, :, 1:], relaxed[26 - direction, :, :, -1:]], axis=2)
        pulled.append(shifted)
    return jnp.stack(pulled)


def extend_whole(relaxed, lower, upper):
    joined = jnp.concatenate([lower[:, None], relaxed, upper[:, None]], axis=1)
    return jnp.concatenate([joined[:, :, -1:], joined, joined[:, :, :1]], axis=2)


def reference(prec_pops, main_pops, cell_type, rates):
    relaxer = relax_matrix(rates)
    unused, prec_flat, prec_density, prec_velocity = collide(prec_pops, relaxer)
    prec_relaxed = prec_flat.reshape(prec_pops.shape)
    main_flat, main_relax, main_density, main_velocity = collide(main_pops, relaxer)
    main_relaxed = apply_cells(main_flat, main_relax, main_density, main_velocity, cell_type).reshape(main_pops.shape)
    prec_next = stream_pull(extend_whole(prec_relaxed, prec_relaxed[:, -1], prec_relaxed[:, 0]), prec_relaxed)
    inlet = jnp.concatenate([prec_relaxed[:, -1], prec_relaxed[:, -1]], axis=1)
    main_next = stream_pull(extend_whole(main_relaxed, inlet, main_relaxed[:, -1]), main_relaxed)
    return prec_next, main_next
```

```python
import functools

import jax
import jax.numpy as jnp
from jax import lax
from jax.experimental import pallas as pl
from jax.experimental.pallas import tpu as pltpu
from jax.sharding import PartitionSpec as P

MESH = pl.DeviceIdType.MESH
F32 = jnp.float32
LANES = 128
ROWS = 8
TOP = 8


def scale_of(moment):
    a, b, e = moment // 9, moment // 3 % 3, moment % 3
    return (0.5 if a else 1.0) * (0.5 if b else 1.0) * (0.5 if e else 1.0)


def third_of(moment):
    a, b, e = moment // 9, moment // 3 % 3, moment % 3
    return (1.0 / 3.0) ** ((a == 2) + (b == 2) + (e == 2))


def axis_triples():
    for stride in (9, 3, 1):
        for base in range(27):
            if base // stride % 3 == 0:
                yield base, base + stride, base + 2 * stride


def to_moments(f):
    m = list(f)
    for low, mid, high in axis_triples():
        total = m[high] + m[low]
        m[low], m[mid], m[high] = total + m[mid], m[high] - m[low], total
    return m


def to_populations(m):
    g = list(m)
    for low, mid, high in axis_triples():
        g[low], g[mid], g[high] = g[high] - g[mid], g[low] - (g[high] + g[high]), g[high] + g[mid]
    return g


def collide(f, keep, gain, disk=None):
    m = to_moments(f)
    rho, jx, jy, jz = m[0], m[9], m[3], m[1]
    inverse = 1.0 / rho
    ux, uy, uz = jx * inverse, jy * inverse, jz * inverse
    qx, qy, qz = jx * ux, jy * uy, jz * uz
    third = rho * (1.0 / 3.0)
    ex, ey, ez = third + qx, third + qy, third + qz
    exy, exz, eyz = ex + qy, ex + qz, ey + qz
    even = {18: ex, 6: ey, 2: ez, 24: exy, 20: exz, 8: eyz, 26: exy + qz}
    odd = {}
    for k in range(27):
        a, b, e = k // 9, k // 3 % 3, k % 3
        ones = (a == 1) + (b == 1) + (e == 1)
        if ones == 1:
            odd[k] = jx if a == 1 else jy if b == 1 else jz
        elif ones == 2:
            odd[k] = jx * uy if e != 1 else jx * uz if b != 1 else jy * uz
    out = [None] * 27
    shared = {}
    for k in range(27):
        a, b, e = k // 9, k // 3 % 3, k % 3
        if k == 0:
            out[k] = rho
        elif k in (9, 3, 1):
            out[k] = odd[k] * 0.5
        elif k == 13:
            out[k] = keep(k) * m[k]
        elif k in even:
            out[k] = keep(k) * m[k] + gain(k) * even[k]
        else:
            pair = (a == 1, b == 1, e == 1)
            if pair not in shared:
                shared[pair] = odd[k]
            out[k] = keep(k) * m[k] + gain(k) * shared[pair]
    if disk is not None:
        drag = jnp.where(disk, (-0.5 * 0.75) * jx * jnp.abs(ux), 0.0)
        out[9] = out[9] + drag * 0.5
        side = drag * (0.25 / 3.0)
        out[15] = out[15] + side
        out[11] = out[11] + side
        out[17] = out[17] + drag * (0.125 / 9.0)
    return to_populations(out)


def even_orders(k):
    a, b, e = k // 9, k // 3 % 3, k % 3
    return a != 1 and b != 1 and e != 1


def rows_across(g, i, part, row):
    planes, ztiles, pitch = g.shape[2:5]
    flat = g.reshape(27 * planes * ztiles * pitch, LANES)
    return flat, pl.ds(((i * planes + 1) * ztiles + part * ROWS) * pitch + row, ROWS, stride=pitch)


def load_across(g, i, part, row):
    flat, rows = rows_across(g, i, part, row)
    return flat[rows, :]


def store_across(g, i, part, row, value):
    flat, rows = rows_across(g, i, part, row)
    flat[rows, :] = value


def exchange(
    size,
    rates,
    prec_hbm,
    main_hbm,
    cell_hbm,
    main_g,
    prec_g,
    main_in,
    prec_in,
    cell_in,
    table,
    main_out_y,
    main_got_y,
    main_out_c,
    main_got_c,
    prec_out_y,
    prec_got_y,
    prec_out_c,
    prec_got_c,
    load_sem,
    cell_sem,
    main_send,
    main_recv,
    prec_send,
    prec_recv,
    extra_send,
):
    nx, ny = size
    gx, gy = lax.axis_index("gx"), lax.axis_index("gy")
    main_x, main_y = main_in.shape[1], main_in.shape[2]
    prec_x, prec_y = prec_in.shape[1], prec_in.shape[2]
    ztiles = main_g.shape[3]
    first, last = gx == 0, gx == nx - 1
    east, west = lax.rem(gx + 1, nx), lax.rem(gx + nx - 1, nx)
    north, south = lax.rem(gy + 1, ny), lax.rem(gy + ny - 1, ny)
    half = ny // 2

    barrier = pltpu.get_barrier_semaphore()
    for other in (
        (west, gy), (east, gy), (gx, south), (gx, north),
        (west, south), (west, north), (east, south), (east, north),
    ):
        pl.semaphore_signal(barrier, inc=1, device_id=other, device_id_type=MESH)

    @pl.when(first)
    def _():
        for block in (2 * gy, 2 * gy + 1, 2 * gy + ny - 1, 2 * gy + 2):
            pl.semaphore_signal(
                barrier, inc=1, device_id=(nx - 1, lax.rem(block, ny)), device_id_type=MESH
            )

    def main_load(x):
        return pltpu.make_async_copy(main_hbm.at[:, x], main_in.at[:, x], load_sem.at[x])

    def prec_load(x):
        return pltpu.make_async_copy(prec_hbm.at[:, x], prec_in.at[:, x], load_sem.at[main_x + x])

    cell_load = pltpu.make_async_copy(cell_hbm, cell_in, cell_sem)
    cell_load.start()
    main_load(main_x - 1).start()
    main_load(0).start()
    prec_load(prec_x - 1).start()
    prec_load(0).start()
    for x in range(1, main_x - 1):
        main_load(x).start()
    for x in range(1, prec_x - 1):
        prec_load(x).start()

    for k in range(27):
        rate = rates[k]
        kept = scale_of(k) * (1.0 - rate)
        table[k] = jnp.full((ROWS, LANES), kept, F32)
        factor = third_of(k) * (3.0 if even_orders(k) else 1.0)
        table[27 + k] = jnp.full((ROWS, LANES), scale_of(k) * factor * rate, F32)

    def keep(k):
        return table[k]

    def gain(k):
        return table[27 + k]

    def tile_of(step):
        row = pl.multiple_of(lax.div(step, ztiles) * ROWS, ROWS)
        z = lax.rem(step, ztiles)
        return row, z, pl.multiple_of(z * LANES, LANES)

    def main_plane(x):
        def body(step, carry):
            row, z, lane = tile_of(step)
            rows, lanes = pl.ds(row, ROWS), pl.ds(lane, LANES)
            flags = cell_in[x, rows, lanes]
            g = collide([main_in[i, x, rows, lanes] for i in range(27)], keep, gain, flags == 2)
            solid = flags == 1
            for i in range(27):
                value = jnp.where(solid, main_in[26 - i, x, rows, lanes], g[i])
                main_g[i // 9, i % 9, x + 1, z, pl.ds(pl.multiple_of(TOP + row, ROWS), ROWS), :] = value
            return carry

        lax.fori_loop(0, main_y // ROWS * ztiles, body, 0)

    def prec_plane(x):
        def body(step, carry):
            row, z, lane = tile_of(step)
            rows, lanes = pl.ds(row, ROWS), pl.ds(lane, LANES)
            g = collide([prec_in[i, x, rows, lanes] for i in range(27)], keep, gain)
            for i in range(27):
                prec_g[i // 9, i % 9, x + 1, z, pl.ds(pl.multiple_of(TOP + row, ROWS), ROWS), :] = g[i]
            return carry

        lax.fori_loop(0, prec_y // ROWS * ztiles, body, 0)

    def remote(src, dst, send, recv, device):
        return pltpu.make_async_remote_copy(
            src_ref=src, dst_ref=dst, send_sem=send, recv_sem=recv, device_id=device, device_id_type=MESH
        )

    def x_face(g, count, rows, east_side, send, recv):
        inner = pl.ds(TOP, rows)
        if east_side:
            return remote(g.at[2, :, count, :, inner], g.at[2, :, 0, :, inner], send.at[0], recv.at[0], (east, gy))
        return remote(g.at[0, :, 1, :, inner], g.at[0, :, count + 1, :, inner], send.at[1], recv.at[1], (west, gy))

    main_east = x_face(main_g, main_x, main_y, True, main_send, main_recv)
    main_west = x_face(main_g, main_x, main_y, False, main_send, main_recv)
    prec_east = x_face(prec_g, prec_x, prec_y, True, prec_send, prec_recv)
    prec_west = x_face(prec_g, prec_x, prec_y, False, prec_send, prec_recv)

    def inlet(target):
        place = pl.ds(pl.multiple_of(TOP + lax.rem(gy, 2) * prec_y, ROWS), prec_y)
        return remote(
            prec_g.at[2, :, prec_x, :, pl.ds(TOP, prec_y)],
            main_g.at[2, :, 0, :, place],
            extra_send.at[target],
            main_recv.at[0],
            (0, lax.div(gy, 2) + target * half),
        )

    main_load(main_x - 1).wait()
    cell_load.wait()
    main_plane(main_x - 1)
    pl.semaphore_wait(barrier, jnp.where(last, 12, 8))

    @pl.when(jnp.logical_not(last))
    def _():
        main_east.start()

    main_load(0).wait()
    main_plane(0)

    @pl.when(jnp.logical_not(first))
    def _():
        main_west.start()

    prec_load(prec_x - 1).wait()
    prec_plane(prec_x - 1)
    prec_east.start()

    @pl.when(last)
    def _():
        inlet(0).start()
        inlet(1).start()

    prec_load(0).wait()
    prec_plane(0)
    prec_west.start()

    def prec_rest(x, carry):
        prec_load(x).wait()
        prec_plane(x)
        return carry

    lax.fori_loop(1, prec_x - 1, prec_rest, 0)

    def pack(g, count, rows, out_y, out_c):
        for side in range(2):
            row = TOP + rows - 1 if side == 0 else TOP
            for a in range(3):
                for e in range(3):
                    i = 9 * a + (6 if side == 0 else 0) + e
                    for part in range(count * ztiles // ROWS):
                        out_y[side, 3 * a + e, pl.ds(part * ROWS, ROWS), :] = load_across(g, i, part, row)
        for corner in range(4):
            side, a, x = corner % 2, 2 if corner < 2 else 0, count if corner < 2 else 1
            row = TOP + rows - 1 if side == 0 else TOP
            for e in range(3):
                for z in range(ztiles):
                    out_c[corner, pl.ds(e * ztiles + z, 1), :] = g[a, (6 if side == 0 else 0) + e, x, z, pl.ds(row, 1), :]

    def y_copies(out_y, got_y, send, recv):
        return [
            remote(out_y.at[side], got_y.at[side], send.at[2 + side], recv.at[2 + side], (gx, (north, south)[side]))
            for side in range(2)
        ]

    def corner_copies(out_c, got_c, send, recv):
        return [
            remote(
                out_c.at[corner], got_c.at[corner], send.at[4 + corner], recv.at[4 + corner],
                (east if corner < 2 else west, (north, south)[corner % 2]),
            )
            for corner in range(4)
        ]

    def inlet_corner(corner, target):
        block = lax.rem(lax.div(gy + 1, 2), half) if corner == 0 else lax.rem(lax.div(gy, 2) + half - 1, half)
        return remote(
            prec_out_c.at[corner], main_got_c.at[corner], extra_send.at[2 + target], main_recv.at[4 + corner],
            (0, block + target * half),
        )

    pack(prec_g, prec_x, prec_y, prec_out_y, prec_out_c)
    prec_y_copies = y_copies(prec_out_y, prec_got_y, prec_send, prec_recv)
    prec_corners = corner_copies(prec_out_c, prec_got_c, prec_send, prec_recv)
    main_y_copies = y_copies(main_out_y, main_got_y, main_send, main_recv)
    main_corners = corner_copies(main_out_c, main_got_c, main_send, main_recv)
    odd = lax.rem(gy, 2) == 1
    for copy in prec_y_copies + prec_corners:
        copy.start()

    @pl.when(jnp.logical_and(last, odd))
    def _():
        inlet_corner(0, 0).start()
        inlet_corner(0, 1).start()

    @pl.when(jnp.logical_and(last, jnp.logical_not(odd)))
    def _():
        inlet_corner(1, 0).start()
        inlet_corner(1, 1).start()

    def main_rest(x, carry):
        main_load(x).wait()
        main_plane(x)
        return carry

    lax.fori_loop(1, main_x - 1, main_rest, 0)
    pack(main_g, main_x, main_y, main_out_y, main_out_c)
    for copy in main_y_copies:
        copy.start()

    @pl.when(jnp.logical_not(last))
    def _():
        main_corners[0].start()
        main_corners[1].start()

    @pl.when(jnp.logical_not(first))
    def _():
        main_corners[2].start()
        main_corners[3].start()

    def unpack(g, count, rows, got_y):
        for side in range(2):
            row = TOP - 1 if side == 0 else TOP + rows
            for a in range(3):
                for e in range(3):
                    i = 9 * a + (6 if side == 0 else 0) + e
                    for part in range(count * ztiles // ROWS):
                        store_across(g, i, part, row, got_y[side, 3 * a + e, pl.ds(part * ROWS, ROWS), :])

    def unpack_corner(g, count, rows, got_c, corner):
        side, a, x = corner % 2, 2 if corner < 2 else 0, 0 if corner < 2 else count + 1
        row = TOP - 1 if side == 0 else TOP + rows
        for e in range(3):
            for z in range(ztiles):
                g[a, (6 if side == 0 else 0) + e, x, z, pl.ds(row, 1), :] = got_c[corner, pl.ds(e * ztiles + z, 1), :]

    for side in range(2):
        prec_y_copies[side].wait_recv()
    unpack(prec_g, prec_x, prec_y, prec_got_y)
    for corner in range(4):
        prec_corners[corner].wait_recv()
        unpack_corner(prec_g, prec_x, prec_y, prec_got_c, corner)
    for side in range(2):
        main_y_copies[side].wait_recv()
    unpack(main_g, main_x, main_y, main_got_y)
    for corner in range(2):
        main_corners[corner].wait_recv()
        unpack_corner(main_g, main_x, main_y, main_got_c, corner)

    @pl.when(jnp.logical_not(last))
    def _():
        for corner in range(2, 4):
            main_corners[corner].wait_recv()
            unpack_corner(main_g, main_x, main_y, main_got_c, corner)

    prec_east.wait_recv()
    prec_west.wait_recv()
    main_east.wait_recv()

    @pl.when(jnp.logical_not(last))
    def _():
        main_west.wait_recv()

    for copy in [prec_east, prec_west, *prec_y_copies, *prec_corners, *main_y_copies]:
        copy.wait_send()

    @pl.when(jnp.logical_not(last))
    def _():
        for copy in (main_east, main_corners[0], main_corners[1]):
            copy.wait_send()

    @pl.when(jnp.logical_not(first))
    def _():
        for copy in (main_west, main_corners[2], main_corners[3]):
            copy.wait_send()

    @pl.when(last)
    def _():
        for target in range(2):
            inlet(target).wait_send()
            inlet_corner(0, target).wait_send()


def stream(nx, main_g, prec_g, prec_next, main_next, prec_out, main_out, prec_sem, main_sem):
    last = lax.axis_index("gx") == nx - 1

    def plane(g, out, count, rows, x, clamp):
        lane = lax.broadcasted_iota(jnp.int32, (ROWS, LANES), 1)
        low, high = lane == 0, lane == LANES - 1
        ztiles = g.shape[3]

        def body(step, carry):
            row = pl.multiple_of(step * ROWS, ROWS)
            for i in range(27):
                cx, cy, cz = i // 9 - 1, i // 3 % 3 - 1, i % 3 - 1
                source = x + 1 - cx
                if clamp and cx == -1:
                    source = jnp.where(last, jnp.minimum(source, count), source)
                tiles = [g[i // 9, i % 9, source, z, pl.ds(TOP - cy + row, ROWS), :] for z in range(ztiles)]
                if cz:
                    j = 26 - i
                    wall = 0 if cz == 1 else ztiles - 1
                    bounced = g[j // 9, j % 9, x + 1, wall, pl.ds(pl.multiple_of(TOP + row, ROWS), ROWS), :]
                    moved = [pltpu.roll(tile, 1 if cz == 1 else LANES - 1, 1) for tile in tiles]
                    if cz == 1:
                        tiles = [jnp.where(low, moved[z - 1] if z else bounced, moved[z]) for z in range(ztiles)]
                    else:
                        tiles = [
                            jnp.where(high, moved[z + 1] if z < ztiles - 1 else bounced, moved[z])
                            for z in range(ztiles)
                        ]
                for z in range(ztiles):
                    out[x, i, pl.ds(row, ROWS), pl.ds(z * LANES, LANES)] = tiles[z]
            return carry

        lax.fori_loop(0, rows // ROWS, body, 0)

    def run(g, out, dest, sem, clamp):
        count, rows = out.shape[0], out.shape[2]

        def copy(x):
            return pltpu.make_async_copy(out.at[x], dest.at[:, x], sem.at[x])

        def body(x, carry):
            plane(g, out, count, rows, x, clamp)
            copy(x).start()
            return carry

        lax.fori_loop(0, count, body, 0)
        return copy

    main_copy = run(main_g, main_out, main_next, main_sem, True)
    prec_copy = run(prec_g, prec_out, prec_next, prec_sem, False)
    for x in range(main_out.shape[0]):
        main_copy(x).wait()
    for x in range(prec_out.shape[0]):
        prec_copy(x).wait()


def solution(mesh):
    nx, ny = mesh.shape["gx"], mesh.shape["gy"]

    def shards(prec_pops, main_pops, cell_type, rates):
        main_x, main_y, depth = main_pops.shape[1:]
        prec_x, prec_y = prec_pops.shape[1:3]
        ztiles = depth // LANES
        main_shape = (3, 9, main_x + 2, ztiles, main_y + 2 * TOP, LANES)
        prec_shape = (3, 9, prec_x + 2, ztiles, prec_y + 2 * TOP, LANES)
        in_hbm = pl.BlockSpec(memory_space=pltpu.HBM)
        on_chip = pl.BlockSpec(memory_space=pltpu.VMEM)
        main_g, prec_g = pl.pallas_call(
            functools.partial(exchange, (nx, ny)),
            name="exchange",
            out_shape=(pltpu.VMEM(main_shape, F32), pltpu.VMEM(prec_shape, F32)),
            in_specs=[pl.BlockSpec(memory_space=pltpu.SMEM), in_hbm, in_hbm, in_hbm],
            out_specs=(on_chip, on_chip),
            scratch_shapes=[
                pltpu.VMEM(main_pops.shape, F32),
                pltpu.VMEM(prec_pops.shape, F32),
                pltpu.VMEM(cell_type.shape, jnp.int32),
                pltpu.VMEM((54, ROWS, LANES), F32),
                pltpu.VMEM((2, 9, main_x * ztiles, LANES), F32),
                pltpu.VMEM((2, 9, main_x * ztiles, LANES), F32),
                pltpu.VMEM((4, ROWS, LANES), F32),
                pltpu.VMEM((4, ROWS, LANES), F32),
                pltpu.VMEM((2, 9, prec_x * ztiles, LANES), F32),
                pltpu.VMEM((2, 9, prec_x * ztiles, LANES), F32),
                pltpu.VMEM((4, ROWS, LANES), F32),
                pltpu.VMEM((4, ROWS, LANES), F32),
                pltpu.SemaphoreType.DMA((main_x + prec_x,)),
                pltpu.SemaphoreType.DMA,
                pltpu.SemaphoreType.DMA((8,)),
                pltpu.SemaphoreType.DMA((8,)),
                pltpu.SemaphoreType.DMA((8,)),
                pltpu.SemaphoreType.DMA((8,)),
                pltpu.SemaphoreType.DMA((4,)),
            ],
            compiler_params=pltpu.CompilerParams(
                collective_id=0, has_side_effects=True, vmem_limit_bytes=24 * 1024 * 1024
            ),
        )(*(pltpu.with_memory_space_constraint(x, pltpu.HBM) for x in (rates, prec_pops, main_pops, cell_type)))
        prec_next, main_next = pl.pallas_call(
            functools.partial(stream, nx),
            name="stream",
            out_shape=(
                jax.ShapeDtypeStruct(prec_pops.shape, F32),
                jax.ShapeDtypeStruct(main_pops.shape, F32),
            ),
            in_specs=[on_chip, on_chip],
            out_specs=(in_hbm, in_hbm),
            scratch_shapes=[
                pltpu.VMEM((prec_x, 27, prec_y, depth), F32),
                pltpu.VMEM((main_x, 27, main_y, depth), F32),
                pltpu.SemaphoreType.DMA((prec_x,)),
                pltpu.SemaphoreType.DMA((main_x,)),
            ],
            compiler_params=pltpu.CompilerParams(vmem_limit_bytes=24 * 1024 * 1024),
        )(main_g, prec_g)
        return prec_next, main_next

    placed = (P(None, "gx", "gy", None), P(None, "gx", "gy", None), P("gx", "gy", None), P())
    return jax.shard_map(
        shards,
        mesh=mesh,
        in_specs=placed,
        out_specs=(P(None, "gx", "gy", None), P(None, "gx", "gy", None)),
        check_vma=False,
    )
```

```python
import functools

import jax
import jax.numpy as jnp
from jax import lax
from jax.experimental import pallas as pl
from jax.experimental.pallas import tpu as pltpu
from jax.sharding import PartitionSpec as P

MESH = pl.DeviceIdType.MESH
F32 = jnp.float32
LANES = 128
ROWS = 8
GROUP = 4
TOP = 8


def scale_of(moment):
    a, b, e = moment // 9, moment // 3 % 3, moment % 3
    return (0.5 if a else 1.0) * (0.5 if b else 1.0) * (0.5 if e else 1.0)


def third_of(moment):
    a, b, e = moment // 9, moment // 3 % 3, moment % 3
    return (1.0 / 3.0) ** ((a == 2) + (b == 2) + (e == 2))


def axis_triples():
    for stride in (9, 3, 1):
        for base in range(27):
            if base // stride % 3 == 0:
                yield base, base + stride, base + 2 * stride


def to_moments(f):
    m = list(f)
    for low, mid, high in axis_triples():
        total = m[high] + m[low]
        m[low], m[mid], m[high] = total + m[mid], m[high] - m[low], total
    return m


def to_populations(m):
    g = list(m)
    for low, mid, high in axis_triples():
        g[low], g[mid], g[high] = g[high] - g[mid], g[low] - (g[high] + g[high]), g[high] + g[mid]
    return g


def collide(f, keep, gain, disk=None):
    m = to_moments(f)
    rho, jx, jy, jz = m[0], m[9], m[3], m[1]
    inverse = 1.0 / rho
    ux, uy, uz = jx * inverse, jy * inverse, jz * inverse
    qx, qy, qz = jx * ux, jy * uy, jz * uz
    third = rho * (1.0 / 3.0)
    ex, ey, ez = third + qx, third + qy, third + qz
    exy, exz, eyz = ex + qy, ex + qz, ey + qz
    even = {18: ex, 6: ey, 2: ez, 24: exy, 20: exz, 8: eyz, 26: exy + qz}
    odd = {}
    for k in range(27):
        a, b, e = k // 9, k // 3 % 3, k % 3
        ones = (a == 1) + (b == 1) + (e == 1)
        if ones == 1:
            odd[k] = jx if a == 1 else jy if b == 1 else jz
        elif ones == 2:
            odd[k] = jx * uy if e != 1 else jx * uz if b != 1 else jy * uz
    out = [None] * 27
    shared = {}
    for k in range(27):
        a, b, e = k // 9, k // 3 % 3, k % 3
        if k == 0:
            out[k] = rho
        elif k in (9, 3, 1):
            out[k] = odd[k] * 0.5
        elif k == 13:
            out[k] = keep(k) * m[k]
        elif k in even:
            out[k] = keep(k) * m[k] + gain(k) * even[k]
        else:
            pair = (a == 1, b == 1, e == 1)
            if pair not in shared:
                shared[pair] = odd[k]
            out[k] = keep(k) * m[k] + gain(k) * shared[pair]
    if disk is not None:
        drag = jnp.where(disk, (-0.5 * 0.75) * jx * jnp.abs(ux), 0.0)
        out[9] = out[9] + drag * 0.5
        side = drag * (0.25 / 3.0)
        out[15] = out[15] + side
        out[11] = out[11] + side
        out[17] = out[17] + drag * (0.125 / 9.0)
    return to_populations(out)


def even_orders(k):
    a, b, e = k // 9, k // 3 % 3, k % 3
    return a != 1 and b != 1 and e != 1


def rows_across(g, i, part, row):
    planes, ztiles, pitch = g.shape[2:5]
    flat = g.reshape(27 * planes * ztiles * pitch, LANES)
    return flat, pl.ds(((i * planes + 1) * ztiles + part * ROWS) * pitch + row, ROWS, stride=pitch)


def load_across(g, i, part, row):
    flat, rows = rows_across(g, i, part, row)
    return flat[rows, :]


def store_across(g, i, part, row, value):
    flat, rows = rows_across(g, i, part, row)
    flat[rows, :] = value


def exchange(
    size,
    rates,
    prec_hbm,
    main_hbm,
    cell_hbm,
    main_g,
    prec_g,
    main_in,
    prec_in,
    cell_in,
    table,
    main_out_y,
    main_got_y,
    main_out_c,
    main_got_c,
    prec_out_y,
    prec_got_y,
    prec_out_c,
    prec_got_c,
    load_sem,
    cell_sem,
    main_send,
    main_recv,
    prec_send,
    prec_recv,
    inlet_send,
    inlet_c,
    main_relay,
    prec_relay,
    relay_recv,
):
    nx, ny = size
    gx, gy = lax.axis_index("gx"), lax.axis_index("gy")
    main_x, main_y = main_in.shape[1], main_in.shape[2]
    prec_x, prec_y = prec_in.shape[1], prec_in.shape[2]
    ztiles = main_g.shape[3]
    first, last = gx == 0, gx == nx - 1
    east, west = lax.rem(gx + 1, nx), lax.rem(gx + nx - 1, nx)
    north, south = lax.rem(gy + 1, ny), lax.rem(gy + ny - 1, ny)
    half = ny // 2

    place = lax.rem(gx, GROUP)
    up_source = jnp.logical_and(place == GROUP - 1, jnp.logical_not(last))
    down_source = jnp.logical_and(place == 0, jnp.logical_not(first))
    up_relay = jnp.logical_and(place == 0, gx + GROUP < nx)
    down_relay = jnp.logical_and(place == GROUP - 1, gx - GROUP >= 0)
    crossing = jnp.logical_or(up_source, down_source)
    relaying = jnp.logical_or(up_relay, down_relay)
    relay_from = jnp.where(up_relay, gx + GROUP - 1, gx - GROUP + 1)
    relay_to = jnp.where(up_relay, gx + GROUP, gx - GROUP)
    relay_of = jnp.where(up_source, gx - GROUP + 1, gx + GROUP - 1)
    relay_back = jnp.where(down_source, gx - GROUP, gx + GROUP)

    odd = lax.rem(gy, 2) == 1
    corner_block = jnp.where(odd, lax.rem(lax.div(gy + 1, 2), half), lax.rem(lax.div(gy, 2) + half - 1, half))
    inlet_targets = [lax.div(gy, 2), lax.div(gy, 2) + half, corner_block, corner_block + half]

    barrier = pltpu.get_barrier_semaphore()

    def greet(device):
        pl.semaphore_signal(barrier, inc=1, device_id=device, device_id_type=MESH)

    for other in (
        (west, gy), (east, gy), (gx, south), (gx, north),
        (west, south), (west, north), (east, south), (east, north),
    ):
        greet(other)

    @pl.when(relaying)
    def _():
        greet((relay_from, gy))

    @pl.when(crossing)
    def _():
        greet((relay_back, gy))

    @pl.when(first)
    def _():
        for block in (2 * gy, 2 * gy + 1, 2 * gy + ny - 1, 2 * gy + 2):
            source = lax.rem(block, ny)

            @pl.when(source != gy)
            def _():
                greet((0, source))

    def one_if(condition):
        return jnp.where(condition, 1, 0)

    greetings = 8 + one_if(relaying) + one_if(crossing)
    for target in inlet_targets:
        greetings = greetings + one_if(jnp.logical_and(first, target != gy))

    def main_load(x):
        return pltpu.make_async_copy(main_hbm.at[:, x], main_in.at[:, x], load_sem.at[x])

    def prec_load(x):
        return pltpu.make_async_copy(prec_hbm.at[:, x], prec_in.at[:, x], load_sem.at[main_x + x])

    cell_load = pltpu.make_async_copy(cell_hbm, cell_in, cell_sem)
    cell_load.start()
    prec_load(prec_x - 1).start()
    main_load(main_x - 1).start()
    main_load(0).start()
    prec_load(0).start()
    for x in range(1, main_x - 1):
        main_load(x).start()
    for x in range(1, prec_x - 1):
        prec_load(x).start()

    for k in range(27):
        rate = rates[k]
        kept = scale_of(k) * (1.0 - rate)
        table[k] = jnp.full((ROWS, LANES), kept, F32)
        factor = third_of(k) * (3.0 if even_orders(k) else 1.0)
        table[27 + k] = jnp.full((ROWS, LANES), scale_of(k) * factor * rate, F32)

    def keep(k):
        return table[k]

    def gain(k):
        return table[27 + k]

    def tile_of(step):
        row = pl.multiple_of(lax.div(step, ztiles) * ROWS, ROWS)
        z = lax.rem(step, ztiles)
        return row, z, pl.multiple_of(z * LANES, LANES)

    def main_plane(x):
        def body(step, carry):
            row, z, lane = tile_of(step)
            rows, lanes = pl.ds(row, ROWS), pl.ds(lane, LANES)
            flags = cell_in[x, rows, lanes]
            g = collide([main_in[i, x, rows, lanes] for i in range(27)], keep, gain, flags == 2)
            solid = flags == 1
            for i in range(27):
                value = jnp.where(solid, main_in[26 - i, x, rows, lanes], g[i])
                main_g[i // 9, i % 9, x + 1, z, pl.ds(pl.multiple_of(TOP + row, ROWS), ROWS), :] = value
            return carry

        lax.fori_loop(0, main_y // ROWS * ztiles, body, 0)

    def prec_plane(x):
        def body(step, carry):
            row, z, lane = tile_of(step)
            rows, lanes = pl.ds(row, ROWS), pl.ds(lane, LANES)
            g = collide([prec_in[i, x, rows, lanes] for i in range(27)], keep, gain)
            for i in range(27):
                prec_g[i // 9, i % 9, x + 1, z, pl.ds(pl.multiple_of(TOP + row, ROWS), ROWS), :] = g[i]
            return carry

        lax.fori_loop(0, prec_y // ROWS * ztiles, body, 0)

    def remote(src, dst, send, recv, device):
        return pltpu.make_async_remote_copy(
            src_ref=src, dst_ref=dst, send_sem=send, recv_sem=recv, device_id=device, device_id_type=MESH
        )

    near = ztiles - ztiles // 2

    class Faces:
        def __init__(self, g, count, rows, send, recv, relay, arrival):
            inner = pl.ds(TOP, rows)
            lower, upper = pl.ds(0, near), pl.ds(near, ztiles // 2)

            def face(side, zs):
                source, dest = (g.at[2, :, count, zs, inner], g.at[2, :, 0, zs, inner])
                if side:
                    source, dest = (g.at[0, :, 1, zs, inner], g.at[0, :, count + 1, zs, inner])
                return source, dest, send.at[side], recv.at[side], (west if side else east, gy)

            whole = pl.ds(0, ztiles)
            self.whole = [remote(*face(side, whole)) for side in range(2)]
            self.direct = [remote(*face(side, lower)) for side in range(2)]
            self.to_relay = [
                remote(face(side, upper)[0], relay, send.at[8], arrival, (relay_of, gy)) for side in range(2)
            ]
            self.from_relay = [
                remote(relay, face(side, upper)[1], send.at[9], recv.at[side], (relay_to, gy)) for side in range(2)
            ]

        def start(self, side):
            split = down_source if side else up_source

            @pl.when(split)
            def _():
                self.to_relay[side].start()
                self.direct[side].start()

            @pl.when(jnp.logical_not(split))
            def _():
                self.whole[side].start()

        def wait_send(self, side):
            split = down_source if side else up_source

            @pl.when(split)
            def _():
                self.to_relay[side].wait_send()
                self.direct[side].wait_send()

            @pl.when(jnp.logical_not(split))
            def _():
                self.whole[side].wait_send()

    main_faces = Faces(main_g, main_x, main_y, main_send, main_recv, main_relay, relay_recv.at[0])
    prec_faces = Faces(prec_g, prec_x, prec_y, prec_send, prec_recv, prec_relay, relay_recv.at[1])

    def pack_corner(g, count, rows, out_c, corner):
        side, a, x = corner % 2, 2 if corner < 2 else 0, count if corner < 2 else 1
        row = TOP + rows - 1 if side == 0 else TOP
        for e in range(3):
            for z in range(ztiles):
                out_c[corner, pl.ds(e * ztiles + z, 1), :] = g[a, (6 if side == 0 else 0) + e, x, z, pl.ds(row, 1), :]

    def corner_copies(out_c, got_c, send, recv):
        return [
            remote(
                out_c.at[corner], got_c.at[corner], send.at[4 + corner], recv.at[4 + corner],
                (east if corner < 2 else west, (north, south)[corner % 2]),
            )
            for corner in range(4)
        ]

    prec_corners = corner_copies(prec_out_c, prec_got_c, prec_send, prec_recv)
    main_corners = corner_copies(main_out_c, main_got_c, main_send, main_recv)

    prec_load(prec_x - 1).wait()
    prec_plane(prec_x - 1)
    pack_corner(prec_g, prec_x, prec_y, prec_out_c, 0)
    pack_corner(prec_g, prec_x, prec_y, prec_out_c, 1)
    main_load(main_x - 1).wait()
    cell_load.wait()
    main_plane(main_x - 1)
    pack_corner(main_g, main_x, main_y, main_out_c, 0)
    pack_corner(main_g, main_x, main_y, main_out_c, 1)
    pl.semaphore_wait(barrier, greetings)
    prec_corners[0].start()
    prec_corners[1].start()

    @pl.when(jnp.logical_not(last))
    def _():
        main_corners[0].start()
        main_corners[1].start()

    prec_faces.start(0)

    @pl.when(jnp.logical_not(last))
    def _():
        main_faces.start(0)

    main_load(0).wait()
    main_plane(0)
    pack_corner(main_g, main_x, main_y, main_out_c, 2)
    pack_corner(main_g, main_x, main_y, main_out_c, 3)

    @pl.when(jnp.logical_not(first))
    def _():
        main_corners[2].start()
        main_corners[3].start()
        main_faces.start(1)

    prec_load(0).wait()
    prec_plane(0)
    pack_corner(prec_g, prec_x, prec_y, prec_out_c, 2)
    pack_corner(prec_g, prec_x, prec_y, prec_out_c, 3)
    prec_corners[2].start()
    prec_corners[3].start()
    prec_faces.start(1)

    def prec_rest(x, carry):
        prec_load(x).wait()
        prec_plane(x)
        return carry

    lax.fori_loop(1, prec_x - 1, prec_rest, 0)

    def pack(g, count, rows, out_y):
        for side in range(2):
            row = TOP + rows - 1 if side == 0 else TOP
            for a in range(3):
                for e in range(3):
                    i = 9 * a + (6 if side == 0 else 0) + e
                    for part in range(count * ztiles // ROWS):
                        out_y[side, 3 * a + e, pl.ds(part * ROWS, ROWS), :] = load_across(g, i, part, row)

    def y_copies(out_y, got_y, send, recv):
        return [
            remote(out_y.at[side], got_y.at[side], send.at[2 + side], recv.at[2 + side], (gx, (north, south)[side]))
            for side in range(2)
        ]

    pack(prec_g, prec_x, prec_y, prec_out_y)
    prec_y_copies = y_copies(prec_out_y, prec_got_y, prec_send, prec_recv)
    main_y_copies = y_copies(main_out_y, main_got_y, main_send, main_recv)
    for copy in prec_y_copies:
        copy.start()

    def main_rest(x, carry):
        main_load(x).wait()
        main_plane(x)
        return carry

    lax.fori_loop(1, main_x - 1, main_rest, 0)
    pack(main_g, main_x, main_y, main_out_y)
    for copy in main_y_copies:
        copy.start()

    @pl.when(relaying)
    def _():
        main_faces.to_relay[0].wait_recv()
        prec_faces.to_relay[0].wait_recv()

    @pl.when(up_relay)
    def _():
        main_faces.from_relay[0].start()
        prec_faces.from_relay[0].start()

    @pl.when(down_relay)
    def _():
        main_faces.from_relay[1].start()
        prec_faces.from_relay[1].start()

    def inlet_copies(target, run):
        where = inlet_targets[target]
        if target < 2:
            rows = pl.ds(pl.multiple_of(TOP + lax.rem(gy, 2) * prec_y, ROWS), prec_y)
            pairs = [(True, prec_g.at[2, :, 0, :, pl.ds(TOP, prec_y)], main_g.at[2, :, 0, :, rows], main_recv.at[0])]
        else:
            pairs = [
                (odd if corner == 0 else jnp.logical_not(odd), inlet_c, main_got_c.at[corner], main_recv.at[4 + corner])
                for corner in range(2)
            ]
        for chosen, source, dest, arrival in pairs:

            @pl.when(jnp.logical_and(chosen, where != gy))
            def _():
                run(remote(source, dest, inlet_send.at[target], arrival, (0, where)), True)

            @pl.when(jnp.logical_and(chosen, where == gy))
            def _():
                run(pltpu.make_async_copy(source, dest, arrival), False)

    @pl.when(first)
    def _():
        prec_faces.whole[0].wait_recv()
        for target in range(2):
            inlet_copies(target, lambda copy, far: copy.start())
        for e in range(3):
            for z in range(ztiles):
                line = pl.ds(e * ztiles + z, 1)

                @pl.when(odd)
                def _():
                    inlet_c[line, :] = prec_g[2, 6 + e, 0, z, pl.ds(TOP + prec_y - 1, 1), :]

                @pl.when(jnp.logical_not(odd))
                def _():
                    inlet_c[line, :] = prec_g[2, e, 0, z, pl.ds(TOP, 1), :]

        for target in range(2, 4):
            inlet_copies(target, lambda copy, far: copy.start())

    def unpack(g, count, rows, got_y):
        for side in range(2):
            row = TOP - 1 if side == 0 else TOP + rows
            for a in range(3):
                for e in range(3):
                    i = 9 * a + (6 if side == 0 else 0) + e
                    for part in range(count * ztiles // ROWS):
                        store_across(g, i, part, row, got_y[side, 3 * a + e, pl.ds(part * ROWS, ROWS), :])

    def unpack_corner(g, count, rows, got_c, corner):
        side, a, x = corner % 2, 2 if corner < 2 else 0, 0 if corner < 2 else count + 1
        row = TOP - 1 if side == 0 else TOP + rows
        for e in range(3):
            for z in range(ztiles):
                g[a, (6 if side == 0 else 0) + e, x, z, pl.ds(row, 1), :] = got_c[corner, pl.ds(e * ztiles + z, 1), :]

    for side in range(2):
        prec_y_copies[side].wait_recv()
    unpack(prec_g, prec_x, prec_y, prec_got_y)
    for corner in range(4):
        prec_corners[corner].wait_recv()
        unpack_corner(prec_g, prec_x, prec_y, prec_got_c, corner)
    for side in range(2):
        main_y_copies[side].wait_recv()
    unpack(main_g, main_x, main_y, main_got_y)
    for corner in range(2):
        main_corners[corner].wait_recv()
        unpack_corner(main_g, main_x, main_y, main_got_c, corner)

    @pl.when(jnp.logical_not(last))
    def _():
        for corner in range(2, 4):
            main_corners[corner].wait_recv()
            unpack_corner(main_g, main_x, main_y, main_got_c, corner)

    @pl.when(jnp.logical_not(first))
    def _():
        prec_faces.whole[0].wait_recv()

    prec_faces.whole[1].wait_recv()
    main_faces.whole[0].wait_recv()

    @pl.when(jnp.logical_not(last))
    def _():
        main_faces.whole[1].wait_recv()

    for copy in [*prec_y_copies, *prec_corners, *main_y_copies]:
        copy.wait_send()
    prec_faces.wait_send(0)
    prec_faces.wait_send(1)

    @pl.when(jnp.logical_not(last))
    def _():
        main_corners[0].wait_send()
        main_corners[1].wait_send()
        main_faces.wait_send(0)

    @pl.when(jnp.logical_not(first))
    def _():
        main_corners[2].wait_send()
        main_corners[3].wait_send()
        main_faces.wait_send(1)

    @pl.when(relaying)
    def _():
        main_faces.from_relay[0].wait_send()
        prec_faces.from_relay[0].wait_send()

    @pl.when(first)
    def _():
        for target in range(4):

            @pl.when(inlet_targets[target] != gy)
            def _():
                if target < 2:
                    inlet_copies(target, lambda copy, far: copy.wait_send() if far else None)
                else:
                    remote(
                        inlet_c, main_got_c.at[0], inlet_send.at[target], main_recv.at[4], (0, inlet_targets[target])
                    ).wait_send()


def stream(nx, main_g, prec_g, prec_next, main_next, prec_out, main_out, prec_sem, main_sem):
    last = lax.axis_index("gx") == nx - 1

    def plane(g, out, count, rows, x, clamp):
        lane = lax.broadcasted_iota(jnp.int32, (ROWS, LANES), 1)
        low, high = lane == 0, lane == LANES - 1
        ztiles = g.shape[3]

        def body(step, carry):
            row = pl.multiple_of(step * ROWS, ROWS)
            for i in range(27):
                cx, cy, cz = i // 9 - 1, i // 3 % 3 - 1, i % 3 - 1
                source = x + 1 - cx
                if clamp and cx == -1:
                    source = jnp.where(last, jnp.minimum(source, count), source)
                tiles = [g[i // 9, i % 9, source, z, pl.ds(TOP - cy + row, ROWS), :] for z in range(ztiles)]
                if cz:
                    j = 26 - i
                    wall = 0 if cz == 1 else ztiles - 1
                    bounced = g[j // 9, j % 9, x + 1, wall, pl.ds(pl.multiple_of(TOP + row, ROWS), ROWS), :]
                    moved = [pltpu.roll(tile, 1 if cz == 1 else LANES - 1, 1) for tile in tiles]
                    if cz == 1:
                        tiles = [jnp.where(low, moved[z - 1] if z else bounced, moved[z]) for z in range(ztiles)]
                    else:
                        tiles = [
                            jnp.where(high, moved[z + 1] if z < ztiles - 1 else bounced, moved[z])
                            for z in range(ztiles)
                        ]
                for z in range(ztiles):
                    out[x, i, pl.ds(row, ROWS), pl.ds(z * LANES, LANES)] = tiles[z]
            return carry

        lax.fori_loop(0, rows // ROWS, body, 0)

    def run(g, out, dest, sem, clamp):
        count, rows = out.shape[0], out.shape[2]

        def copy(x):
            return pltpu.make_async_copy(out.at[x], dest.at[:, x], sem.at[x])

        def body(x, carry):
            plane(g, out, count, rows, x, clamp)
            copy(x).start()
            return carry

        lax.fori_loop(0, count, body, 0)
        return copy

    main_copy = run(main_g, main_out, main_next, main_sem, True)
    prec_copy = run(prec_g, prec_out, prec_next, prec_sem, False)
    for x in range(main_out.shape[0]):
        main_copy(x).wait()
    for x in range(prec_out.shape[0]):
        prec_copy(x).wait()


def solution(mesh):
    nx, ny = mesh.shape["gx"], mesh.shape["gy"]

    def shards(prec_pops, main_pops, cell_type, rates):
        main_x, main_y, depth = main_pops.shape[1:]
        prec_x, prec_y = prec_pops.shape[1:3]
        ztiles = depth // LANES
        main_shape = (3, 9, main_x + 2, ztiles, main_y + 2 * TOP, LANES)
        prec_shape = (3, 9, prec_x + 2, ztiles, prec_y + 2 * TOP, LANES)
        in_hbm = pl.BlockSpec(memory_space=pltpu.HBM)
        on_chip = pl.BlockSpec(memory_space=pltpu.VMEM)
        main_g, prec_g = pl.pallas_call(
            functools.partial(exchange, (nx, ny)),
            name="exchange",
            out_shape=(pltpu.VMEM(main_shape, F32), pltpu.VMEM(prec_shape, F32)),
            in_specs=[pl.BlockSpec(memory_space=pltpu.SMEM), in_hbm, in_hbm, in_hbm],
            out_specs=(on_chip, on_chip),
            scratch_shapes=[
                pltpu.VMEM(main_pops.shape, F32),
                pltpu.VMEM(prec_pops.shape, F32),
                pltpu.VMEM(cell_type.shape, jnp.int32),
                pltpu.VMEM((54, ROWS, LANES), F32),
                pltpu.VMEM((2, 9, main_x * ztiles, LANES), F32),
                pltpu.VMEM((2, 9, main_x * ztiles, LANES), F32),
                pltpu.VMEM((4, ROWS, LANES), F32),
                pltpu.VMEM((4, ROWS, LANES), F32),
                pltpu.VMEM((2, 9, prec_x * ztiles, LANES), F32),
                pltpu.VMEM((2, 9, prec_x * ztiles, LANES), F32),
                pltpu.VMEM((4, ROWS, LANES), F32),
                pltpu.VMEM((4, ROWS, LANES), F32),
                pltpu.SemaphoreType.DMA((main_x + prec_x,)),
                pltpu.SemaphoreType.DMA,
                pltpu.SemaphoreType.DMA((10,)),
                pltpu.SemaphoreType.DMA((8,)),
                pltpu.SemaphoreType.DMA((10,)),
                pltpu.SemaphoreType.DMA((8,)),
                pltpu.SemaphoreType.DMA((4,)),
                pltpu.VMEM((ROWS, LANES), F32),
                pltpu.VMEM((9, ztiles // 2, main_y, LANES), F32),
                pltpu.VMEM((9, ztiles // 2, prec_y, LANES), F32),
                pltpu.SemaphoreType.DMA((2,)),
            ],
            compiler_params=pltpu.CompilerParams(
                collective_id=0, has_side_effects=True, vmem_limit_bytes=24 * 1024 * 1024
            ),
        )(*(pltpu.with_memory_space_constraint(x, pltpu.HBM) for x in (rates, prec_pops, main_pops, cell_type)))
        prec_next, main_next = pl.pallas_call(
            functools.partial(stream, nx),
            name="stream",
            out_shape=(
                jax.ShapeDtypeStruct(prec_pops.shape, F32),
                jax.ShapeDtypeStruct(main_pops.shape, F32),
            ),
            in_specs=[on_chip, on_chip],
            out_specs=(in_hbm, in_hbm),
            scratch_shapes=[
                pltpu.VMEM((prec_x, 27, prec_y, depth), F32),
                pltpu.VMEM((main_x, 27, main_y, depth), F32),
                pltpu.SemaphoreType.DMA((prec_x,)),
                pltpu.SemaphoreType.DMA((main_x,)),
            ],
            compiler_params=pltpu.CompilerParams(vmem_limit_bytes=24 * 1024 * 1024),
        )(main_g, prec_g)
        return prec_next, main_next

    placed = (P(None, "gx", "gy", None), P(None, "gx", "gy", None), P("gx", "gy", None), P())
    return jax.shard_map(
        shards,
        mesh=mesh,
        in_specs=placed,
        out_specs=(P(None, "gx", "gy", None), P(None, "gx", "gy", None)),
        check_vma=False,
    )
```

```python
import functools

import jax
import jax.numpy as jnp
from jax import lax
from jax.experimental import pallas as pl
from jax.experimental.pallas import tpu as pltpu
from jax.sharding import PartitionSpec as P

MESH = pl.DeviceIdType.MESH
F32 = jnp.float32
LANES = 128
ROWS = 8
GROUP = 4
TOP = 8


def scale_of(moment):
    a, b, e = moment // 9, moment // 3 % 3, moment % 3
    return (0.5 if a else 1.0) * (0.5 if b else 1.0) * (0.5 if e else 1.0)


def third_of(moment):
    a, b, e = moment // 9, moment // 3 % 3, moment % 3
    return (1.0 / 3.0) ** ((a == 2) + (b == 2) + (e == 2))


def axis_triples():
    for stride in (9, 3, 1):
        for base in range(27):
            if base // stride % 3 == 0:
                yield base, base + stride, base + 2 * stride


def to_moments(f):
    m = list(f)
    for low, mid, high in axis_triples():
        total = m[high] + m[low]
        m[low], m[mid], m[high] = total + m[mid], m[high] - m[low], total
    return m


def to_populations(m):
    g = list(m)
    for low, mid, high in axis_triples():
        g[low], g[mid], g[high] = g[high] - g[mid], g[low] - (g[high] + g[high]), g[high] + g[mid]
    return g


def collide(f, keep, gain, disk=None):
    m = to_moments(f)
    rho, jx, jy, jz = m[0], m[9], m[3], m[1]
    inverse = 1.0 / rho
    ux, uy, uz = jx * inverse, jy * inverse, jz * inverse
    qx, qy, qz = jx * ux, jy * uy, jz * uz
    third = rho * (1.0 / 3.0)
    ex, ey, ez = third + qx, third + qy, third + qz
    exy, exz, eyz = ex + qy, ex + qz, ey + qz
    even = {18: ex, 6: ey, 2: ez, 24: exy, 20: exz, 8: eyz, 26: exy + qz}
    odd = {}
    for k in range(27):
        a, b, e = k // 9, k // 3 % 3, k % 3
        ones = (a == 1) + (b == 1) + (e == 1)
        if ones == 1:
            odd[k] = jx if a == 1 else jy if b == 1 else jz
        elif ones == 2:
            odd[k] = jx * uy if e != 1 else jx * uz if b != 1 else jy * uz
    out = [None] * 27
    shared = {}
    for k in range(27):
        a, b, e = k // 9, k // 3 % 3, k % 3
        if k == 0:
            out[k] = rho
        elif k in (9, 3, 1):
            out[k] = odd[k] * 0.5
        elif k == 13:
            out[k] = keep(k) * m[k]
        elif k in even:
            out[k] = keep(k) * m[k] + gain(k) * even[k]
        else:
            pair = (a == 1, b == 1, e == 1)
            if pair not in shared:
                shared[pair] = odd[k]
            out[k] = keep(k) * m[k] + gain(k) * shared[pair]
    if disk is not None:
        drag = jnp.where(disk, (-0.5 * 0.75) * jx * jnp.abs(ux), 0.0)
        out[9] = out[9] + drag * 0.5
        side = drag * (0.25 / 3.0)
        out[15] = out[15] + side
        out[11] = out[11] + side
        out[17] = out[17] + drag * (0.125 / 9.0)
    return to_populations(out)


def even_orders(k):
    a, b, e = k // 9, k // 3 % 3, k % 3
    return a != 1 and b != 1 and e != 1


def rows_across(g, i, part, row):
    planes, ztiles, pitch = g.shape[2:5]
    flat = g.reshape(27 * planes * ztiles * pitch, LANES)
    return flat, pl.ds(((i * planes + 1) * ztiles + part * ROWS) * pitch + row, ROWS, stride=pitch)


def load_across(g, i, part, row):
    flat, rows = rows_across(g, i, part, row)
    return flat[rows, :]


def store_across(g, i, part, row, value):
    flat, rows = rows_across(g, i, part, row)
    flat[rows, :] = value


def exchange(
    size,
    rates,
    prec_hbm,
    main_hbm,
    cell_hbm,
    main_g,
    prec_g,
    main_in,
    prec_in,
    cell_in,
    table,
    main_out_y,
    main_got_y,
    prec_out_y,
    prec_got_y,
    packet,
    packet_x,
    packet_y,
    inlet_c,
    main_relay,
    prec_relay,
    inlet_relay,
    load_sem,
    cell_sem,
    main_send,
    main_recv,
    prec_send,
    prec_recv,
    packet_send,
    packet_recv,
    inlet_send,
    inlet_recv,
    relay_recv,
    late_ready,
):
    nx, ny = size
    gx, gy = lax.axis_index("gx"), lax.axis_index("gy")
    main_x, main_y = main_in.shape[1], main_in.shape[2]
    prec_x, prec_y = prec_in.shape[1], prec_in.shape[2]
    ztiles = main_g.shape[3]
    first, last = gx == 0, gx == nx - 1
    inner_first, inner_last = jnp.logical_not(first), jnp.logical_not(last)
    east, west = lax.rem(gx + 1, nx), lax.rem(gx + nx - 1, nx)
    north, south = lax.rem(gy + 1, ny), lax.rem(gy + ny - 1, ny)
    half = ny // 2

    place = lax.rem(gx, GROUP)
    up_source = jnp.logical_and(place == GROUP - 1, inner_last)
    down_source = jnp.logical_and(place == 0, inner_first)
    up_relay = jnp.logical_and(place == 0, gx + GROUP < nx)
    down_relay = jnp.logical_and(place == GROUP - 1, gx - GROUP >= 0)
    crossing = jnp.logical_or(up_source, down_source)
    relaying = jnp.logical_or(up_relay, down_relay)
    relay_from = jnp.where(up_relay, gx + GROUP - 1, gx - GROUP + 1)
    relay_to = jnp.where(up_relay, gx + GROUP, gx - GROUP)
    relay_of = jnp.where(up_source, gx - GROUP + 1, gx + GROUP - 1)
    relay_back = jnp.where(down_source, gx - GROUP, gx + GROUP)

    passing = gx == nx - GROUP
    odd = lax.rem(gy, 2) == 1
    inlet_block = lax.div(gy, 2)
    corner_block = jnp.where(odd, lax.rem(lax.div(gy + 1, 2), half), lax.rem(lax.div(gy, 2) + half - 1, half))

    barrier = pltpu.get_barrier_semaphore()

    def greet(device):
        pl.semaphore_signal(barrier, inc=1, device_id=device, device_id_type=MESH)

    for other in ((west, gy), (gx, south), (gx, north)):
        greet(other)

    @pl.when(inner_last)
    def _():
        greet((east, gy))

    @pl.when(relaying)
    def _():
        greet((relay_from, gy))

    @pl.when(crossing)
    def _():
        greet((relay_back, gy))

    @pl.when(passing)
    def _():
        greet((nx - 1, gy))

    @pl.when(first)
    def _():
        source = jnp.where(gy < half, nx - 1, nx - GROUP)
        greet((source, lax.rem(2 * gy, ny)))
        greet((source, lax.rem(2 * gy + 1, ny)))
        greet((nx - 1, lax.rem(2 * gy + ny - 1, ny)))
        greet((nx - 1, lax.rem(2 * gy + 2, ny)))

    def one_if(condition):
        return jnp.where(condition, 1, 0)

    greetings = 3 + one_if(inner_first) + one_if(relaying) + one_if(crossing) + one_if(passing) + 4 * one_if(last)

    def main_load(x):
        return pltpu.make_async_copy(main_hbm.at[:, x], main_in.at[:, x], load_sem.at[x])

    def prec_load(x):
        return pltpu.make_async_copy(prec_hbm.at[:, x], prec_in.at[:, x], load_sem.at[main_x + x])

    cell_load = pltpu.make_async_copy(cell_hbm, cell_in, cell_sem)
    prec_load(prec_x - 1).start()
    cell_load.start()
    main_load(main_x - 1).start()
    main_load(0).start()
    prec_load(0).start()
    for x in range(1, main_x - 1):
        main_load(x).start()
    for x in range(1, prec_x - 1):
        prec_load(x).start()

    for k in range(27):
        rate = rates[k]
        kept = scale_of(k) * (1.0 - rate)
        table[k] = jnp.full((ROWS, LANES), kept, F32)
        factor = third_of(k) * (3.0 if even_orders(k) else 1.0)
        table[27 + k] = jnp.full((ROWS, LANES), scale_of(k) * factor * rate, F32)

    def keep(k):
        return table[k]

    def gain(k):
        return table[27 + k]

    def tile_of(step):
        row = pl.multiple_of(lax.div(step, ztiles) * ROWS, ROWS)
        z = lax.rem(step, ztiles)
        return row, z, pl.multiple_of(z * LANES, LANES)

    def main_plane(x):
        def body(step, carry):
            row, z, lane = tile_of(step)
            rows, lanes = pl.ds(row, ROWS), pl.ds(lane, LANES)
            flags = cell_in[x, rows, lanes]
            g = collide([main_in[i, x, rows, lanes] for i in range(27)], keep, gain, flags == 2)
            solid = flags == 1
            for i in range(27):
                value = jnp.where(solid, main_in[26 - i, x, rows, lanes], g[i])
                main_g[i // 9, i % 9, x + 1, z, pl.ds(pl.multiple_of(TOP + row, ROWS), ROWS), :] = value
            return carry

        lax.fori_loop(0, main_y // ROWS * ztiles, body, 0)

    def prec_plane(x):
        def body(step, carry):
            row, z, lane = tile_of(step)
            rows, lanes = pl.ds(row, ROWS), pl.ds(lane, LANES)
            g = collide([prec_in[i, x, rows, lanes] for i in range(27)], keep, gain)
            for i in range(27):
                prec_g[i // 9, i % 9, x + 1, z, pl.ds(pl.multiple_of(TOP + row, ROWS), ROWS), :] = g[i]
            return carry

        lax.fori_loop(0, prec_y // ROWS * ztiles, body, 0)

    def remote(src, dst, send, recv, device):
        return pltpu.make_async_remote_copy(
            src_ref=src, dst_ref=dst, send_sem=send, recv_sem=recv, device_id=device, device_id_type=MESH
        )

    near = ztiles - ztiles // 2

    class Faces:
        def __init__(self, g, count, rows, send, recv, relay, arrival):
            inner = pl.ds(TOP, rows)
            lower, upper = pl.ds(0, near), pl.ds(near, ztiles // 2)

            def face(side, zs):
                source, dest = (g.at[2, :, count, zs, inner], g.at[2, :, 0, zs, inner])
                if side:
                    source, dest = (g.at[0, :, 1, zs, inner], g.at[0, :, count + 1, zs, inner])
                return source, dest, send.at[side], recv.at[side], (west if side else east, gy)

            whole = pl.ds(0, ztiles)
            self.whole = [remote(*face(side, whole)) for side in range(2)]
            self.direct = [remote(*face(side, lower)) for side in range(2)]
            self.to_relay = [
                remote(face(side, upper)[0], relay, send.at[4], arrival, (relay_of, gy)) for side in range(2)
            ]
            self.from_relay = [
                remote(relay, face(side, upper)[1], send.at[5], recv.at[side], (relay_to, gy)) for side in range(2)
            ]

        def run(self, side, act):
            split = down_source if side else up_source

            @pl.when(split)
            def _():
                act(self.to_relay[side])
                act(self.direct[side])

            @pl.when(jnp.logical_not(split))
            def _():
                act(self.whole[side])

    def start(copy):
        copy.start()

    def sent(copy):
        copy.wait_send()

    main_faces = Faces(main_g, main_x, main_y, main_send, main_recv, main_relay, relay_recv.at[0])
    prec_faces = Faces(prec_g, prec_x, prec_y, prec_send, prec_recv, prec_relay, relay_recv.at[1])

    def pack_corners(lattice, side):
        g, count, rows = ((main_g, main_x, main_y), (prec_g, prec_x, prec_y))[lattice]
        a, x = (0, 1) if side else (2, count)
        for up in range(2):
            row = TOP if up else TOP + rows - 1
            for e in range(3):
                for z in range(ztiles):
                    line = g[a, (0 if up else 6) + e, x, z, pl.ds(row, 1), :]
                    packet[side, up, lattice, pl.ds(e * ztiles + z, 1), :] = line

    packets_x = [
        remote(packet.at[side], packet_x.at[side], packet_send.at[side], packet_recv.at[side], ((east, west)[side], gy))
        for side in range(2)
    ]
    packets_y = [
        remote(
            packet_x.at[:, up], packet_y.at[up], packet_send.at[2 + up], packet_recv.at[2 + up], (gx, (north, south)[up])
        )
        for up in range(2)
    ]

    inlet_rows = pl.ds(pl.multiple_of(TOP + lax.rem(gy, 2) * prec_y, ROWS), prec_y)
    outlet = prec_g.at[2, :, prec_x, :, pl.ds(TOP, prec_y)]
    inlet_direct = remote(
        outlet, main_g.at[2, :, 0, :, inlet_rows], inlet_send.at[0], main_recv.at[0], (0, inlet_block)
    )
    inlet_to_relay = remote(outlet, inlet_relay, inlet_send.at[1], relay_recv.at[2], (nx - GROUP, gy))
    inlet_from_relay = remote(
        inlet_relay, main_g.at[2, :, 0, :, inlet_rows], inlet_send.at[0], main_recv.at[0], (0, inlet_block + half)
    )
    inlet_corners = [
        [
            remote(
                packet.at[0, up, 1], inlet_c.at[up], inlet_send.at[2 + target], inlet_recv.at[up],
                (0, corner_block + target * half),
            )
            for target in range(2)
        ]
        for up in range(2)
    ]

    def inlet_run(act):
        act(inlet_to_relay)
        act(inlet_direct)
        for up, chosen in ((0, odd), (1, jnp.logical_not(odd))):

            @pl.when(chosen)
            def _():
                act(inlet_corners[up][0])
                act(inlet_corners[up][1])

    prec_load(prec_x - 1).wait()
    prec_plane(prec_x - 1)
    pack_corners(1, 0)

    @pl.when(last)
    def _():
        pl.semaphore_wait(barrier, greetings)
        pl.semaphore_signal(late_ready, inc=1, device_id=(0, gy), device_id_type=MESH)
        inlet_run(start)
        prec_faces.whole[0].start()

    main_load(main_x - 1).wait()
    cell_load.wait()
    main_plane(main_x - 1)
    pack_corners(0, 0)

    @pl.when(inner_last)
    def _():
        pl.semaphore_wait(barrier, greetings)

    packets_x[0].start()

    @pl.when(inner_last)
    def _():
        main_faces.run(0, start)
        prec_faces.run(0, start)

    main_load(0).wait()
    main_plane(0)
    pack_corners(0, 1)
    prec_load(0).wait()
    prec_plane(0)
    pack_corners(1, 1)

    @pl.when(inner_first)
    def _():
        packets_x[1].start()
        main_faces.run(1, start)
        prec_faces.run(1, start)

    def prec_rest(x, carry):
        prec_load(x).wait()
        prec_plane(x)
        return carry

    lax.fori_loop(1, prec_x - 1, prec_rest, 0)

    def pack(g, count, rows, out_y):
        for side in range(2):
            row = TOP + rows - 1 if side == 0 else TOP
            for a in range(3):
                for e in range(3):
                    i = 9 * a + (6 if side == 0 else 0) + e
                    for part in range(count * ztiles // ROWS):
                        out_y[side, 3 * a + e, pl.ds(part * ROWS, ROWS), :] = load_across(g, i, part, row)

    def y_copies(out_y, got_y, send, recv):
        return [
            remote(out_y.at[side], got_y.at[side], send.at[2 + side], recv.at[2 + side], (gx, (north, south)[side]))
            for side in range(2)
        ]

    pack(prec_g, prec_x, prec_y, prec_out_y)
    prec_y_copies = y_copies(prec_out_y, prec_got_y, prec_send, prec_recv)
    main_y_copies = y_copies(main_out_y, main_got_y, main_send, main_recv)
    for copy in prec_y_copies:
        copy.start()

    def main_rest(x, carry):
        main_load(x).wait()
        main_plane(x)
        return carry

    lax.fori_loop(1, main_x - 1, main_rest, 0)
    pack(main_g, main_x, main_y, main_out_y)
    for copy in main_y_copies:
        copy.start()

    @pl.when(relaying)
    def _():
        main_faces.to_relay[0].wait_recv()

    @pl.when(up_relay)
    def _():
        main_faces.from_relay[0].start()

    @pl.when(down_relay)
    def _():
        main_faces.from_relay[1].start()

    @pl.when(relaying)
    def _():
        prec_faces.to_relay[0].wait_recv()

    @pl.when(up_relay)
    def _():
        prec_faces.from_relay[0].start()

    @pl.when(down_relay)
    def _():
        prec_faces.from_relay[1].start()

    @pl.when(passing)
    def _():
        inlet_to_relay.wait_recv()
        inlet_from_relay.start()

    @pl.when(first)
    def _():
        pl.semaphore_wait(late_ready, 1)
        packets_x[1].start()
        prec_faces.whole[1].start()

    for side in range(2):
        packets_x[side].wait_recv()
    for up in range(2):
        packets_y[up].start()

    def unpack(g, count, rows, got_y):
        for side in range(2):
            row = TOP - 1 if side == 0 else TOP + rows
            for a in range(3):
                for e in range(3):
                    i = 9 * a + (6 if side == 0 else 0) + e
                    for part in range(count * ztiles // ROWS):
                        store_across(g, i, part, row, got_y[side, 3 * a + e, pl.ds(part * ROWS, ROWS), :])

    def unpack_corner(lattice, side, up, tile):
        g, count, rows = ((main_g, main_x, main_y), (prec_g, prec_x, prec_y))[lattice]
        a, x = (0, count + 1) if side else (2, 0)
        row = TOP + rows if up else TOP - 1
        for e in range(3):
            for z in range(ztiles):
                g[a, (0 if up else 6) + e, x, z, pl.ds(row, 1), :] = tile[pl.ds(e * ztiles + z, 1), :]

    for side in range(2):
        prec_y_copies[side].wait_recv()
    unpack(prec_g, prec_x, prec_y, prec_got_y)
    for side in range(2):
        main_y_copies[side].wait_recv()
    unpack(main_g, main_x, main_y, main_got_y)
    for up in range(2):
        packets_y[up].wait_recv()
        for side in range(2):
            unpack_corner(1, side, up, packet_y.at[up, side, 1])
        unpack_corner(0, 1, up, packet_y.at[up, 1, 0])

        @pl.when(inner_first)
        def _():
            unpack_corner(0, 0, up, packet_y.at[up, 0, 0])

        @pl.when(first)
        def _():
            inlet_corners[up][0].wait_recv()
            unpack_corner(0, 0, up, inlet_c.at[up])

    prec_faces.whole[0].wait_recv()
    prec_faces.whole[1].wait_recv()
    main_faces.whole[0].wait_recv()

    @pl.when(inner_last)
    def _():
        main_faces.whole[1].wait_recv()

    for copy in [*prec_y_copies, *main_y_copies, *packets_x, *packets_y]:
        copy.wait_send()
    prec_faces.run(0, sent)
    prec_faces.run(1, sent)

    @pl.when(inner_last)
    def _():
        main_faces.run(0, sent)

    @pl.when(inner_first)
    def _():
        main_faces.run(1, sent)

    @pl.when(relaying)
    def _():
        main_faces.from_relay[0].wait_send()
        prec_faces.from_relay[0].wait_send()

    @pl.when(passing)
    def _():
        inlet_from_relay.wait_send()

    @pl.when(last)
    def _():
        inlet_run(sent)


def stream(nx, main_g, prec_g, prec_next, main_next, prec_out, main_out, prec_sem, main_sem):
    last = lax.axis_index("gx") == nx - 1

    def plane(g, out, count, rows, x, clamp):
        lane = lax.broadcasted_iota(jnp.int32, (ROWS, LANES), 1)
        low, high = lane == 0, lane == LANES - 1
        ztiles = g.shape[3]

        def body(step, carry):
            row = pl.multiple_of(step * ROWS, ROWS)
            for i in range(27):
                cx, cy, cz = i // 9 - 1, i // 3 % 3 - 1, i % 3 - 1
                source = x + 1 - cx
                if clamp and cx == -1:
                    source = jnp.where(last, jnp.minimum(source, count), source)
                tiles = [g[i // 9, i % 9, source, z, pl.ds(TOP - cy + row, ROWS), :] for z in range(ztiles)]
                if cz:
                    j = 26 - i
                    wall = 0 if cz == 1 else ztiles - 1
                    bounced = g[j // 9, j % 9, x + 1, wall, pl.ds(pl.multiple_of(TOP + row, ROWS), ROWS), :]
                    moved = [pltpu.roll(tile, 1 if cz == 1 else LANES - 1, 1) for tile in tiles]
                    if cz == 1:
                        tiles = [jnp.where(low, moved[z - 1] if z else bounced, moved[z]) for z in range(ztiles)]
                    else:
                        tiles = [
                            jnp.where(high, moved[z + 1] if z < ztiles - 1 else bounced, moved[z])
                            for z in range(ztiles)
                        ]
                for z in range(ztiles):
                    out[x, i, pl.ds(row, ROWS), pl.ds(z * LANES, LANES)] = tiles[z]
            return carry

        lax.fori_loop(0, rows // ROWS, body, 0)

    def run(g, out, dest, sem, clamp):
        count, rows = out.shape[0], out.shape[2]

        def copy(x):
            return pltpu.make_async_copy(out.at[x], dest.at[:, x], sem.at[x])

        def body(x, carry):
            plane(g, out, count, rows, x, clamp)
            copy(x).start()
            return carry

        lax.fori_loop(0, count, body, 0)
        return copy

    main_copy = run(main_g, main_out, main_next, main_sem, True)
    prec_copy = run(prec_g, prec_out, prec_next, prec_sem, False)
    for x in range(main_out.shape[0]):
        main_copy(x).wait()
    for x in range(prec_out.shape[0]):
        prec_copy(x).wait()


def solution(mesh):
    nx, ny = mesh.shape["gx"], mesh.shape["gy"]

    def shards(prec_pops, main_pops, cell_type, rates):
        main_x, main_y, depth = main_pops.shape[1:]
        prec_x, prec_y = prec_pops.shape[1:3]
        ztiles = depth // LANES
        main_shape = (3, 9, main_x + 2, ztiles, main_y + 2 * TOP, LANES)
        prec_shape = (3, 9, prec_x + 2, ztiles, prec_y + 2 * TOP, LANES)
        in_hbm = pl.BlockSpec(memory_space=pltpu.HBM)
        on_chip = pl.BlockSpec(memory_space=pltpu.VMEM)
        main_g, prec_g = pl.pallas_call(
            functools.partial(exchange, (nx, ny)),
            name="exchange",
            out_shape=(pltpu.VMEM(main_shape, F32), pltpu.VMEM(prec_shape, F32)),
            in_specs=[pl.BlockSpec(memory_space=pltpu.SMEM), in_hbm, in_hbm, in_hbm],
            out_specs=(on_chip, on_chip),
            scratch_shapes=[
                pltpu.VMEM(main_pops.shape, F32),
                pltpu.VMEM(prec_pops.shape, F32),
                pltpu.VMEM(cell_type.shape, jnp.int32),
                pltpu.VMEM((54, ROWS, LANES), F32),
                pltpu.VMEM((2, 9, main_x * ztiles, LANES), F32),
                pltpu.VMEM((2, 9, main_x * ztiles, LANES), F32),
                pltpu.VMEM((2, 9, prec_x * ztiles, LANES), F32),
                pltpu.VMEM((2, 9, prec_x * ztiles, LANES), F32),
                pltpu.VMEM((2, 2, 2, ROWS, LANES), F32),
                pltpu.VMEM((2, 2, 2, ROWS, LANES), F32),
                pltpu.VMEM((2, 2, 2, ROWS, LANES), F32),
                pltpu.VMEM((2, ROWS, LANES), F32),
                pltpu.VMEM((9, ztiles // 2, main_y, LANES), F32),
                pltpu.VMEM((9, ztiles // 2, prec_y, LANES), F32),
                pltpu.VMEM((9, ztiles, prec_y, LANES), F32),
                pltpu.SemaphoreType.DMA((main_x + prec_x,)),
                pltpu.SemaphoreType.DMA,
                pltpu.SemaphoreType.DMA((6,)),
                pltpu.SemaphoreType.DMA((4,)),
                pltpu.SemaphoreType.DMA((6,)),
                pltpu.SemaphoreType.DMA((4,)),
                pltpu.SemaphoreType.DMA((4,)),
                pltpu.SemaphoreType.DMA((4,)),
                pltpu.SemaphoreType.DMA((4,)),
                pltpu.SemaphoreType.DMA((2,)),
                pltpu.SemaphoreType.DMA((3,)),
                pltpu.SemaphoreType.REGULAR,
            ],
            compiler_params=pltpu.CompilerParams(
                collective_id=0, has_side_effects=True, vmem_limit_bytes=24 * 1024 * 1024
            ),
        )(*(pltpu.with_memory_space_constraint(x, pltpu.HBM) for x in (rates, prec_pops, main_pops, cell_type)))
        prec_next, main_next = pl.pallas_call(
            functools.partial(stream, nx),
            name="stream",
            out_shape=(
                jax.ShapeDtypeStruct(prec_pops.shape, F32),
                jax.ShapeDtypeStruct(main_pops.shape, F32),
            ),
            in_specs=[on_chip, on_chip],
            out_specs=(in_hbm, in_hbm),
            scratch_shapes=[
                pltpu.VMEM((prec_x, 27, prec_y, depth), F32),
                pltpu.VMEM((main_x, 27, main_y, depth), F32),
                pltpu.SemaphoreType.DMA((prec_x,)),
                pltpu.SemaphoreType.DMA((main_x,)),
            ],
            compiler_params=pltpu.CompilerParams(vmem_limit_bytes=24 * 1024 * 1024),
        )(main_g, prec_g)
        return prec_next, main_next

    placed = (P(None, "gx", "gy", None), P(None, "gx", "gy", None), P("gx", "gy", None), P())
    return jax.shard_map(
        shards,
        mesh=mesh,
        in_specs=placed,
        out_specs=(P(None, "gx", "gy", None), P(None, "gx", "gy", None)),
        check_vma=False,
    )
```

```python
import functools

import jax
import jax.numpy as jnp
from jax import lax
from jax.experimental import pallas as pl
from jax.experimental.pallas import tpu as pltpu
from jax.sharding import PartitionSpec as P

MESH = pl.DeviceIdType.MESH
F32 = jnp.float32
LANES = 128
ROWS = 8
GROUP = 4
TOP = 8


def scale_of(moment):
    a, b, e = moment // 9, moment // 3 % 3, moment % 3
    return (0.5 if a else 1.0) * (0.5 if b else 1.0) * (0.5 if e else 1.0)


def third_of(moment):
    a, b, e = moment // 9, moment // 3 % 3, moment % 3
    return (1.0 / 3.0) ** ((a == 2) + (b == 2) + (e == 2))


def axis_triples():
    for stride in (9, 3, 1):
        for base in range(27):
            if base // stride % 3 == 0:
                yield base, base + stride, base + 2 * stride


def to_moments(f):
    m = list(f)
    for low, mid, high in axis_triples():
        total = m[high] + m[low]
        m[low], m[mid], m[high] = total + m[mid], m[high] - m[low], total
    return m


def to_populations(m):
    g = list(m)
    for low, mid, high in axis_triples():
        g[low], g[mid], g[high] = g[high] - g[mid], g[low] - (g[high] + g[high]), g[high] + g[mid]
    return g


def collide(f, keep, gain, disk=None):
    m = to_moments(f)
    rho, jx, jy, jz = m[0], m[9], m[3], m[1]
    inverse = 1.0 / rho
    ux, uy, uz = jx * inverse, jy * inverse, jz * inverse
    qx, qy, qz = jx * ux, jy * uy, jz * uz
    third = rho * (1.0 / 3.0)
    ex, ey, ez = third + qx, third + qy, third + qz
    exy, exz, eyz = ex + qy, ex + qz, ey + qz
    even = {18: ex, 6: ey, 2: ez, 24: exy, 20: exz, 8: eyz, 26: exy + qz}
    odd = {}
    for k in range(27):
        a, b, e = k // 9, k // 3 % 3, k % 3
        ones = (a == 1) + (b == 1) + (e == 1)
        if ones == 1:
            odd[k] = jx if a == 1 else jy if b == 1 else jz
        elif ones == 2:
            odd[k] = jx * uy if e != 1 else jx * uz if b != 1 else jy * uz
    out = [None] * 27
    shared = {}
    for k in range(27):
        a, b, e = k // 9, k // 3 % 3, k % 3
        if k == 0:
            out[k] = rho
        elif k in (9, 3, 1):
            out[k] = odd[k] * 0.5
        elif k == 13:
            out[k] = keep(k) * m[k]
        elif k in even:
            out[k] = keep(k) * m[k] + gain(k) * even[k]
        else:
            pair = (a == 1, b == 1, e == 1)
            if pair not in shared:
                shared[pair] = odd[k]
            out[k] = keep(k) * m[k] + gain(k) * shared[pair]
    if disk is not None:
        drag = jnp.where(disk, (-0.5 * 0.75) * jx * jnp.abs(ux), 0.0)
        out[9] = out[9] + drag * 0.5
        side = drag * (0.25 / 3.0)
        out[15] = out[15] + side
        out[11] = out[11] + side
        out[17] = out[17] + drag * (0.125 / 9.0)
    return to_populations(out)


def even_orders(k):
    a, b, e = k // 9, k // 3 % 3, k % 3
    return a != 1 and b != 1 and e != 1


def rows_across(g, i, part, row):
    planes, ztiles, pitch = g.shape[2:5]
    flat = g.reshape(27 * planes * ztiles * pitch, LANES)
    return flat, pl.ds(((i * planes + 1) * ztiles + part * ROWS) * pitch + row, ROWS, stride=pitch)


def load_across(g, i, part, row):
    flat, rows = rows_across(g, i, part, row)
    return flat[rows, :]


def store_across(g, i, part, row, value):
    flat, rows = rows_across(g, i, part, row)
    flat[rows, :] = value


def stream_plane(g, out, slot, count, x, clamp):
    lane = lax.broadcasted_iota(jnp.int32, (ROWS, LANES), 1)
    low, high = lane == 0, lane == LANES - 1
    ztiles = g.shape[3]

    def body(step, carry):
        row = pl.multiple_of(step * ROWS, ROWS)
        for i in range(27):
            cx, cy, cz = i // 9 - 1, i // 3 % 3 - 1, i % 3 - 1
            source = x + 1 - cx
            if clamp is not None and cx == -1:
                source = jnp.where(clamp, jnp.minimum(source, count), source)
            tiles = [g[i // 9, i % 9, source, z, pl.ds(TOP - cy + row, ROWS), :] for z in range(ztiles)]
            if cz:
                j = 26 - i
                wall = 0 if cz == 1 else ztiles - 1
                bounced = g[j // 9, j % 9, x + 1, wall, pl.ds(pl.multiple_of(TOP + row, ROWS), ROWS), :]
                moved = [pltpu.roll(tile, 1 if cz == 1 else LANES - 1, 1) for tile in tiles]
                if cz == 1:
                    tiles = [jnp.where(low, moved[z - 1] if z else bounced, moved[z]) for z in range(ztiles)]
                else:
                    tiles = [
                        jnp.where(high, moved[z + 1] if z < ztiles - 1 else bounced, moved[z]) for z in range(ztiles)
                    ]
            for z in range(ztiles):
                out[slot, i, pl.ds(row, ROWS), pl.ds(z * LANES, LANES)] = tiles[z]
        return carry

    lax.fori_loop(0, out.shape[2] // ROWS, body, 0)


def exchange(
    size,
    rates,
    prec_hbm,
    main_hbm,
    cell_hbm,
    main_g,
    prec_g,
    main_mid,
    prec_mid,
    main_in,
    prec_in,
    cell_in,
    table,
    main_out_y,
    main_got_y,
    prec_out_y,
    prec_got_y,
    packet,
    packet_x,
    packet_y,
    inlet_c,
    main_relay,
    prec_relay,
    inlet_relay,
    load_sem,
    cell_sem,
    main_send,
    main_recv,
    prec_send,
    prec_recv,
    packet_send,
    packet_recv,
    inlet_send,
    inlet_recv,
    relay_recv,
    late_ready,
    near_ready,
):
    nx, ny = size
    gx, gy = lax.axis_index("gx"), lax.axis_index("gy")
    main_x, main_y = main_in.shape[1], main_in.shape[2]
    prec_x, prec_y = prec_in.shape[1], prec_in.shape[2]
    ztiles = main_g.shape[3]
    first, last = gx == 0, gx == nx - 1
    inner_first, inner_last = jnp.logical_not(first), jnp.logical_not(last)
    east, west = lax.rem(gx + 1, nx), lax.rem(gx + nx - 1, nx)
    north, south = lax.rem(gy + 1, ny), lax.rem(gy + ny - 1, ny)
    half = ny // 2

    place = lax.rem(gx, GROUP)
    up_source = jnp.logical_and(place == GROUP - 1, inner_last)
    down_source = jnp.logical_and(place == 0, inner_first)
    up_relay = jnp.logical_and(place == 0, gx + GROUP < nx)
    down_relay = jnp.logical_and(place == GROUP - 1, gx - GROUP >= 0)
    crossing = jnp.logical_or(up_source, down_source)
    relaying = jnp.logical_or(up_relay, down_relay)
    relay_from = jnp.where(up_relay, gx + GROUP - 1, gx - GROUP + 1)
    relay_to = jnp.where(up_relay, gx + GROUP, gx - GROUP)
    relay_of = jnp.where(up_source, gx - GROUP + 1, gx + GROUP - 1)
    relay_back = jnp.where(down_source, gx - GROUP, gx + GROUP)

    passing = gx == nx - GROUP
    odd = lax.rem(gy, 2) == 1
    inlet_block = lax.div(gy, 2)
    corner_block = jnp.where(odd, lax.rem(lax.div(gy + 1, 2), half), lax.rem(lax.div(gy, 2) + half - 1, half))

    beside_last = gx == nx - 2
    below_last = gx == nx - 1 - GROUP
    barrier = pltpu.get_barrier_semaphore()

    def greet(device):
        pl.semaphore_signal(barrier, inc=1, device_id=device, device_id_type=MESH)

    greet((west, gy))

    @pl.when(last)
    def _():
        greet((west, south))
        greet((west, north))
        greet((gx - GROUP, gy))

    @pl.when(inner_last)
    def _():
        greet((gx, south))
        greet((gx, north))

    @pl.when(gx < nx - 2)
    def _():
        greet((east, gy))

    @pl.when(relaying)
    def _():
        greet((relay_from, gy))

    @pl.when(jnp.logical_and(crossing, jnp.logical_not(below_last)))
    def _():
        greet((relay_back, gy))

    @pl.when(passing)
    def _():
        greet((nx - 1, gy))

    @pl.when(first)
    def _():
        source = jnp.where(gy < half, nx - 1, nx - GROUP)
        greet((source, lax.rem(2 * gy, ny)))
        greet((source, lax.rem(2 * gy + 1, ny)))
        greet((nx - 1, lax.rem(2 * gy + ny - 1, ny)))
        greet((nx - 1, lax.rem(2 * gy + 2, ny)))
        greet((nx - 1, south))
        greet((nx - 1, north))

    def one_if(condition):
        return jnp.where(condition, 1, 0)

    greetings = 3 + one_if(inner_first) + one_if(relaying) + one_if(crossing) + one_if(passing)
    greetings = jnp.where(last, 7, greetings + 2 * one_if(beside_last) + one_if(below_last))

    def main_load(x):
        return pltpu.make_async_copy(main_hbm.at[:, x], main_in.at[:, x], load_sem.at[x])

    def prec_load(x):
        return pltpu.make_async_copy(prec_hbm.at[:, x], prec_in.at[:, x], load_sem.at[main_x + x])

    cell_load = pltpu.make_async_copy(cell_hbm, cell_in, cell_sem)
    prec_load(prec_x - 1).start()
    cell_load.start()
    main_load(main_x - 1).start()
    main_load(0).start()
    prec_load(0).start()
    for x in range(1, main_x - 1):
        main_load(x).start()
    for x in range(1, prec_x - 1):
        prec_load(x).start()

    @pl.when(last)
    def _():
        pl.semaphore_wait(barrier, greetings)
        pl.semaphore_signal(late_ready, inc=1, device_id=(0, gy), device_id_type=MESH)

    for k in range(27):
        rate = rates[k]
        kept = scale_of(k) * (1.0 - rate)
        table[k] = jnp.full((ROWS, LANES), kept, F32)
        factor = third_of(k) * (3.0 if even_orders(k) else 1.0)
        table[27 + k] = jnp.full((ROWS, LANES), scale_of(k) * factor * rate, F32)

    def keep(k):
        return table[k]

    def gain(k):
        return table[27 + k]

    def tile_of(step):
        row = pl.multiple_of(lax.div(step, ztiles) * ROWS, ROWS)
        z = lax.rem(step, ztiles)
        return row, z, pl.multiple_of(z * LANES, LANES)

    def main_plane(x):
        def body(step, carry):
            row, z, lane = tile_of(step)
            rows, lanes = pl.ds(row, ROWS), pl.ds(lane, LANES)
            flags = cell_in[x, rows, lanes]
            g = collide([main_in[i, x, rows, lanes] for i in range(27)], keep, gain, flags == 2)
            solid = flags == 1
            for i in range(27):
                value = jnp.where(solid, main_in[26 - i, x, rows, lanes], g[i])
                main_g[i // 9, i % 9, x + 1, z, pl.ds(pl.multiple_of(TOP + row, ROWS), ROWS), :] = value
            return carry

        lax.fori_loop(0, main_y // ROWS * ztiles, body, 0)

    def prec_plane(x):
        def body(step, carry):
            row, z, lane = tile_of(step)
            rows, lanes = pl.ds(row, ROWS), pl.ds(lane, LANES)
            g = collide([prec_in[i, x, rows, lanes] for i in range(27)], keep, gain)
            for i in range(27):
                prec_g[i // 9, i % 9, x + 1, z, pl.ds(pl.multiple_of(TOP + row, ROWS), ROWS), :] = g[i]
            return carry

        lax.fori_loop(0, prec_y // ROWS * ztiles, body, 0)

    def remote(src, dst, send, recv, device):
        return pltpu.make_async_remote_copy(
            src_ref=src, dst_ref=dst, send_sem=send, recv_sem=recv, device_id=device, device_id_type=MESH
        )

    near = ztiles - ztiles // 2

    class Faces:
        def __init__(self, g, count, rows, send, recv, relay, arrival):
            inner = pl.ds(TOP, rows)
            lower, upper = pl.ds(0, near), pl.ds(near, ztiles // 2)

            def face(side, zs):
                source, dest = (g.at[2, :, count, zs, inner], g.at[2, :, 0, zs, inner])
                if side:
                    source, dest = (g.at[0, :, 1, zs, inner], g.at[0, :, count + 1, zs, inner])
                return source, dest, send.at[side], recv.at[side], (west if side else east, gy)

            whole = pl.ds(0, ztiles)
            self.whole = [remote(*face(side, whole)) for side in range(2)]
            self.direct = [remote(*face(side, lower)) for side in range(2)]
            self.to_relay = [
                remote(face(side, upper)[0], relay, send.at[4], arrival, (relay_of, gy)) for side in range(2)
            ]
            self.from_relay = [
                remote(relay, face(side, upper)[1], send.at[5], recv.at[side], (relay_to, gy)) for side in range(2)
            ]

        def run(self, side, act):
            split = down_source if side else up_source

            @pl.when(split)
            def _():
                act(self.to_relay[side])
                act(self.direct[side])

            @pl.when(jnp.logical_not(split))
            def _():
                act(self.whole[side])

    def start(copy):
        copy.start()

    def sent(copy):
        copy.wait_send()

    main_faces = Faces(main_g, main_x, main_y, main_send, main_recv, main_relay, relay_recv.at[0])
    prec_faces = Faces(prec_g, prec_x, prec_y, prec_send, prec_recv, prec_relay, relay_recv.at[1])

    def pack_corners(lattice, side):
        g, count, rows = ((main_g, main_x, main_y), (prec_g, prec_x, prec_y))[lattice]
        a, x = (0, 1) if side else (2, count)
        for up in range(2):
            row = TOP if up else TOP + rows - 1
            for e in range(3):
                for z in range(ztiles):
                    line = g[a, (0 if up else 6) + e, x, z, pl.ds(row, 1), :]
                    packet[side, up, lattice, pl.ds(e * ztiles + z, 1), :] = line

    packets_x = [
        remote(packet.at[side], packet_x.at[side], packet_send.at[side], packet_recv.at[side], ((east, west)[side], gy))
        for side in range(2)
    ]
    packets_y = [
        remote(
            packet_x.at[:, up], packet_y.at[up], packet_send.at[2 + up], packet_recv.at[2 + up], (gx, (north, south)[up])
        )
        for up in range(2)
    ]

    wrap_corners = [
        remote(
            packet.at[0, up, 1], packet_y.at[up, 0, 1], inlet_send.at[4 + up], inlet_recv.at[2 + up],
            (0, (north, south)[up]),
        )
        for up in range(2)
    ]
    west_packets_y = [
        remote(
            packet_x.at[1, up], packet_y.at[up, 1], packet_send.at[2 + up], packet_recv.at[2 + up],
            (gx, (north, south)[up]),
        )
        for up in range(2)
    ]

    inlet_rows = pl.ds(pl.multiple_of(TOP + lax.rem(gy, 2) * prec_y, ROWS), prec_y)
    outlet = prec_g.at[2, :, prec_x, :, pl.ds(TOP, prec_y)]
    inlet_direct = remote(
        outlet, main_g.at[2, :, 0, :, inlet_rows], inlet_send.at[0], main_recv.at[0], (0, inlet_block)
    )
    inlet_to_relay = remote(outlet, inlet_relay, inlet_send.at[1], relay_recv.at[2], (nx - GROUP, gy))
    inlet_from_relay = remote(
        inlet_relay, main_g.at[2, :, 0, :, inlet_rows], inlet_send.at[0], main_recv.at[0], (0, inlet_block + half)
    )
    inlet_corners = [
        [
            remote(
                packet.at[0, up, 1], inlet_c.at[up], inlet_send.at[2 + target], inlet_recv.at[up],
                (0, corner_block + target * half),
            )
            for target in range(2)
        ]
        for up in range(2)
    ]

    def inlet_run(act):
        act(wrap_corners[0])
        act(wrap_corners[1])
        act(inlet_to_relay)
        act(inlet_direct)
        for up, chosen in ((0, odd), (1, jnp.logical_not(odd))):

            @pl.when(chosen)
            def _():
                act(inlet_corners[up][0])
                act(inlet_corners[up][1])

    prec_load(prec_x - 1).wait()
    prec_plane(prec_x - 1)
    pack_corners(1, 0)

    @pl.when(last)
    def _():
        inlet_run(start)
        prec_faces.whole[0].start()

    main_load(main_x - 1).wait()
    cell_load.wait()
    main_plane(main_x - 1)
    pack_corners(0, 0)

    @pl.when(inner_last)
    def _():
        pl.semaphore_wait(barrier, greetings)

    def ready(device):
        pl.semaphore_signal(near_ready, inc=1, device_id=device, device_id_type=MESH)

    @pl.when(beside_last)
    def _():
        for row in (gy, south, north):
            ready((nx - 1, row))

    @pl.when(below_last)
    def _():
        ready((nx - 1, gy))

    @pl.when(inner_last)
    def _():
        packets_x[0].start()
        main_faces.run(0, start)
        prec_faces.run(0, start)

    main_load(0).wait()
    main_plane(0)
    pack_corners(0, 1)
    prec_load(0).wait()
    prec_plane(0)
    pack_corners(1, 1)

    @pl.when(last)
    def _():
        pl.semaphore_wait(near_ready, 4)

    @pl.when(inner_first)
    def _():
        packets_x[1].start()
        main_faces.run(1, start)
        prec_faces.run(1, start)

    def prec_rest(x, carry):
        prec_load(x).wait()
        prec_plane(x)
        return carry

    lax.fori_loop(1, prec_x - 1, prec_rest, 0)

    def pack(g, count, rows, out_y):
        for side in range(2):
            row = TOP + rows - 1 if side == 0 else TOP
            for a in range(3):
                for e in range(3):
                    i = 9 * a + (6 if side == 0 else 0) + e
                    for part in range(count * ztiles // ROWS):
                        out_y[side, 3 * a + e, pl.ds(part * ROWS, ROWS), :] = load_across(g, i, part, row)

    def y_copies(out_y, got_y, send, recv):
        return [
            remote(out_y.at[side], got_y.at[side], send.at[2 + side], recv.at[2 + side], (gx, (north, south)[side]))
            for side in range(2)
        ]

    pack(prec_g, prec_x, prec_y, prec_out_y)
    prec_y_copies = y_copies(prec_out_y, prec_got_y, prec_send, prec_recv)
    main_y_copies = y_copies(main_out_y, main_got_y, main_send, main_recv)
    for copy in prec_y_copies:
        copy.start()

    def main_rest(x, carry):
        main_load(x).wait()
        main_plane(x)
        return carry

    lax.fori_loop(1, main_x - 1, main_rest, 0)
    pack(main_g, main_x, main_y, main_out_y)
    for copy in main_y_copies:
        copy.start()

    @pl.when(relaying)
    def _():
        main_faces.to_relay[0].wait_recv()

    @pl.when(up_relay)
    def _():
        main_faces.from_relay[0].start()

    @pl.when(down_relay)
    def _():
        main_faces.from_relay[1].start()

    @pl.when(relaying)
    def _():
        prec_faces.to_relay[0].wait_recv()

    @pl.when(up_relay)
    def _():
        prec_faces.from_relay[0].start()

    @pl.when(down_relay)
    def _():
        prec_faces.from_relay[1].start()

    @pl.when(passing)
    def _():
        inlet_to_relay.wait_recv()
        inlet_from_relay.start()

    packets_x[1].wait_recv()

    @pl.when(inner_first)
    def _():
        packets_x[0].wait_recv()
        for up in range(2):
            packets_y[up].start()

    @pl.when(first)
    def _():
        for up in range(2):
            west_packets_y[up].start()

    def unpack(g, count, rows, got_y):
        for side in range(2):
            row = TOP - 1 if side == 0 else TOP + rows
            for a in range(3):
                for e in range(3):
                    i = 9 * a + (6 if side == 0 else 0) + e
                    for part in range(count * ztiles // ROWS):
                        store_across(g, i, part, row, got_y[side, 3 * a + e, pl.ds(part * ROWS, ROWS), :])

    def unpack_corner(lattice, side, up, tile):
        g, count, rows = ((main_g, main_x, main_y), (prec_g, prec_x, prec_y))[lattice]
        a, x = (0, count + 1) if side else (2, 0)
        row = TOP + rows if up else TOP - 1
        for e in range(3):
            for z in range(ztiles):
                g[a, (0 if up else 6) + e, x, z, pl.ds(row, 1), :] = tile[pl.ds(e * ztiles + z, 1), :]

    for side in range(2):
        prec_y_copies[side].wait_recv()
    unpack(prec_g, prec_x, prec_y, prec_got_y)
    for side in range(2):
        main_y_copies[side].wait_recv()
    unpack(main_g, main_x, main_y, main_got_y)

    def main_middle(x, carry):
        stream_plane(main_g, main_mid, x - 1, main_x, x, None)
        return carry

    def prec_middle(x, carry):
        stream_plane(prec_g, prec_mid, x - 1, prec_x, x, None)
        return carry

    lax.fori_loop(1, main_x - 1, main_middle, 0)
    lax.fori_loop(1, prec_x - 1, prec_middle, 0)

    @pl.when(first)
    def _():
        pl.semaphore_wait(late_ready, 1)
        packets_x[1].start()
        prec_faces.whole[1].start()

    for up in range(2):

        @pl.when(inner_first)
        def _():
            packets_y[up].wait_recv()
            unpack_corner(0, 0, up, packet_y.at[up, 0, 0])

        @pl.when(first)
        def _():
            west_packets_y[up].wait_recv()
            wrap_corners[up].wait_recv()
            inlet_corners[up][0].wait_recv()
            unpack_corner(0, 0, up, inlet_c.at[up])

        unpack_corner(0, 1, up, packet_y.at[up, 1, 0])
        for side in range(2):
            unpack_corner(1, side, up, packet_y.at[up, side, 1])

    prec_faces.whole[0].wait_recv()
    prec_faces.whole[1].wait_recv()
    main_faces.whole[0].wait_recv()

    @pl.when(inner_last)
    def _():
        main_faces.whole[1].wait_recv()

    for copy in [*prec_y_copies, *main_y_copies, packets_x[1]]:
        copy.wait_send()
    prec_faces.run(0, sent)
    prec_faces.run(1, sent)

    @pl.when(inner_last)
    def _():
        packets_x[0].wait_send()
        main_faces.run(0, sent)

    @pl.when(inner_first)
    def _():
        for up in range(2):
            packets_y[up].wait_send()
        main_faces.run(1, sent)

    @pl.when(first)
    def _():
        for up in range(2):
            west_packets_y[up].wait_send()

    @pl.when(relaying)
    def _():
        main_faces.from_relay[0].wait_send()
        prec_faces.from_relay[0].wait_send()

    @pl.when(passing)
    def _():
        inlet_from_relay.wait_send()

    @pl.when(last)
    def _():
        inlet_run(sent)


def stream(nx, main_g, prec_g, main_mid, prec_mid, prec_next, main_next, prec_out, main_out, prec_sem, main_sem):
    last = lax.axis_index("gx") == nx - 1
    copies = []
    for mid, dest, sem in ((main_mid, main_next, main_sem), (prec_mid, prec_next, prec_sem)):
        for x in range(1, dest.shape[1] - 1):
            copies.append(pltpu.make_async_copy(mid.at[x - 1], dest.at[:, x], sem.at[x]))
            copies[-1].start()
    for g, out, dest, sem, clamp in (
        (main_g, main_out, main_next, main_sem, last),
        (prec_g, prec_out, prec_next, prec_sem, None),
    ):
        count = dest.shape[1]
        for slot, x in enumerate((0, count - 1)):
            stream_plane(g, out, slot, count, x, clamp)
            copies.append(pltpu.make_async_copy(out.at[slot], dest.at[:, x], sem.at[x]))
            copies[-1].start()
    for copy in copies:
        copy.wait()


def solution(mesh):
    nx, ny = mesh.shape["gx"], mesh.shape["gy"]

    def shards(prec_pops, main_pops, cell_type, rates):
        main_x, main_y, depth = main_pops.shape[1:]
        prec_x, prec_y = prec_pops.shape[1:3]
        ztiles = depth // LANES
        main_shape = (3, 9, main_x + 2, ztiles, main_y + 2 * TOP, LANES)
        prec_shape = (3, 9, prec_x + 2, ztiles, prec_y + 2 * TOP, LANES)
        in_hbm = pl.BlockSpec(memory_space=pltpu.HBM)
        on_chip = pl.BlockSpec(memory_space=pltpu.VMEM)
        main_g, prec_g, main_mid, prec_mid = pl.pallas_call(
            functools.partial(exchange, (nx, ny)),
            name="exchange",
            out_shape=(
                pltpu.VMEM(main_shape, F32),
                pltpu.VMEM(prec_shape, F32),
                pltpu.VMEM((main_x - 2, 27, main_y, depth), F32),
                pltpu.VMEM((prec_x - 2, 27, prec_y, depth), F32),
            ),
            in_specs=[pl.BlockSpec(memory_space=pltpu.SMEM), in_hbm, in_hbm, in_hbm],
            out_specs=(on_chip,) * 4,
            scratch_shapes=[
                pltpu.VMEM(main_pops.shape, F32),
                pltpu.VMEM(prec_pops.shape, F32),
                pltpu.VMEM(cell_type.shape, jnp.int32),
                pltpu.VMEM((54, ROWS, LANES), F32),
                pltpu.VMEM((2, 9, main_x * ztiles, LANES), F32),
                pltpu.VMEM((2, 9, main_x * ztiles, LANES), F32),
                pltpu.VMEM((2, 9, prec_x * ztiles, LANES), F32),
                pltpu.VMEM((2, 9, prec_x * ztiles, LANES), F32),
                pltpu.VMEM((2, 2, 2, ROWS, LANES), F32),
                pltpu.VMEM((2, 2, 2, ROWS, LANES), F32),
                pltpu.VMEM((2, 2, 2, ROWS, LANES), F32),
                pltpu.VMEM((2, ROWS, LANES), F32),
                pltpu.VMEM((9, ztiles // 2, main_y, LANES), F32),
                pltpu.VMEM((9, ztiles // 2, prec_y, LANES), F32),
                pltpu.VMEM((9, ztiles, prec_y, LANES), F32),
                pltpu.SemaphoreType.DMA((main_x + prec_x,)),
                pltpu.SemaphoreType.DMA,
                pltpu.SemaphoreType.DMA((6,)),
                pltpu.SemaphoreType.DMA((4,)),
                pltpu.SemaphoreType.DMA((6,)),
                pltpu.SemaphoreType.DMA((4,)),
                pltpu.SemaphoreType.DMA((4,)),
                pltpu.SemaphoreType.DMA((4,)),
                pltpu.SemaphoreType.DMA((6,)),
                pltpu.SemaphoreType.DMA((4,)),
                pltpu.SemaphoreType.DMA((3,)),
                pltpu.SemaphoreType.REGULAR,
                pltpu.SemaphoreType.REGULAR,
            ],
            compiler_params=pltpu.CompilerParams(
                collective_id=0, has_side_effects=True, vmem_limit_bytes=24 * 1024 * 1024
            ),
        )(*(pltpu.with_memory_space_constraint(x, pltpu.HBM) for x in (rates, prec_pops, main_pops, cell_type)))
        prec_next, main_next = pl.pallas_call(
            functools.partial(stream, nx),
            name="stream",
            out_shape=(
                jax.ShapeDtypeStruct(prec_pops.shape, F32),
                jax.ShapeDtypeStruct(main_pops.shape, F32),
            ),
            in_specs=[on_chip] * 4,
            out_specs=(in_hbm, in_hbm),
            scratch_shapes=[
                pltpu.VMEM((2, 27, prec_y, depth), F32),
                pltpu.VMEM((2, 27, main_y, depth), F32),
                pltpu.SemaphoreType.DMA((prec_x,)),
                pltpu.SemaphoreType.DMA((main_x,)),
            ],
            compiler_params=pltpu.CompilerParams(vmem_limit_bytes=24 * 1024 * 1024),
        )(main_g, prec_g, main_mid, prec_mid)
        return prec_next, main_next

    placed = (P(None, "gx", "gy", None), P(None, "gx", "gy", None), P("gx", "gy", None), P())
    return jax.shard_map(
        shards,
        mesh=mesh,
        in_specs=placed,
        out_specs=(P(None, "gx", "gy", None), P(None, "gx", "gy", None)),
        check_vma=False,
    )
```

```python
import functools

import jax
import jax.numpy as jnp
from jax import lax
from jax.experimental import pallas as pl
from jax.experimental.pallas import tpu as pltpu
from jax.sharding import PartitionSpec as P

MESH = pl.DeviceIdType.MESH
F32 = jnp.float32
LANES = 128
ROWS = 8
GROUP = 4
TOP = 8


def scale_of(moment):
    a, b, e = moment // 9, moment // 3 % 3, moment % 3
    return (0.5 if a else 1.0) * (0.5 if b else 1.0) * (0.5 if e else 1.0)


def third_of(moment):
    a, b, e = moment // 9, moment // 3 % 3, moment % 3
    return (1.0 / 3.0) ** ((a == 2) + (b == 2) + (e == 2))


def axis_triples():
    for stride in (9, 3, 1):
        for base in range(27):
            if base // stride % 3 == 0:
                yield base, base + stride, base + 2 * stride


def to_moments(f):
    m = list(f)
    for low, mid, high in axis_triples():
        total = m[high] + m[low]
        m[low], m[mid], m[high] = total + m[mid], m[high] - m[low], total
    return m


def to_populations(m):
    g = list(m)
    for low, mid, high in axis_triples():
        g[low], g[mid], g[high] = g[high] - g[mid], g[low] - (g[high] + g[high]), g[high] + g[mid]
    return g


def collide(f, keep, gain, disk=None):
    m = to_moments(f)
    rho, jx, jy, jz = m[0], m[9], m[3], m[1]
    inverse = 1.0 / rho
    ux, uy, uz = jx * inverse, jy * inverse, jz * inverse
    qx, qy, qz = jx * ux, jy * uy, jz * uz
    third = rho * (1.0 / 3.0)
    ex, ey, ez = third + qx, third + qy, third + qz
    exy, exz, eyz = ex + qy, ex + qz, ey + qz
    even = {18: ex, 6: ey, 2: ez, 24: exy, 20: exz, 8: eyz, 26: exy + qz}
    odd = {}
    for k in range(27):
        a, b, e = k // 9, k // 3 % 3, k % 3
        ones = (a == 1) + (b == 1) + (e == 1)
        if ones == 1:
            odd[k] = jx if a == 1 else jy if b == 1 else jz
        elif ones == 2:
            odd[k] = jx * uy if e != 1 else jx * uz if b != 1 else jy * uz
    out = [None] * 27
    shared = {}
    for k in range(27):
        a, b, e = k // 9, k // 3 % 3, k % 3
        if k == 0:
            out[k] = rho
        elif k in (9, 3, 1):
            out[k] = odd[k] * 0.5
        elif k == 13:
            out[k] = keep(k) * m[k]
        elif k in even:
            out[k] = keep(k) * m[k] + gain(k) * even[k]
        else:
            pair = (a == 1, b == 1, e == 1)
            if pair not in shared:
                shared[pair] = odd[k]
            out[k] = keep(k) * m[k] + gain(k) * shared[pair]
    if disk is not None:
        drag = jnp.where(disk, (-0.5 * 0.75) * jx * jnp.abs(ux), 0.0)
        out[9] = out[9] + drag * 0.5
        side = drag * (0.25 / 3.0)
        out[15] = out[15] + side
        out[11] = out[11] + side
        out[17] = out[17] + drag * (0.125 / 9.0)
    return to_populations(out)


def even_orders(k):
    a, b, e = k // 9, k // 3 % 3, k % 3
    return a != 1 and b != 1 and e != 1


def rows_across(g, i, part, row):
    planes, ztiles, pitch = g.shape[2:5]
    flat = g.reshape(27 * planes * ztiles * pitch, LANES)
    return flat, pl.ds(((i * planes + 1) * ztiles + part * ROWS) * pitch + row, ROWS, stride=pitch)


def load_across(g, i, part, row):
    flat, rows = rows_across(g, i, part, row)
    return flat[rows, :]


def store_across(g, i, part, row, value):
    flat, rows = rows_across(g, i, part, row)
    flat[rows, :] = value


def stream_plane(g, out, slot, count, x, clamp):
    lane = lax.broadcasted_iota(jnp.int32, (ROWS, LANES), 1)
    low, high = lane == 0, lane == LANES - 1
    ztiles = g.shape[3]

    def body(step, carry):
        row = pl.multiple_of(step * ROWS, ROWS)
        for i in range(27):
            cx, cy, cz = i // 9 - 1, i // 3 % 3 - 1, i % 3 - 1
            source = x + 1 - cx
            if clamp is not None and cx == -1:
                source = jnp.where(clamp, jnp.minimum(source, count), source)
            tiles = [g[i // 9, i % 9, source, z, pl.ds(TOP - cy + row, ROWS), :] for z in range(ztiles)]
            if cz:
                j = 26 - i
                wall = 0 if cz == 1 else ztiles - 1
                bounced = g[j // 9, j % 9, x + 1, wall, pl.ds(pl.multiple_of(TOP + row, ROWS), ROWS), :]
                moved = [pltpu.roll(tile, 1 if cz == 1 else LANES - 1, 1) for tile in tiles]
                if cz == 1:
                    tiles = [jnp.where(low, moved[z - 1] if z else bounced, moved[z]) for z in range(ztiles)]
                else:
                    tiles = [
                        jnp.where(high, moved[z + 1] if z < ztiles - 1 else bounced, moved[z]) for z in range(ztiles)
                    ]
            for z in range(ztiles):
                out[slot, i, pl.ds(row, ROWS), pl.ds(z * LANES, LANES)] = tiles[z]
        return carry

    lax.fori_loop(0, out.shape[2] // ROWS, body, 0)


def exchange(
    size,
    rates,
    prec_hbm,
    main_hbm,
    cell_hbm,
    main_g,
    prec_g,
    main_mid,
    prec_mid,
    main_in,
    prec_in,
    cell_in,
    table,
    main_out_y,
    main_got_y,
    prec_out_y,
    prec_got_y,
    packet,
    packet_x,
    packet_y,
    inlet_c,
    main_relay,
    prec_relay,
    inlet_relay,
    load_sem,
    cell_sem,
    main_send,
    main_recv,
    prec_send,
    prec_recv,
    packet_send,
    packet_recv,
    inlet_send,
    inlet_recv,
    relay_recv,
    late_ready,
    near_ready,
):
    nx, ny = size
    gx, gy = lax.axis_index("gx"), lax.axis_index("gy")
    main_x, main_y = main_in.shape[1], main_in.shape[2]
    prec_x, prec_y = prec_in.shape[1], prec_in.shape[2]
    ztiles = main_g.shape[3]
    first, last = gx == 0, gx == nx - 1
    inner_first, inner_last = jnp.logical_not(first), jnp.logical_not(last)
    east, west = lax.rem(gx + 1, nx), lax.rem(gx + nx - 1, nx)
    north, south = lax.rem(gy + 1, ny), lax.rem(gy + ny - 1, ny)
    half = ny // 2

    place = lax.rem(gx, GROUP)
    up_source = jnp.logical_and(place == GROUP - 1, inner_last)
    down_source = jnp.logical_and(place == 0, inner_first)
    up_relay = jnp.logical_and(place == 0, gx + GROUP < nx)
    down_relay = jnp.logical_and(place == GROUP - 1, gx - GROUP >= 0)
    crossing = jnp.logical_or(up_source, down_source)
    up_second = place == GROUP - 2
    down_second = jnp.logical_and(place == 1, gx >= 2)
    second = jnp.logical_or(up_second, down_second)
    second_to = jnp.where(up_second, lax.rem(gx + 2, nx), gx - 2)
    relaying = jnp.logical_or(up_relay, down_relay)
    relay_from = jnp.where(up_relay, gx + GROUP - 1, gx - GROUP + 1)
    relay_to = jnp.where(up_relay, gx + GROUP, gx - GROUP)
    relay_of = jnp.where(up_source, gx - GROUP + 1, gx + GROUP - 1)
    relay_back = jnp.where(down_source, gx - GROUP, gx + GROUP)

    passing = gx == nx - GROUP
    odd = lax.rem(gy, 2) == 1
    inlet_block = lax.div(gy, 2)
    corner_block = jnp.where(odd, lax.rem(lax.div(gy + 1, 2), half), lax.rem(lax.div(gy, 2) + half - 1, half))

    straight = jnp.logical_and(last, lax.rem(gy, 4) == 0)
    passing_face = jnp.logical_and(gx == nx - 2, lax.rem(gy, 4) != 0)

    holding = gx == GROUP - 1
    beside_last = gx == nx - 2
    below_last = gx == nx - 1 - GROUP
    barrier = pltpu.get_barrier_semaphore()

    def greet(device):
        pl.semaphore_signal(barrier, inc=1, device_id=device, device_id_type=MESH)

    greet((west, gy))

    @pl.when(last)
    def _():
        greet((west, south))
        greet((west, north))
        greet((gx - GROUP, gy))

    @pl.when(inner_last)
    def _():
        greet((gx, south))
        greet((gx, north))

        greet((east, gy))

    @pl.when(place == 0)
    def _():
        greet((lax.rem(gx + nx - 2, nx), gy))

    @pl.when(up_source)
    def _():
        greet((gx + 2, gy))

    @pl.when(relaying)
    def _():
        greet((relay_from, gy))

    @pl.when(jnp.logical_and(crossing, jnp.logical_not(below_last)))
    def _():
        greet((relay_back, gy))

    @pl.when(jnp.logical_or(passing, holding))
    def _():
        greet((nx - 1, gy))

    @pl.when(holding)
    def _():
        greet((0, gy))

    @pl.when(first)
    def _():
        source = jnp.where(gy < half, nx - 1, nx - GROUP)
        greet((source, lax.rem(2 * gy, ny)))
        greet((source, lax.rem(2 * gy + 1, ny)))
        greet((nx - 1, lax.rem(2 * gy + ny - 1, ny)))
        greet((nx - 1, lax.rem(2 * gy + 2, ny)))
        greet((nx - 1, south))
        greet((nx - 1, north))

    def one_if(condition):
        return jnp.where(condition, 1, 0)

    greetings = 3 + one_if(inner_first) + one_if(relaying) + one_if(crossing) + one_if(passing) + one_if(second)
    greetings = greetings + one_if(first)
    greetings = jnp.where(last, 9, greetings + 2 * one_if(beside_last) + one_if(below_last))

    def main_load(x):
        return pltpu.make_async_copy(main_hbm.at[:, x], main_in.at[:, x], load_sem.at[x])

    def prec_load(x):
        return pltpu.make_async_copy(prec_hbm.at[:, x], prec_in.at[:, x], load_sem.at[main_x + x])

    cell_load = pltpu.make_async_copy(cell_hbm, cell_in, cell_sem)
    prec_load(prec_x - 1).start()
    cell_load.start()
    main_load(main_x - 1).start()
    main_load(0).start()
    prec_load(0).start()
    for x in range(1, main_x - 1):
        main_load(x).start()
    for x in range(1, prec_x - 1):
        prec_load(x).start()

    @pl.when(last)
    def _():
        pl.semaphore_wait(barrier, greetings)
        pl.semaphore_signal(late_ready, inc=1, device_id=(0, gy), device_id_type=MESH)
        pl.semaphore_signal(late_ready, inc=1, device_id=(GROUP - 1, gy), device_id_type=MESH)

    for k in range(27):
        rate = rates[k]
        kept = scale_of(k) * (1.0 - rate)
        table[k] = jnp.full((ROWS, LANES), kept, F32)
        factor = third_of(k) * (3.0 if even_orders(k) else 1.0)
        table[27 + k] = jnp.full((ROWS, LANES), scale_of(k) * factor * rate, F32)

    def keep(k):
        return table[k]

    def gain(k):
        return table[27 + k]

    def tile_of(step):
        row = pl.multiple_of(lax.div(step, ztiles) * ROWS, ROWS)
        z = lax.rem(step, ztiles)
        return row, z, pl.multiple_of(z * LANES, LANES)

    def main_plane(x):
        def body(step, carry):
            row, z, lane = tile_of(step)
            rows, lanes = pl.ds(row, ROWS), pl.ds(lane, LANES)
            flags = cell_in[x, rows, lanes]
            g = collide([main_in[i, x, rows, lanes] for i in range(27)], keep, gain, flags == 2)
            solid = flags == 1
            for i in range(27):
                value = jnp.where(solid, main_in[26 - i, x, rows, lanes], g[i])
                main_g[i // 9, i % 9, x + 1, z, pl.ds(pl.multiple_of(TOP + row, ROWS), ROWS), :] = value
            return carry

        lax.fori_loop(0, main_y // ROWS * ztiles, body, 0)

    def prec_plane(x):
        def body(step, carry):
            row, z, lane = tile_of(step)
            rows, lanes = pl.ds(row, ROWS), pl.ds(lane, LANES)
            g = collide([prec_in[i, x, rows, lanes] for i in range(27)], keep, gain)
            for i in range(27):
                prec_g[i // 9, i % 9, x + 1, z, pl.ds(pl.multiple_of(TOP + row, ROWS), ROWS), :] = g[i]
            return carry

        lax.fori_loop(0, prec_y // ROWS * ztiles, body, 0)

    def remote(src, dst, send, recv, device):
        return pltpu.make_async_remote_copy(
            src_ref=src, dst_ref=dst, send_sem=send, recv_sem=recv, device_id=device, device_id_type=MESH
        )

    near = ztiles - ztiles // 2

    def face(g, count, rows, side, zs, send, recv):
        inner = pl.ds(TOP, rows)
        source, dest = (g.at[2, :, count, zs, inner], g.at[2, :, 0, zs, inner])
        if side:
            source, dest = (g.at[0, :, 1, zs, inner], g.at[0, :, count + 1, zs, inner])
        return source, dest, send.at[side], recv.at[side], (west if side else east, gy)

    class MainFaces:
        def __init__(self):
            whole, lower, upper = pl.ds(0, ztiles), pl.ds(0, near), pl.ds(near, ztiles // 2)
            parts = (main_g, main_x, main_y)
            self.whole = [remote(*face(*parts, side, whole, main_send, main_recv)) for side in range(2)]
            self.direct = [remote(*face(*parts, side, lower, main_send, main_recv)) for side in range(2)]
            ends = [face(*parts, side, upper, main_send, main_recv) for side in range(2)]
            self.to_relay = [
                remote(end[0], main_relay, main_send.at[4], relay_recv.at[0], (relay_of, gy)) for end in ends
            ]
            self.from_relay = [remote(main_relay, end[1], main_send.at[5], end[3], (relay_to, gy)) for end in ends]

        def run(self, side, act):
            split = down_source if side else up_source

            @pl.when(split)
            def _():
                act(self.to_relay[side])
                act(self.direct[side])

            @pl.when(jnp.logical_not(split))
            def _():
                act(self.whole[side])

    class PrecFaces:
        def __init__(self):
            ends = [face(prec_g, prec_x, prec_y, side, pl.ds(0, ztiles), prec_send, prec_recv) for side in range(2)]
            self.whole = [remote(*end) for end in ends]
            self.to_relay = [
                remote(ends[side][0], prec_relay, prec_send.at[4], relay_recv.at[1], ((west, east)[side], gy))
                for side in range(2)
            ]
            self.from_relay = [remote(prec_relay, end[1], prec_send.at[5], end[3], (second_to, gy)) for end in ends]
            self.west_to_hold = remote(
                ends[1][0], prec_relay, prec_send.at[1], relay_recv.at[1], (GROUP - 1, gy)
            )
            self.west_from_hold = remote(prec_relay, ends[1][1], prec_send.at[5], ends[1][3], (nx - 1, gy))
        def run(self, side, act):
            split = down_source if side else up_source

            @pl.when(split)
            def _():
                act(self.to_relay[side])

            @pl.when(jnp.logical_not(split))
            def _():
                act(self.whole[side])

    def start(copy):
        copy.start()

    def sent(copy):
        copy.wait_send()

    main_faces, prec_faces = MainFaces(), PrecFaces()

    def pack_corners(lattice, side):
        g, count, rows = ((main_g, main_x, main_y), (prec_g, prec_x, prec_y))[lattice]
        a, x = (0, 1) if side else (2, count)
        for up in range(2):
            row = TOP if up else TOP + rows - 1
            for e in range(3):
                for z in range(ztiles):
                    line = g[a, (0 if up else 6) + e, x, z, pl.ds(row, 1), :]
                    packet[side, up, lattice, pl.ds(e * ztiles + z, 1), :] = line

    packets_x = [
        remote(packet.at[side], packet_x.at[side], packet_send.at[side], packet_recv.at[side], ((east, west)[side], gy))
        for side in range(2)
    ]
    packets_y = [
        remote(
            packet_x.at[:, up], packet_y.at[up], packet_send.at[2 + up], packet_recv.at[2 + up], (gx, (north, south)[up])
        )
        for up in range(2)
    ]

    wrap_corners = [
        remote(
            packet.at[0, up, 1], packet_y.at[up, 0, 1], inlet_send.at[4 + up], inlet_recv.at[2 + up],
            (0, (north, south)[up]),
        )
        for up in range(2)
    ]
    west_packets_y = [
        remote(
            packet_x.at[1, up], packet_y.at[up, 1], packet_send.at[2 + up], packet_recv.at[2 + up],
            (gx, (north, south)[up]),
        )
        for up in range(2)
    ]

    inlet_rows = pl.ds(pl.multiple_of(TOP + lax.rem(gy, 2) * prec_y, ROWS), prec_y)
    outlet = prec_g.at[2, :, prec_x, :, pl.ds(TOP, prec_y)]
    inlet_direct = remote(
        outlet, main_g.at[2, :, 0, :, inlet_rows], inlet_send.at[0], main_recv.at[0], (0, inlet_block)
    )
    inlet_to_relay = remote(outlet, inlet_relay, inlet_send.at[1], relay_recv.at[2], (nx - GROUP, gy))
    inlet_from_relay = remote(
        inlet_relay, main_g.at[2, :, 0, :, inlet_rows], inlet_send.at[0], main_recv.at[0], (0, inlet_block + half)
    )
    inlet_corners = [
        [
            remote(
                packet.at[0, up, 1], inlet_c.at[up], inlet_send.at[2 + target], inlet_recv.at[up],
                (0, corner_block + target * half),
            )
            for target in range(2)
        ]
        for up in range(2)
    ]

    def inlet_run(act):
        act(wrap_corners[0])
        act(wrap_corners[1])
        for up, chosen in ((0, odd), (1, jnp.logical_not(odd))):

            @pl.when(chosen)
            def _():
                act(inlet_corners[up][0])
                act(inlet_corners[up][1])

        act(inlet_to_relay)

        @pl.when(jnp.logical_not(straight))
        def _():
            act(prec_faces.to_relay[0])

        act(inlet_direct)

        @pl.when(straight)
        def _():
            act(prec_faces.whole[0])

    prec_load(prec_x - 1).wait()
    prec_plane(prec_x - 1)
    pack_corners(1, 0)

    @pl.when(last)
    def _():
        inlet_run(start)

    main_load(main_x - 1).wait()
    cell_load.wait()
    main_plane(main_x - 1)
    pack_corners(0, 0)

    @pl.when(inner_last)
    def _():
        pl.semaphore_wait(barrier, greetings)

    def ready(device):
        pl.semaphore_signal(near_ready, inc=1, device_id=device, device_id_type=MESH)

    @pl.when(beside_last)
    def _():
        for row in (gy, south, north):
            ready((nx - 1, row))

    @pl.when(below_last)
    def _():
        ready((nx - 1, gy))

    @pl.when(inner_last)
    def _():
        packets_x[0].start()

    @pl.when(jnp.logical_and(inner_last, jnp.logical_not(down_source)))
    def _():
        main_faces.run(0, start)
        prec_faces.run(0, start)

    main_load(0).wait()
    main_plane(0)
    pack_corners(0, 1)
    prec_load(0).wait()
    prec_plane(0)
    pack_corners(1, 1)

    @pl.when(last)
    def _():
        pl.semaphore_wait(near_ready, 4)

    @pl.when(inner_first)
    def _():
        packets_x[1].start()
        prec_faces.run(1, start)
        main_faces.run(1, start)

    @pl.when(first)
    def _():
        prec_faces.west_to_hold.start()

    @pl.when(down_source)
    def _():
        main_faces.run(0, start)
        prec_faces.run(0, start)

    def prec_rest(x, carry):
        prec_load(x).wait()
        prec_plane(x)
        return carry

    lax.fori_loop(1, prec_x - 1, prec_rest, 0)

    def pack(g, count, rows, out_y):
        for side in range(2):
            row = TOP + rows - 1 if side == 0 else TOP
            for a in range(3):
                for e in range(3):
                    i = 9 * a + (6 if side == 0 else 0) + e
                    for part in range(count * ztiles // ROWS):
                        out_y[side, 3 * a + e, pl.ds(part * ROWS, ROWS), :] = load_across(g, i, part, row)

    def y_copies(out_y, got_y, send, recv):
        return [
            remote(out_y.at[side], got_y.at[side], send.at[2 + side], recv.at[2 + side], (gx, (north, south)[side]))
            for side in range(2)
        ]

    pack(prec_g, prec_x, prec_y, prec_out_y)
    prec_y_copies = y_copies(prec_out_y, prec_got_y, prec_send, prec_recv)
    main_y_copies = y_copies(main_out_y, main_got_y, main_send, main_recv)
    for copy in prec_y_copies:
        copy.start()

    def main_rest(x, carry):
        main_load(x).wait()
        main_plane(x)
        return carry

    lax.fori_loop(1, main_x // 2, main_rest, 0)

    @pl.when(passing)
    def _():
        inlet_to_relay.wait_recv()
        inlet_from_relay.start()

    @pl.when(passing_face)
    def _():
        prec_faces.to_relay[0].wait_recv()
        prec_faces.from_relay[0].start()

    lax.fori_loop(main_x // 2, main_x - 1, main_rest, 0)
    pack(main_g, main_x, main_y, main_out_y)
    for copy in main_y_copies:
        copy.start()

    @pl.when(relaying)
    def _():
        main_faces.to_relay[0].wait_recv()

    @pl.when(up_relay)
    def _():
        main_faces.from_relay[0].start()

    @pl.when(down_relay)
    def _():
        main_faces.from_relay[1].start()

    @pl.when(jnp.logical_and(second, jnp.logical_not(beside_last)))
    def _():
        prec_faces.to_relay[0].wait_recv()

    @pl.when(jnp.logical_and(up_second, jnp.logical_not(beside_last)))
    def _():
        prec_faces.from_relay[0].start()

    @pl.when(down_second)
    def _():
        prec_faces.from_relay[1].start()

    packets_x[1].wait_recv()

    @pl.when(inner_first)
    def _():
        packets_x[0].wait_recv()
        for up in range(2):
            packets_y[up].start()

    @pl.when(first)
    def _():
        for up in range(2):
            west_packets_y[up].start()

    def unpack(g, count, rows, got_y):
        for side in range(2):
            row = TOP - 1 if side == 0 else TOP + rows
            for a in range(3):
                for e in range(3):
                    i = 9 * a + (6 if side == 0 else 0) + e
                    for part in range(count * ztiles // ROWS):
                        store_across(g, i, part, row, got_y[side, 3 * a + e, pl.ds(part * ROWS, ROWS), :])

    def unpack_corner(lattice, side, up, tile):
        g, count, rows = ((main_g, main_x, main_y), (prec_g, prec_x, prec_y))[lattice]
        a, x = (0, count + 1) if side else (2, 0)
        row = TOP + rows if up else TOP - 1
        for e in range(3):
            for z in range(ztiles):
                g[a, (0 if up else 6) + e, x, z, pl.ds(row, 1), :] = tile[pl.ds(e * ztiles + z, 1), :]

    for side in range(2):
        prec_y_copies[side].wait_recv()
    unpack(prec_g, prec_x, prec_y, prec_got_y)
    for side in range(2):
        main_y_copies[side].wait_recv()
    unpack(main_g, main_x, main_y, main_got_y)

    def main_middle(x, carry):
        stream_plane(main_g, main_mid, x - 1, main_x, x, None)
        return carry

    def prec_middle(x, carry):
        stream_plane(prec_g, prec_mid, x - 1, prec_x, x, None)
        return carry

    lax.fori_loop(1, main_x - 1, main_middle, 0)
    lax.fori_loop(1, prec_x - 1, prec_middle, 0)

    @pl.when(first)
    def _():
        pl.semaphore_wait(late_ready, 1)
        packets_x[1].start()

    @pl.when(holding)
    def _():
        prec_faces.west_to_hold.wait_recv()
        pl.semaphore_wait(late_ready, 1)
        prec_faces.west_from_hold.start()

    for up in range(2):

        @pl.when(inner_first)
        def _():
            packets_y[up].wait_recv()
            unpack_corner(0, 0, up, packet_y.at[up, 0, 0])

        @pl.when(first)
        def _():
            west_packets_y[up].wait_recv()
            wrap_corners[up].wait_recv()
            inlet_corners[up][0].wait_recv()
            unpack_corner(0, 0, up, inlet_c.at[up])

        unpack_corner(0, 1, up, packet_y.at[up, 1, 0])
        for side in range(2):
            unpack_corner(1, side, up, packet_y.at[up, side, 1])

    prec_faces.whole[0].wait_recv()
    prec_faces.whole[1].wait_recv()
    main_faces.whole[0].wait_recv()

    @pl.when(inner_last)
    def _():
        main_faces.whole[1].wait_recv()

    for copy in [*prec_y_copies, *main_y_copies, packets_x[1]]:
        copy.wait_send()

    @pl.when(first)
    def _():
        prec_faces.west_to_hold.wait_send()

    @pl.when(holding)
    def _():
        prec_faces.west_from_hold.wait_send()

    @pl.when(inner_last)
    def _():
        prec_faces.run(0, sent)
        packets_x[0].wait_send()
        main_faces.run(0, sent)

    @pl.when(inner_first)
    def _():
        for up in range(2):
            packets_y[up].wait_send()
        main_faces.run(1, sent)
        prec_faces.run(1, sent)

    @pl.when(first)
    def _():
        for up in range(2):
            west_packets_y[up].wait_send()

    @pl.when(relaying)
    def _():
        main_faces.from_relay[0].wait_send()

    @pl.when(jnp.logical_or(passing_face, jnp.logical_and(second, jnp.logical_not(beside_last))))
    def _():
        prec_faces.from_relay[0].wait_send()

    @pl.when(passing)
    def _():
        inlet_from_relay.wait_send()

    @pl.when(last)
    def _():
        inlet_run(sent)


def stream(nx, main_g, prec_g, main_mid, prec_mid, prec_next, main_next, prec_out, main_out, prec_sem, main_sem):
    last = lax.axis_index("gx") == nx - 1
    copies = []
    for mid, dest, sem in ((main_mid, main_next, main_sem), (prec_mid, prec_next, prec_sem)):
        for x in range(1, dest.shape[1] - 1):
            copies.append(pltpu.make_async_copy(mid.at[x - 1], dest.at[:, x], sem.at[x]))
            copies[-1].start()
    for g, out, dest, sem, clamp in (
        (main_g, main_out, main_next, main_sem, last),
        (prec_g, prec_out, prec_next, prec_sem, None),
    ):
        count = dest.shape[1]
        for slot, x in enumerate((0, count - 1)):
            stream_plane(g, out, slot, count, x, clamp)
            copies.append(pltpu.make_async_copy(out.at[slot], dest.at[:, x], sem.at[x]))
            copies[-1].start()
    for copy in copies:
        copy.wait()


def solution(mesh):
    nx, ny = mesh.shape["gx"], mesh.shape["gy"]

    def shards(prec_pops, main_pops, cell_type, rates):
        main_x, main_y, depth = main_pops.shape[1:]
        prec_x, prec_y = prec_pops.shape[1:3]
        ztiles = depth // LANES
        main_shape = (3, 9, main_x + 2, ztiles, main_y + 2 * TOP, LANES)
        prec_shape = (3, 9, prec_x + 2, ztiles, prec_y + 2 * TOP, LANES)
        in_hbm = pl.BlockSpec(memory_space=pltpu.HBM)
        on_chip = pl.BlockSpec(memory_space=pltpu.VMEM)
        main_g, prec_g, main_mid, prec_mid = pl.pallas_call(
            functools.partial(exchange, (nx, ny)),
            name="exchange",
            out_shape=(
                pltpu.VMEM(main_shape, F32),
                pltpu.VMEM(prec_shape, F32),
                pltpu.VMEM((main_x - 2, 27, main_y, depth), F32),
                pltpu.VMEM((prec_x - 2, 27, prec_y, depth), F32),
            ),
            in_specs=[pl.BlockSpec(memory_space=pltpu.SMEM), in_hbm, in_hbm, in_hbm],
            out_specs=(on_chip,) * 4,
            scratch_shapes=[
                pltpu.VMEM(main_pops.shape, F32),
                pltpu.VMEM(prec_pops.shape, F32),
                pltpu.VMEM(cell_type.shape, jnp.int32),
                pltpu.VMEM((54, ROWS, LANES), F32),
                pltpu.VMEM((2, 9, main_x * ztiles, LANES), F32),
                pltpu.VMEM((2, 9, main_x * ztiles, LANES), F32),
                pltpu.VMEM((2, 9, prec_x * ztiles, LANES), F32),
                pltpu.VMEM((2, 9, prec_x * ztiles, LANES), F32),
                pltpu.VMEM((2, 2, 2, ROWS, LANES), F32),
                pltpu.VMEM((2, 2, 2, ROWS, LANES), F32),
                pltpu.VMEM((2, 2, 2, ROWS, LANES), F32),
                pltpu.VMEM((2, ROWS, LANES), F32),
                pltpu.VMEM((9, ztiles // 2, main_y, LANES), F32),
                pltpu.VMEM((9, ztiles, prec_y, LANES), F32),
                pltpu.VMEM((9, ztiles, prec_y, LANES), F32),
                pltpu.SemaphoreType.DMA((main_x + prec_x,)),
                pltpu.SemaphoreType.DMA,
                pltpu.SemaphoreType.DMA((6,)),
                pltpu.SemaphoreType.DMA((4,)),
                pltpu.SemaphoreType.DMA((6,)),
                pltpu.SemaphoreType.DMA((4,)),
                pltpu.SemaphoreType.DMA((4,)),
                pltpu.SemaphoreType.DMA((4,)),
                pltpu.SemaphoreType.DMA((6,)),
                pltpu.SemaphoreType.DMA((4,)),
                pltpu.SemaphoreType.DMA((3,)),
                pltpu.SemaphoreType.REGULAR,
                pltpu.SemaphoreType.REGULAR,
            ],
            compiler_params=pltpu.CompilerParams(
                collective_id=0, has_side_effects=True, vmem_limit_bytes=24 * 1024 * 1024
            ),
        )(*(pltpu.with_memory_space_constraint(x, pltpu.HBM) for x in (rates, prec_pops, main_pops, cell_type)))
        prec_next, main_next = pl.pallas_call(
            functools.partial(stream, nx),
            name="stream",
            out_shape=(
                jax.ShapeDtypeStruct(prec_pops.shape, F32),
                jax.ShapeDtypeStruct(main_pops.shape, F32),
            ),
            in_specs=[on_chip] * 4,
            out_specs=(in_hbm, in_hbm),
            scratch_shapes=[
                pltpu.VMEM((2, 27, prec_y, depth), F32),
                pltpu.VMEM((2, 27, main_y, depth), F32),
                pltpu.SemaphoreType.DMA((prec_x,)),
                pltpu.SemaphoreType.DMA((main_x,)),
            ],
            compiler_params=pltpu.CompilerParams(vmem_limit_bytes=24 * 1024 * 1024),
        )(main_g, prec_g, main_mid, prec_mid)
        return prec_next, main_next

    placed = (P(None, "gx", "gy", None), P(None, "gx", "gy", None), P("gx", "gy", None), P())
    return jax.shard_map(
        shards,
        mesh=mesh,
        in_specs=placed,
        out_specs=(P(None, "gx", "gy", None), P(None, "gx", "gy", None)),
        check_vma=False,
    )
```

```python
import functools

import jax
import jax.numpy as jnp
from jax import lax
from jax.experimental import pallas as pl
from jax.experimental.pallas import tpu as pltpu
from jax.sharding import PartitionSpec as P

MESH = pl.DeviceIdType.MESH
F32 = jnp.float32
LANES = 128
ROWS = 8
GROUP = 4
TOP = 8


def scale_of(moment):
    a, b, e = moment // 9, moment // 3 % 3, moment % 3
    return (0.5 if a else 1.0) * (0.5 if b else 1.0) * (0.5 if e else 1.0)


def third_of(moment):
    a, b, e = moment // 9, moment // 3 % 3, moment % 3
    return (1.0 / 3.0) ** ((a == 2) + (b == 2) + (e == 2))


def axis_triples():
    for stride in (9, 3, 1):
        for base in range(27):
            if base // stride % 3 == 0:
                yield base, base + stride, base + 2 * stride


def to_moments(f):
    m = list(f)
    for low, mid, high in axis_triples():
        total = m[high] + m[low]
        m[low], m[mid], m[high] = total + m[mid], m[high] - m[low], total
    return m


def to_populations(m):
    g = list(m)
    for low, mid, high in axis_triples():
        g[low], g[mid], g[high] = g[high] - g[mid], g[low] - (g[high] + g[high]), g[high] + g[mid]
    return g


def collide(f, keep, gain, disk=None):
    m = to_moments(f)
    rho, jx, jy, jz = m[0], m[9], m[3], m[1]
    inverse = 1.0 / rho
    ux, uy, uz = jx * inverse, jy * inverse, jz * inverse
    qx, qy, qz = jx * ux, jy * uy, jz * uz
    third = rho * (1.0 / 3.0)
    ex, ey, ez = third + qx, third + qy, third + qz
    exy, exz, eyz = ex + qy, ex + qz, ey + qz
    even = {18: ex, 6: ey, 2: ez, 24: exy, 20: exz, 8: eyz, 26: exy + qz}
    odd = {}
    for k in range(27):
        a, b, e = k // 9, k // 3 % 3, k % 3
        ones = (a == 1) + (b == 1) + (e == 1)
        if ones == 1:
            odd[k] = jx if a == 1 else jy if b == 1 else jz
        elif ones == 2:
            odd[k] = jx * uy if e != 1 else jx * uz if b != 1 else jy * uz
    out = [None] * 27
    shared = {}
    for k in range(27):
        a, b, e = k // 9, k // 3 % 3, k % 3
        if k == 0:
            out[k] = rho
        elif k in (9, 3, 1):
            out[k] = odd[k] * 0.5
        elif k == 13:
            out[k] = keep(k) * m[k]
        elif k in even:
            out[k] = keep(k) * m[k] + gain(k) * even[k]
        else:
            pair = (a == 1, b == 1, e == 1)
            if pair not in shared:
                shared[pair] = odd[k]
            out[k] = keep(k) * m[k] + gain(k) * shared[pair]
    if disk is not None:
        drag = jnp.where(disk, (-0.5 * 0.75) * jx * jnp.abs(ux), 0.0)
        out[9] = out[9] + drag * 0.5
        side = drag * (0.25 / 3.0)
        out[15] = out[15] + side
        out[11] = out[11] + side
        out[17] = out[17] + drag * (0.125 / 9.0)
    return to_populations(out)


def even_orders(k):
    a, b, e = k // 9, k // 3 % 3, k % 3
    return a != 1 and b != 1 and e != 1


def rows_across(g, i, part, row):
    planes, ztiles, pitch = g.shape[2:5]
    flat = g.reshape(27 * planes * ztiles * pitch, LANES)
    return flat, pl.ds(((i * planes + 1) * ztiles + part * ROWS) * pitch + row, ROWS, stride=pitch)


def load_across(g, i, part, row):
    flat, rows = rows_across(g, i, part, row)
    return flat[rows, :]


def store_across(g, i, part, row, value):
    flat, rows = rows_across(g, i, part, row)
    flat[rows, :] = value


def stream_plane(g, out, slot, count, x, clamp):
    lane = lax.broadcasted_iota(jnp.int32, (ROWS, LANES), 1)
    low, high = lane == 0, lane == LANES - 1
    ztiles = g.shape[3]

    def body(step, carry):
        row = pl.multiple_of(step * ROWS, ROWS)
        for i in range(27):
            cx, cy, cz = i // 9 - 1, i // 3 % 3 - 1, i % 3 - 1
            source = x + 1 - cx
            if clamp is not None and cx == -1:
                source = jnp.where(clamp, jnp.minimum(source, count), source)
            tiles = [g[i // 9, i % 9, source, z, pl.ds(TOP - cy + row, ROWS), :] for z in range(ztiles)]
            if cz:
                j = 26 - i
                wall = 0 if cz == 1 else ztiles - 1
                bounced = g[j // 9, j % 9, x + 1, wall, pl.ds(pl.multiple_of(TOP + row, ROWS), ROWS), :]
                moved = [pltpu.roll(tile, 1 if cz == 1 else LANES - 1, 1) for tile in tiles]
                if cz == 1:
                    tiles = [jnp.where(low, moved[z - 1] if z else bounced, moved[z]) for z in range(ztiles)]
                else:
                    tiles = [
                        jnp.where(high, moved[z + 1] if z < ztiles - 1 else bounced, moved[z]) for z in range(ztiles)
                    ]
            for z in range(ztiles):
                out[slot, i, pl.ds(row, ROWS), pl.ds(z * LANES, LANES)] = tiles[z]
        return carry

    lax.fori_loop(0, out.shape[2] // ROWS, body, 0)


def exchange(
    size,
    rates_hbm,
    prec_hbm,
    main_hbm,
    cell_hbm,
    main_g,
    prec_g,
    main_mid,
    prec_mid,
    main_in,
    prec_in,
    cell_in,
    table,
    main_out_y,
    main_got_y,
    prec_out_y,
    prec_got_y,
    packet,
    packet_x,
    packet_y,
    inlet_c,
    main_relay,
    prec_relay,
    inlet_relay,
    load_sem,
    cell_sem,
    main_send,
    main_recv,
    prec_send,
    prec_recv,
    packet_send,
    packet_recv,
    inlet_send,
    inlet_recv,
    relay_recv,
    late_ready,
    near_ready,
    rates,
    rates_sem,
):
    nx, ny = size
    gx, gy = lax.axis_index("gx"), lax.axis_index("gy")
    main_x, main_y = main_in.shape[1], main_in.shape[2]
    prec_x, prec_y = prec_in.shape[1], prec_in.shape[2]
    ztiles = main_g.shape[3]
    first, last = gx == 0, gx == nx - 1
    inner_first, inner_last = jnp.logical_not(first), jnp.logical_not(last)
    east, west = lax.rem(gx + 1, nx), lax.rem(gx + nx - 1, nx)
    north, south = lax.rem(gy + 1, ny), lax.rem(gy + ny - 1, ny)
    half = ny // 2

    place = lax.rem(gx, GROUP)
    up_source = jnp.logical_and(place == GROUP - 1, inner_last)
    down_source = jnp.logical_and(place == 0, inner_first)
    up_relay = jnp.logical_and(place == 0, gx + GROUP < nx)
    down_relay = jnp.logical_and(place == GROUP - 1, gx - GROUP >= 0)
    crossing = jnp.logical_or(up_source, down_source)
    up_second = place == GROUP - 2
    down_second = jnp.logical_and(place == 1, gx >= 2)
    second = jnp.logical_or(up_second, down_second)
    second_to = jnp.where(up_second, lax.rem(gx + 2, nx), gx - 2)
    relaying = jnp.logical_or(up_relay, down_relay)
    relay_from = jnp.where(up_relay, gx + GROUP - 1, gx - GROUP + 1)
    relay_to = jnp.where(up_relay, gx + GROUP, gx - GROUP)
    relay_of = jnp.where(up_source, gx - GROUP + 1, gx + GROUP - 1)
    relay_back = jnp.where(down_source, gx - GROUP, gx + GROUP)

    passing = gx == nx - GROUP
    odd = lax.rem(gy, 2) == 1
    inlet_block = lax.div(gy, 2)
    corner_block = jnp.where(odd, lax.rem(lax.div(gy + 1, 2), half), lax.rem(lax.div(gy, 2) + half - 1, half))

    straight = jnp.logical_and(last, lax.rem(gy, 4) == 0)
    passing_face = jnp.logical_and(gx == nx - 2, lax.rem(gy, 4) != 0)

    holding = gx == GROUP - 1
    beside_last = gx == nx - 2
    below_last = gx == nx - 1 - GROUP
    barrier = pltpu.get_barrier_semaphore()

    def greet(device):
        pl.semaphore_signal(barrier, inc=1, device_id=device, device_id_type=MESH)

    greet((west, gy))

    @pl.when(last)
    def _():
        greet((west, south))
        greet((west, north))
        greet((gx - GROUP, gy))

    @pl.when(inner_last)
    def _():
        greet((gx, south))
        greet((gx, north))

        greet((east, gy))

    @pl.when(place == 0)
    def _():
        greet((lax.rem(gx + nx - 2, nx), gy))

    @pl.when(up_source)
    def _():
        greet((gx + 2, gy))

    @pl.when(relaying)
    def _():
        greet((relay_from, gy))

    @pl.when(jnp.logical_and(crossing, jnp.logical_not(below_last)))
    def _():
        greet((relay_back, gy))

    @pl.when(jnp.logical_or(passing, holding))
    def _():
        greet((nx - 1, gy))

    @pl.when(holding)
    def _():
        greet((0, gy))

    @pl.when(first)
    def _():
        source = jnp.where(gy < half, nx - 1, nx - GROUP)
        greet((source, lax.rem(2 * gy, ny)))
        greet((source, lax.rem(2 * gy + 1, ny)))
        greet((nx - 1, lax.rem(2 * gy + ny - 1, ny)))
        greet((nx - 1, lax.rem(2 * gy + 2, ny)))
        greet((nx - 1, south))
        greet((nx - 1, north))

    def one_if(condition):
        return jnp.where(condition, 1, 0)

    greetings = 3 + one_if(inner_first) + one_if(relaying) + one_if(crossing) + one_if(passing) + one_if(second)
    greetings = greetings + one_if(first)
    greetings = jnp.where(last, 9, greetings + 2 * one_if(beside_last) + one_if(below_last))

    def main_load(x):
        return pltpu.make_async_copy(main_hbm.at[:, x], main_in.at[:, x], load_sem.at[x])

    def prec_load(x):
        return pltpu.make_async_copy(prec_hbm.at[:, x], prec_in.at[:, x], load_sem.at[main_x + x])

    cell_load = pltpu.make_async_copy(cell_hbm, cell_in, cell_sem)
    rates_load = pltpu.make_async_copy(rates_hbm, rates, rates_sem)
    rates_load.start()
    prec_load(prec_x - 1).start()
    cell_load.start()
    main_load(main_x - 1).start()
    main_load(0).start()
    prec_load(0).start()
    for x in range(1, main_x - 1):
        main_load(x).start()
    for x in range(1, prec_x - 1):
        prec_load(x).start()

    @pl.when(last)
    def _():
        pl.semaphore_wait(barrier, greetings)
        pl.semaphore_signal(late_ready, inc=1, device_id=(0, gy), device_id_type=MESH)
        pl.semaphore_signal(late_ready, inc=1, device_id=(GROUP - 1, gy), device_id_type=MESH)

    rates_load.wait()
    for k in range(27):
        rate = rates[k]
        kept = scale_of(k) * (1.0 - rate)
        table[k] = jnp.full((ROWS, LANES), kept, F32)
        factor = third_of(k) * (3.0 if even_orders(k) else 1.0)
        table[27 + k] = jnp.full((ROWS, LANES), scale_of(k) * factor * rate, F32)

    def keep(k):
        return table[k]

    def gain(k):
        return table[27 + k]

    def tile_of(step):
        row = pl.multiple_of(lax.div(step, ztiles) * ROWS, ROWS)
        z = lax.rem(step, ztiles)
        return row, z, pl.multiple_of(z * LANES, LANES)

    def main_plane(x):
        def body(step, carry):
            row, z, lane = tile_of(step)
            rows, lanes = pl.ds(row, ROWS), pl.ds(lane, LANES)
            flags = cell_in[x, rows, lanes]
            g = collide([main_in[i, x, rows, lanes] for i in range(27)], keep, gain, flags == 2)
            solid = flags == 1
            for i in range(27):
                value = jnp.where(solid, main_in[26 - i, x, rows, lanes], g[i])
                main_g[i // 9, i % 9, x + 1, z, pl.ds(pl.multiple_of(TOP + row, ROWS), ROWS), :] = value
            return carry

        lax.fori_loop(0, main_y // ROWS * ztiles, body, 0)

    def prec_plane(x):
        def body(step, carry):
            row, z, lane = tile_of(step)
            rows, lanes = pl.ds(row, ROWS), pl.ds(lane, LANES)
            g = collide([prec_in[i, x, rows, lanes] for i in range(27)], keep, gain)
            for i in range(27):
                prec_g[i // 9, i % 9, x + 1, z, pl.ds(pl.multiple_of(TOP + row, ROWS), ROWS), :] = g[i]
            return carry

        lax.fori_loop(0, prec_y // ROWS * ztiles, body, 0)

    def remote(src, dst, send, recv, device):
        return pltpu.make_async_remote_copy(
            src_ref=src, dst_ref=dst, send_sem=send, recv_sem=recv, device_id=device, device_id_type=MESH
        )

    near = ztiles - ztiles // 2

    def face(g, count, rows, side, zs, send, recv):
        inner = pl.ds(TOP, rows)
        source, dest = (g.at[2, :, count, zs, inner], g.at[2, :, 0, zs, inner])
        if side:
            source, dest = (g.at[0, :, 1, zs, inner], g.at[0, :, count + 1, zs, inner])
        return source, dest, send.at[side], recv.at[side], (west if side else east, gy)

    class MainFaces:
        def __init__(self):
            whole, lower, upper = pl.ds(0, ztiles), pl.ds(0, near), pl.ds(near, ztiles // 2)
            parts = (main_g, main_x, main_y)
            self.whole = [remote(*face(*parts, side, whole, main_send, main_recv)) for side in range(2)]
            self.direct = [remote(*face(*parts, side, lower, main_send, main_recv)) for side in range(2)]
            ends = [face(*parts, side, upper, main_send, main_recv) for side in range(2)]
            self.to_relay = [
                remote(end[0], main_relay, main_send.at[4], relay_recv.at[0], (relay_of, gy)) for end in ends
            ]
            self.from_relay = [remote(main_relay, end[1], main_send.at[5], end[3], (relay_to, gy)) for end in ends]

        def run(self, side, act):
            split = down_source if side else up_source

            @pl.when(split)
            def _():
                act(self.to_relay[side])
                act(self.direct[side])

            @pl.when(jnp.logical_not(split))
            def _():
                act(self.whole[side])

    class PrecFaces:
        def __init__(self):
            ends = [face(prec_g, prec_x, prec_y, side, pl.ds(0, ztiles), prec_send, prec_recv) for side in range(2)]
            self.whole = [remote(*end) for end in ends]
            self.to_relay = [
                remote(ends[side][0], prec_relay, prec_send.at[4], relay_recv.at[1], ((west, east)[side], gy))
                for side in range(2)
            ]
            self.from_relay = [remote(prec_relay, end[1], prec_send.at[5], end[3], (second_to, gy)) for end in ends]
            self.west_to_hold = remote(
                ends[1][0], prec_relay, prec_send.at[1], relay_recv.at[1], (GROUP - 1, gy)
            )
            self.west_from_hold = remote(prec_relay, ends[1][1], prec_send.at[5], ends[1][3], (nx - 1, gy))
        def run(self, side, act):
            split = down_source if side else up_source

            @pl.when(split)
            def _():
                act(self.to_relay[side])

            @pl.when(jnp.logical_not(split))
            def _():
                act(self.whole[side])

    def start(copy):
        copy.start()

    def sent(copy):
        copy.wait_send()

    main_faces, prec_faces = MainFaces(), PrecFaces()

    def pack_corners(lattice, side):
        g, count, rows = ((main_g, main_x, main_y), (prec_g, prec_x, prec_y))[lattice]
        a, x = (0, 1) if side else (2, count)
        for up in range(2):
            row = TOP if up else TOP + rows - 1
            for e in range(3):
                for z in range(ztiles):
                    line = g[a, (0 if up else 6) + e, x, z, pl.ds(row, 1), :]
                    packet[side, up, lattice, pl.ds(e * ztiles + z, 1), :] = line

    packets_x = [
        remote(packet.at[side], packet_x.at[side], packet_send.at[side], packet_recv.at[side], ((east, west)[side], gy))
        for side in range(2)
    ]
    packets_y = [
        remote(
            packet_x.at[:, up], packet_y.at[up], packet_send.at[2 + up], packet_recv.at[2 + up], (gx, (north, south)[up])
        )
        for up in range(2)
    ]

    wrap_corners = [
        remote(
            packet.at[0, up, 1], packet_y.at[up, 0, 1], inlet_send.at[4 + up], inlet_recv.at[2 + up],
            (0, (north, south)[up]),
        )
        for up in range(2)
    ]
    west_packets_y = [
        remote(
            packet_x.at[1, up], packet_y.at[up, 1], packet_send.at[2 + up], packet_recv.at[2 + up],
            (gx, (north, south)[up]),
        )
        for up in range(2)
    ]

    inlet_rows = pl.ds(pl.multiple_of(TOP + lax.rem(gy, 2) * prec_y, ROWS), prec_y)
    outlet = prec_g.at[2, :, prec_x, :, pl.ds(TOP, prec_y)]
    inlet_direct = remote(
        outlet, main_g.at[2, :, 0, :, inlet_rows], inlet_send.at[0], main_recv.at[0], (0, inlet_block)
    )
    inlet_to_relay = remote(outlet, inlet_relay, inlet_send.at[1], relay_recv.at[2], (nx - GROUP, gy))
    inlet_from_relay = remote(
        inlet_relay, main_g.at[2, :, 0, :, inlet_rows], inlet_send.at[0], main_recv.at[0], (0, inlet_block + half)
    )
    inlet_corners = [
        [
            remote(
                packet.at[0, up, 1], inlet_c.at[up], inlet_send.at[2 + target], inlet_recv.at[up],
                (0, corner_block + target * half),
            )
            for target in range(2)
        ]
        for up in range(2)
    ]

    def inlet_run(act):
        act(wrap_corners[0])
        act(wrap_corners[1])
        for up, chosen in ((0, odd), (1, jnp.logical_not(odd))):

            @pl.when(chosen)
            def _():
                act(inlet_corners[up][0])
                act(inlet_corners[up][1])

        act(inlet_to_relay)

        @pl.when(jnp.logical_not(straight))
        def _():
            act(prec_faces.to_relay[0])

        act(inlet_direct)

        @pl.when(straight)
        def _():
            act(prec_faces.whole[0])

    prec_load(prec_x - 1).wait()
    prec_plane(prec_x - 1)
    pack_corners(1, 0)

    @pl.when(last)
    def _():
        inlet_run(start)

    main_load(main_x - 1).wait()
    cell_load.wait()
    main_plane(main_x - 1)
    pack_corners(0, 0)

    @pl.when(inner_last)
    def _():
        pl.semaphore_wait(barrier, greetings)

    def ready(device):
        pl.semaphore_signal(near_ready, inc=1, device_id=device, device_id_type=MESH)

    @pl.when(beside_last)
    def _():
        for row in (gy, south, north):
            ready((nx - 1, row))

    @pl.when(below_last)
    def _():
        ready((nx - 1, gy))

    @pl.when(inner_last)
    def _():
        packets_x[0].start()

    @pl.when(jnp.logical_and(inner_last, jnp.logical_not(down_source)))
    def _():
        main_faces.run(0, start)
        prec_faces.run(0, start)

    main_load(0).wait()
    main_plane(0)
    pack_corners(0, 1)
    prec_load(0).wait()
    prec_plane(0)
    pack_corners(1, 1)

    @pl.when(last)
    def _():
        pl.semaphore_wait(near_ready, 4)

    @pl.when(inner_first)
    def _():
        packets_x[1].start()
        prec_faces.run(1, start)
        main_faces.run(1, start)

    @pl.when(first)
    def _():
        prec_faces.west_to_hold.start()

    @pl.when(down_source)
    def _():
        main_faces.run(0, start)
        prec_faces.run(0, start)

    def prec_rest(x, carry):
        prec_load(x).wait()
        prec_plane(x)
        return carry

    lax.fori_loop(1, prec_x - 1, prec_rest, 0)

    def pack(g, count, rows, out_y):
        for side in range(2):
            row = TOP + rows - 1 if side == 0 else TOP
            for a in range(3):
                for e in range(3):
                    i = 9 * a + (6 if side == 0 else 0) + e
                    for part in range(count * ztiles // ROWS):
                        out_y[side, 3 * a + e, pl.ds(part * ROWS, ROWS), :] = load_across(g, i, part, row)

    def y_copies(out_y, got_y, send, recv):
        return [
            remote(out_y.at[side], got_y.at[side], send.at[2 + side], recv.at[2 + side], (gx, (north, south)[side]))
            for side in range(2)
        ]

    pack(prec_g, prec_x, prec_y, prec_out_y)
    prec_y_copies = y_copies(prec_out_y, prec_got_y, prec_send, prec_recv)
    main_y_copies = y_copies(main_out_y, main_got_y, main_send, main_recv)
    for copy in prec_y_copies:
        copy.start()

    def main_rest(x, carry):
        main_load(x).wait()
        main_plane(x)
        return carry

    lax.fori_loop(1, main_x // 2, main_rest, 0)

    @pl.when(passing)
    def _():
        inlet_to_relay.wait_recv()
        inlet_from_relay.start()

    @pl.when(passing_face)
    def _():
        prec_faces.to_relay[0].wait_recv()
        prec_faces.from_relay[0].start()

    lax.fori_loop(main_x // 2, main_x - 1, main_rest, 0)
    pack(main_g, main_x, main_y, main_out_y)
    for copy in main_y_copies:
        copy.start()

    @pl.when(relaying)
    def _():
        main_faces.to_relay[0].wait_recv()

    @pl.when(up_relay)
    def _():
        main_faces.from_relay[0].start()

    @pl.when(down_relay)
    def _():
        main_faces.from_relay[1].start()

    @pl.when(jnp.logical_and(second, jnp.logical_not(beside_last)))
    def _():
        prec_faces.to_relay[0].wait_recv()

    @pl.when(jnp.logical_and(up_second, jnp.logical_not(beside_last)))
    def _():
        prec_faces.from_relay[0].start()

    @pl.when(down_second)
    def _():
        prec_faces.from_relay[1].start()

    packets_x[1].wait_recv()

    @pl.when(inner_first)
    def _():
        packets_x[0].wait_recv()
        for up in range(2):
            packets_y[up].start()

    @pl.when(first)
    def _():
        for up in range(2):
            west_packets_y[up].start()

    def unpack(g, count, rows, got_y):
        for side in range(2):
            row = TOP - 1 if side == 0 else TOP + rows
            for a in range(3):
                for e in range(3):
                    i = 9 * a + (6 if side == 0 else 0) + e
                    for part in range(count * ztiles // ROWS):
                        store_across(g, i, part, row, got_y[side, 3 * a + e, pl.ds(part * ROWS, ROWS), :])

    def unpack_corner(lattice, side, up, tile):
        g, count, rows = ((main_g, main_x, main_y), (prec_g, prec_x, prec_y))[lattice]
        a, x = (0, count + 1) if side else (2, 0)
        row = TOP + rows if up else TOP - 1
        for e in range(3):
            for z in range(ztiles):
                g[a, (0 if up else 6) + e, x, z, pl.ds(row, 1), :] = tile[pl.ds(e * ztiles + z, 1), :]

    for side in range(2):
        prec_y_copies[side].wait_recv()
    unpack(prec_g, prec_x, prec_y, prec_got_y)
    for side in range(2):
        main_y_copies[side].wait_recv()
    unpack(main_g, main_x, main_y, main_got_y)

    def main_middle(x, carry):
        stream_plane(main_g, main_mid, x - 1, main_x, x, None)
        return carry

    def prec_middle(x, carry):
        stream_plane(prec_g, prec_mid, x - 1, prec_x, x, None)
        return carry

    lax.fori_loop(1, main_x - 1, main_middle, 0)
    lax.fori_loop(1, prec_x - 1, prec_middle, 0)

    @pl.when(first)
    def _():
        pl.semaphore_wait(late_ready, 1)
        packets_x[1].start()

    @pl.when(holding)
    def _():
        prec_faces.west_to_hold.wait_recv()
        pl.semaphore_wait(late_ready, 1)
        prec_faces.west_from_hold.start()

    for up in range(2):

        @pl.when(inner_first)
        def _():
            packets_y[up].wait_recv()
            unpack_corner(0, 0, up, packet_y.at[up, 0, 0])

        @pl.when(first)
        def _():
            west_packets_y[up].wait_recv()
            wrap_corners[up].wait_recv()
            inlet_corners[up][0].wait_recv()
            unpack_corner(0, 0, up, inlet_c.at[up])

        unpack_corner(0, 1, up, packet_y.at[up, 1, 0])
        for side in range(2):
            unpack_corner(1, side, up, packet_y.at[up, side, 1])

    prec_faces.whole[0].wait_recv()
    prec_faces.whole[1].wait_recv()
    main_faces.whole[0].wait_recv()

    @pl.when(inner_last)
    def _():
        main_faces.whole[1].wait_recv()

    for copy in [*prec_y_copies, *main_y_copies, packets_x[1]]:
        copy.wait_send()

    @pl.when(first)
    def _():
        prec_faces.west_to_hold.wait_send()

    @pl.when(holding)
    def _():
        prec_faces.west_from_hold.wait_send()

    @pl.when(inner_last)
    def _():
        prec_faces.run(0, sent)
        packets_x[0].wait_send()
        main_faces.run(0, sent)

    @pl.when(inner_first)
    def _():
        for up in range(2):
            packets_y[up].wait_send()
        main_faces.run(1, sent)
        prec_faces.run(1, sent)

    @pl.when(first)
    def _():
        for up in range(2):
            west_packets_y[up].wait_send()

    @pl.when(relaying)
    def _():
        main_faces.from_relay[0].wait_send()

    @pl.when(jnp.logical_or(passing_face, jnp.logical_and(second, jnp.logical_not(beside_last))))
    def _():
        prec_faces.from_relay[0].wait_send()

    @pl.when(passing)
    def _():
        inlet_from_relay.wait_send()

    @pl.when(last)
    def _():
        inlet_run(sent)


def stream(nx, main_g, prec_g, main_mid, prec_mid, prec_next, main_next, prec_out, main_out, prec_sem, main_sem):
    last = lax.axis_index("gx") == nx - 1
    copies = []
    for mid, dest, sem in ((main_mid, main_next, main_sem), (prec_mid, prec_next, prec_sem)):
        for x in range(1, dest.shape[1] - 1):
            copies.append(pltpu.make_async_copy(mid.at[x - 1], dest.at[:, x], sem.at[x]))
            copies[-1].start()
    for g, out, dest, sem, clamp in (
        (main_g, main_out, main_next, main_sem, last),
        (prec_g, prec_out, prec_next, prec_sem, None),
    ):
        count = dest.shape[1]
        for slot, x in enumerate((0, count - 1)):
            stream_plane(g, out, slot, count, x, clamp)
            copies.append(pltpu.make_async_copy(out.at[slot], dest.at[:, x], sem.at[x]))
            copies[-1].start()
    for copy in copies:
        copy.wait()


def solution(mesh):
    nx, ny = mesh.shape["gx"], mesh.shape["gy"]

    def shards(prec_pops, main_pops, cell_type, rates):
        main_x, main_y, depth = main_pops.shape[1:]
        prec_x, prec_y = prec_pops.shape[1:3]
        ztiles = depth // LANES
        main_shape = (3, 9, main_x + 2, ztiles, main_y + 2 * TOP, LANES)
        prec_shape = (3, 9, prec_x + 2, ztiles, prec_y + 2 * TOP, LANES)
        in_hbm = pl.BlockSpec(memory_space=pltpu.HBM)
        on_chip = pl.BlockSpec(memory_space=pltpu.VMEM)
        main_g, prec_g, main_mid, prec_mid = pl.pallas_call(
            functools.partial(exchange, (nx, ny)),
            name="exchange",
            out_shape=(
                pltpu.VMEM(main_shape, F32),
                pltpu.VMEM(prec_shape, F32),
                pltpu.VMEM((main_x - 2, 27, main_y, depth), F32),
                pltpu.VMEM((prec_x - 2, 27, prec_y, depth), F32),
            ),
            in_specs=[in_hbm] * 4,
            out_specs=(on_chip,) * 4,
            scratch_shapes=[
                pltpu.VMEM(main_pops.shape, F32),
                pltpu.VMEM(prec_pops.shape, F32),
                pltpu.VMEM(cell_type.shape, jnp.int32),
                pltpu.VMEM((54, ROWS, LANES), F32),
                pltpu.VMEM((2, 9, main_x * ztiles, LANES), F32),
                pltpu.VMEM((2, 9, main_x * ztiles, LANES), F32),
                pltpu.VMEM((2, 9, prec_x * ztiles, LANES), F32),
                pltpu.VMEM((2, 9, prec_x * ztiles, LANES), F32),
                pltpu.VMEM((2, 2, 2, ROWS, LANES), F32),
                pltpu.VMEM((2, 2, 2, ROWS, LANES), F32),
                pltpu.VMEM((2, 2, 2, ROWS, LANES), F32),
                pltpu.VMEM((2, ROWS, LANES), F32),
                pltpu.VMEM((9, ztiles // 2, main_y, LANES), F32),
                pltpu.VMEM((9, ztiles, prec_y, LANES), F32),
                pltpu.VMEM((9, ztiles, prec_y, LANES), F32),
                pltpu.SemaphoreType.DMA((main_x + prec_x,)),
                pltpu.SemaphoreType.DMA,
                pltpu.SemaphoreType.DMA((6,)),
                pltpu.SemaphoreType.DMA((4,)),
                pltpu.SemaphoreType.DMA((6,)),
                pltpu.SemaphoreType.DMA((4,)),
                pltpu.SemaphoreType.DMA((4,)),
                pltpu.SemaphoreType.DMA((4,)),
                pltpu.SemaphoreType.DMA((6,)),
                pltpu.SemaphoreType.DMA((4,)),
                pltpu.SemaphoreType.DMA((3,)),
                pltpu.SemaphoreType.REGULAR,
                pltpu.SemaphoreType.REGULAR,
                pltpu.SMEM((27,), F32),
                pltpu.SemaphoreType.DMA,
            ],
            compiler_params=pltpu.CompilerParams(
                collective_id=0, has_side_effects=True, vmem_limit_bytes=24 * 1024 * 1024
            ),
        )(*(pltpu.with_memory_space_constraint(x, pltpu.HBM) for x in (rates, prec_pops, main_pops, cell_type)))
        prec_next, main_next = pl.pallas_call(
            functools.partial(stream, nx),
            name="stream",
            out_shape=(
                jax.ShapeDtypeStruct(prec_pops.shape, F32),
                jax.ShapeDtypeStruct(main_pops.shape, F32),
            ),
            in_specs=[on_chip] * 4,
            out_specs=(in_hbm, in_hbm),
            scratch_shapes=[
                pltpu.VMEM((2, 27, prec_y, depth), F32),
                pltpu.VMEM((2, 27, main_y, depth), F32),
                pltpu.SemaphoreType.DMA((prec_x,)),
                pltpu.SemaphoreType.DMA((main_x,)),
            ],
            compiler_params=pltpu.CompilerParams(vmem_limit_bytes=24 * 1024 * 1024),
        )(main_g, prec_g, main_mid, prec_mid)
        return prec_next, main_next

    placed = (P(None, "gx", "gy", None), P(None, "gx", "gy", None), P("gx", "gy", None), P())
    return jax.shard_map(
        shards,
        mesh=mesh,
        in_specs=placed,
        out_specs=(P(None, "gx", "gy", None), P(None, "gx", "gy", None)),
        check_vma=False,
    )
```

```python
import functools

import jax
import jax.numpy as jnp
from jax import lax
from jax.experimental import pallas as pl
from jax.experimental.pallas import tpu as pltpu
from jax.sharding import PartitionSpec as P

MESH = pl.DeviceIdType.MESH
F32 = jnp.float32
LANES = 128
ROWS = 8
GROUP = 4
TOP = 8


def scale_of(moment):
    a, b, e = moment // 9, moment // 3 % 3, moment % 3
    return (0.5 if a else 1.0) * (0.5 if b else 1.0) * (0.5 if e else 1.0)


def third_of(moment):
    a, b, e = moment // 9, moment // 3 % 3, moment % 3
    return (1.0 / 3.0) ** ((a == 2) + (b == 2) + (e == 2))


def axis_triples():
    for stride in (9, 3, 1):
        for base in range(27):
            if base // stride % 3 == 0:
                yield base, base + stride, base + 2 * stride


def to_moments(f):
    m = list(f)
    for low, mid, high in axis_triples():
        total = m[high] + m[low]
        m[low], m[mid], m[high] = total + m[mid], m[high] - m[low], total
    return m


def to_populations(m):
    g = list(m)
    for low, mid, high in axis_triples():
        g[low], g[mid], g[high] = g[high] - g[mid], g[low] - (g[high] + g[high]), g[high] + g[mid]
    return g


def collide(f, keep, gain, disk=None):
    m = to_moments(f)
    rho, jx, jy, jz = m[0], m[9], m[3], m[1]
    inverse = 1.0 / rho
    ux, uy, uz = jx * inverse, jy * inverse, jz * inverse
    qx, qy, qz = jx * ux, jy * uy, jz * uz
    third = rho * (1.0 / 3.0)
    ex, ey, ez = third + qx, third + qy, third + qz
    exy, exz, eyz = ex + qy, ex + qz, ey + qz
    even = {18: ex, 6: ey, 2: ez, 24: exy, 20: exz, 8: eyz, 26: exy + qz}
    odd = {}
    for k in range(27):
        a, b, e = k // 9, k // 3 % 3, k % 3
        ones = (a == 1) + (b == 1) + (e == 1)
        if ones == 1:
            odd[k] = jx if a == 1 else jy if b == 1 else jz
        elif ones == 2:
            odd[k] = jx * uy if e != 1 else jx * uz if b != 1 else jy * uz
    out = [None] * 27
    shared = {}
    for k in range(27):
        a, b, e = k // 9, k // 3 % 3, k % 3
        if k == 0:
            out[k] = rho
        elif k in (9, 3, 1):
            out[k] = odd[k] * 0.5
        elif k == 13:
            out[k] = keep(k) * m[k]
        elif k in even:
            out[k] = keep(k) * m[k] + gain(k) * even[k]
        else:
            pair = (a == 1, b == 1, e == 1)
            if pair not in shared:
                shared[pair] = odd[k]
            out[k] = keep(k) * m[k] + gain(k) * shared[pair]
    if disk is not None:
        drag = jnp.where(disk, (-0.5 * 0.75) * jx * jnp.abs(ux), 0.0)
        out[9] = out[9] + drag * 0.5
        side = drag * (0.25 / 3.0)
        out[15] = out[15] + side
        out[11] = out[11] + side
        out[17] = out[17] + drag * (0.125 / 9.0)
    return to_populations(out)


def even_orders(k):
    a, b, e = k // 9, k // 3 % 3, k % 3
    return a != 1 and b != 1 and e != 1


def rows_across(g, i, part, row):
    planes, ztiles, pitch = g.shape[2:5]
    flat = g.reshape(27 * planes * ztiles * pitch, LANES)
    return flat, pl.ds(((i * planes + 1) * ztiles + part * ROWS) * pitch + row, ROWS, stride=pitch)


def load_across(g, i, part, row):
    flat, rows = rows_across(g, i, part, row)
    return flat[rows, :]


def store_across(g, i, part, row, value):
    flat, rows = rows_across(g, i, part, row)
    flat[rows, :] = value


def stream_plane(g, out, slot, count, x, clamp):
    lane = lax.broadcasted_iota(jnp.int32, (ROWS, LANES), 1)
    low, high = lane == 0, lane == LANES - 1
    ztiles = g.shape[3]

    def body(step, carry):
        row = pl.multiple_of(step * ROWS, ROWS)
        for i in range(27):
            cx, cy, cz = i // 9 - 1, i // 3 % 3 - 1, i % 3 - 1
            source = x + 1 - cx
            if clamp is not None and cx == -1:
                source = jnp.where(clamp, jnp.minimum(source, count), source)
            tiles = [g[i // 9, i % 9, source, z, pl.ds(TOP - cy + row, ROWS), :] for z in range(ztiles)]
            if cz:
                j = 26 - i
                wall = 0 if cz == 1 else ztiles - 1
                bounced = g[j // 9, j % 9, x + 1, wall, pl.ds(pl.multiple_of(TOP + row, ROWS), ROWS), :]
                moved = [pltpu.roll(tile, 1 if cz == 1 else LANES - 1, 1) for tile in tiles]
                if cz == 1:
                    tiles = [jnp.where(low, moved[z - 1] if z else bounced, moved[z]) for z in range(ztiles)]
                else:
                    tiles = [
                        jnp.where(high, moved[z + 1] if z < ztiles - 1 else bounced, moved[z]) for z in range(ztiles)
                    ]
            for z in range(ztiles):
                out[slot, i, pl.ds(row, ROWS), pl.ds(z * LANES, LANES)] = tiles[z]
        return carry

    lax.fori_loop(0, out.shape[2] // ROWS, body, 0)


def exchange(
    size,
    rates_hbm,
    prec_hbm,
    main_hbm,
    cell_hbm,
    main_g,
    prec_g,
    main_mid,
    prec_mid,
    main_in,
    prec_in,
    cell_in,
    table,
    main_out_y,
    main_got_y,
    prec_out_y,
    prec_got_y,
    packet,
    packet_x,
    packet_y,
    inlet_c,
    main_relay,
    prec_relay,
    inlet_relay,
    load_sem,
    cell_sem,
    main_send,
    main_recv,
    prec_send,
    prec_recv,
    packet_send,
    packet_recv,
    inlet_send,
    inlet_recv,
    relay_recv,
    late_ready,
    near_ready,
    rates,
    rates_sem,
):
    nx, ny = size
    gx, gy = lax.axis_index("gx"), lax.axis_index("gy")
    main_x, main_y = main_in.shape[1], main_in.shape[2]
    prec_x, prec_y = prec_in.shape[1], prec_in.shape[2]
    ztiles = main_g.shape[3]
    first, last = gx == 0, gx == nx - 1
    inner_first, inner_last = jnp.logical_not(first), jnp.logical_not(last)
    east, west = lax.rem(gx + 1, nx), lax.rem(gx + nx - 1, nx)
    north, south = lax.rem(gy + 1, ny), lax.rem(gy + ny - 1, ny)
    half = ny // 2

    place = lax.rem(gx, GROUP)
    up_source = jnp.logical_and(place == GROUP - 1, inner_last)
    down_source = jnp.logical_and(place == 0, inner_first)
    up_relay = jnp.logical_and(place == 0, gx + GROUP < nx)
    down_relay = jnp.logical_and(place == GROUP - 1, gx - GROUP >= 0)
    crossing = jnp.logical_or(up_source, down_source)
    up_second = place == GROUP - 2
    down_second = jnp.logical_and(place == 1, gx >= 2)
    second = jnp.logical_or(up_second, down_second)
    second_to = jnp.where(up_second, lax.rem(gx + 2, nx), gx - 2)
    relaying = jnp.logical_or(up_relay, down_relay)
    relay_from = jnp.where(up_relay, gx + GROUP - 1, gx - GROUP + 1)
    relay_to = jnp.where(up_relay, gx + GROUP, gx - GROUP)
    relay_of = jnp.where(up_source, gx - GROUP + 1, gx + GROUP - 1)
    relay_back = jnp.where(down_source, gx - GROUP, gx + GROUP)

    passing = gx == nx - GROUP
    odd = lax.rem(gy, 2) == 1
    inlet_block = lax.div(gy, 2)
    corner_block = jnp.where(odd, lax.rem(lax.div(gy + 1, 2), half), lax.rem(lax.div(gy, 2) + half - 1, half))

    straight_row = jnp.logical_and(lax.rem(gy, 4) == 0, gy > 0)
    straight = jnp.logical_and(last, straight_row)
    passing_face = jnp.logical_and(gx == nx - 2, jnp.logical_not(straight_row))

    holding = gx == GROUP - 1
    beside_last = gx == nx - 2
    below_last = gx == nx - 1 - GROUP
    barrier = pltpu.get_barrier_semaphore()

    def greet(device):
        pl.semaphore_signal(barrier, inc=1, device_id=device, device_id_type=MESH)

    greet((west, gy))

    @pl.when(last)
    def _():
        greet((west, south))
        greet((west, north))
        greet((gx - GROUP, gy))

    @pl.when(inner_last)
    def _():
        greet((gx, south))
        greet((gx, north))

        greet((east, gy))

    @pl.when(place == 0)
    def _():
        greet((lax.rem(gx + nx - 2, nx), gy))

    @pl.when(up_source)
    def _():
        greet((gx + 2, gy))

    @pl.when(relaying)
    def _():
        greet((relay_from, gy))

    @pl.when(jnp.logical_and(crossing, jnp.logical_not(below_last)))
    def _():
        greet((relay_back, gy))

    @pl.when(jnp.logical_or(passing, holding))
    def _():
        greet((nx - 1, gy))

    @pl.when(holding)
    def _():
        greet((0, gy))

    @pl.when(first)
    def _():
        source = jnp.where(gy < half, nx - 1, nx - GROUP)
        greet((source, lax.rem(2 * gy, ny)))
        greet((source, lax.rem(2 * gy + 1, ny)))
        greet((nx - 1, lax.rem(2 * gy + ny - 1, ny)))
        greet((nx - 1, lax.rem(2 * gy + 2, ny)))
        greet((nx - 1, south))
        greet((nx - 1, north))

    def one_if(condition):
        return jnp.where(condition, 1, 0)

    greetings = 3 + one_if(inner_first) + one_if(relaying) + one_if(crossing) + one_if(passing) + one_if(second)
    greetings = greetings + one_if(first)
    greetings = jnp.where(last, 9, greetings + 2 * one_if(beside_last) + one_if(below_last))

    def main_load(x):
        return pltpu.make_async_copy(main_hbm.at[:, x], main_in.at[:, x], load_sem.at[x])

    def prec_load(x):
        return pltpu.make_async_copy(prec_hbm.at[:, x], prec_in.at[:, x], load_sem.at[main_x + x])

    cell_load = pltpu.make_async_copy(cell_hbm, cell_in, cell_sem)
    rates_load = pltpu.make_async_copy(rates_hbm, rates, rates_sem)
    rates_load.start()
    prec_load(prec_x - 1).start()
    cell_load.start()
    main_load(main_x - 1).start()
    main_load(0).start()
    prec_load(0).start()
    for x in range(1, main_x - 1):
        main_load(x).start()
    for x in range(1, prec_x - 1):
        prec_load(x).start()

    @pl.when(last)
    def _():
        pl.semaphore_wait(barrier, greetings)
        pl.semaphore_signal(late_ready, inc=1, device_id=(0, gy), device_id_type=MESH)
        pl.semaphore_signal(late_ready, inc=1, device_id=(GROUP - 1, gy), device_id_type=MESH)

    rates_load.wait()
    for k in range(27):
        rate = rates[k]
        kept = scale_of(k) * (1.0 - rate)
        table[k] = jnp.full((ROWS, LANES), kept, F32)
        factor = third_of(k) * (3.0 if even_orders(k) else 1.0)
        table[27 + k] = jnp.full((ROWS, LANES), scale_of(k) * factor * rate, F32)

    def keep(k):
        return table[k]

    def gain(k):
        return table[27 + k]

    def tile_of(step):
        row = pl.multiple_of(lax.div(step, ztiles) * ROWS, ROWS)
        z = lax.rem(step, ztiles)
        return row, z, pl.multiple_of(z * LANES, LANES)

    def main_plane(x):
        def body(step, carry):
            row, z, lane = tile_of(step)
            rows, lanes = pl.ds(row, ROWS), pl.ds(lane, LANES)
            flags = cell_in[x, rows, lanes]
            g = collide([main_in[i, x, rows, lanes] for i in range(27)], keep, gain, flags == 2)
            solid = flags == 1
            for i in range(27):
                value = jnp.where(solid, main_in[26 - i, x, rows, lanes], g[i])
                main_g[i // 9, i % 9, x + 1, z, pl.ds(pl.multiple_of(TOP + row, ROWS), ROWS), :] = value
            return carry

        lax.fori_loop(0, main_y // ROWS * ztiles, body, 0)

    def prec_plane(x):
        def body(step, carry):
            row, z, lane = tile_of(step)
            rows, lanes = pl.ds(row, ROWS), pl.ds(lane, LANES)
            g = collide([prec_in[i, x, rows, lanes] for i in range(27)], keep, gain)
            for i in range(27):
                prec_g[i // 9, i % 9, x + 1, z, pl.ds(pl.multiple_of(TOP + row, ROWS), ROWS), :] = g[i]
            return carry

        lax.fori_loop(0, prec_y // ROWS * ztiles, body, 0)

    def remote(src, dst, send, recv, device):
        return pltpu.make_async_remote_copy(
            src_ref=src, dst_ref=dst, send_sem=send, recv_sem=recv, device_id=device, device_id_type=MESH
        )

    near = ztiles - ztiles // 2

    def face(g, count, rows, side, zs, send, recv):
        inner = pl.ds(TOP, rows)
        source, dest = (g.at[2, :, count, zs, inner], g.at[2, :, 0, zs, inner])
        if side:
            source, dest = (g.at[0, :, 1, zs, inner], g.at[0, :, count + 1, zs, inner])
        return source, dest, send.at[side], recv.at[side], (west if side else east, gy)

    class MainFaces:
        def __init__(self):
            whole, lower, upper = pl.ds(0, ztiles), pl.ds(0, near), pl.ds(near, ztiles // 2)
            parts = (main_g, main_x, main_y)
            self.whole = [remote(*face(*parts, side, whole, main_send, main_recv)) for side in range(2)]
            self.direct = [remote(*face(*parts, side, lower, main_send, main_recv)) for side in range(2)]
            ends = [face(*parts, side, upper, main_send, main_recv) for side in range(2)]
            self.to_relay = [
                remote(end[0], main_relay, main_send.at[4], relay_recv.at[0], (relay_of, gy)) for end in ends
            ]
            self.from_relay = [remote(main_relay, end[1], main_send.at[5], end[3], (relay_to, gy)) for end in ends]

        def run(self, side, act):
            split = down_source if side else up_source

            @pl.when(split)
            def _():
                act(self.to_relay[side])
                act(self.direct[side])

            @pl.when(jnp.logical_not(split))
            def _():
                act(self.whole[side])

    class PrecFaces:
        def __init__(self):
            ends = [face(prec_g, prec_x, prec_y, side, pl.ds(0, ztiles), prec_send, prec_recv) for side in range(2)]
            self.whole = [remote(*end) for end in ends]
            self.to_relay = [
                remote(ends[side][0], prec_relay, prec_send.at[4], relay_recv.at[1], ((west, east)[side], gy))
                for side in range(2)
            ]
            self.from_relay = [remote(prec_relay, end[1], prec_send.at[5], end[3], (second_to, gy)) for end in ends]
            self.west_to_hold = remote(
                ends[1][0], prec_relay, prec_send.at[1], relay_recv.at[1], (GROUP - 1, gy)
            )
            self.west_from_hold = remote(prec_relay, ends[1][1], prec_send.at[5], ends[1][3], (nx - 1, gy))
        def run(self, side, act):
            split = down_source if side else up_source

            @pl.when(split)
            def _():
                act(self.to_relay[side])

            @pl.when(jnp.logical_not(split))
            def _():
                act(self.whole[side])

    def start(copy):
        copy.start()

    def sent(copy):
        copy.wait_send()

    main_faces, prec_faces = MainFaces(), PrecFaces()

    def pack_corners(lattice, side):
        g, count, rows = ((main_g, main_x, main_y), (prec_g, prec_x, prec_y))[lattice]
        a, x = (0, 1) if side else (2, count)
        for up in range(2):
            row = TOP if up else TOP + rows - 1
            for e in range(3):
                for z in range(ztiles):
                    line = g[a, (0 if up else 6) + e, x, z, pl.ds(row, 1), :]
                    packet[side, up, lattice, pl.ds(e * ztiles + z, 1), :] = line

    packets_x = [
        remote(packet.at[side], packet_x.at[side], packet_send.at[side], packet_recv.at[side], ((east, west)[side], gy))
        for side in range(2)
    ]
    packets_y = [
        remote(
            packet_x.at[:, up], packet_y.at[up], packet_send.at[2 + up], packet_recv.at[2 + up], (gx, (north, south)[up])
        )
        for up in range(2)
    ]

    wrap_corners = [
        remote(
            packet.at[0, up, 1], packet_y.at[up, 0, 1], inlet_send.at[4 + up], inlet_recv.at[2 + up],
            (0, (north, south)[up]),
        )
        for up in range(2)
    ]
    west_packets_y = [
        remote(
            packet_x.at[1, up], packet_y.at[up, 1], packet_send.at[2 + up], packet_recv.at[2 + up],
            (gx, (north, south)[up]),
        )
        for up in range(2)
    ]

    inlet_rows = pl.ds(pl.multiple_of(TOP + lax.rem(gy, 2) * prec_y, ROWS), prec_y)
    outlet = prec_g.at[2, :, prec_x, :, pl.ds(TOP, prec_y)]
    inlet_direct = remote(
        outlet, main_g.at[2, :, 0, :, inlet_rows], inlet_send.at[0], main_recv.at[0], (0, inlet_block)
    )
    inlet_to_relay = remote(outlet, inlet_relay, inlet_send.at[1], relay_recv.at[2], (nx - GROUP, gy))
    inlet_from_relay = remote(
        inlet_relay, main_g.at[2, :, 0, :, inlet_rows], inlet_send.at[0], main_recv.at[0], (0, inlet_block + half)
    )
    inlet_corners = [
        [
            remote(
                packet.at[0, up, 1], inlet_c.at[up], inlet_send.at[2 + target], inlet_recv.at[up],
                (0, corner_block + target * half),
            )
            for target in range(2)
        ]
        for up in range(2)
    ]

    def inlet_run(act):
        act(wrap_corners[0])
        act(wrap_corners[1])
        for up, chosen in ((0, odd), (1, jnp.logical_not(odd))):

            @pl.when(chosen)
            def _():
                act(inlet_corners[up][0])
                act(inlet_corners[up][1])

        act(inlet_direct)
        act(inlet_to_relay)

        @pl.when(jnp.logical_not(straight))
        def _():
            act(prec_faces.to_relay[0])

        @pl.when(straight)
        def _():
            act(prec_faces.whole[0])

    prec_load(prec_x - 1).wait()
    prec_plane(prec_x - 1)
    pack_corners(1, 0)

    @pl.when(last)
    def _():
        inlet_run(start)

    main_load(main_x - 1).wait()
    cell_load.wait()
    main_plane(main_x - 1)
    pack_corners(0, 0)

    @pl.when(inner_last)
    def _():
        pl.semaphore_wait(barrier, greetings)

    def ready(device):
        pl.semaphore_signal(near_ready, inc=1, device_id=device, device_id_type=MESH)

    @pl.when(beside_last)
    def _():
        for row in (gy, south, north):
            ready((nx - 1, row))

    @pl.when(below_last)
    def _():
        ready((nx - 1, gy))

    @pl.when(inner_last)
    def _():
        packets_x[0].start()

    @pl.when(jnp.logical_and(inner_last, jnp.logical_not(down_source)))
    def _():
        main_faces.run(0, start)
        prec_faces.run(0, start)

    main_load(0).wait()
    main_plane(0)
    pack_corners(0, 1)
    prec_load(0).wait()
    prec_plane(0)
    pack_corners(1, 1)

    @pl.when(last)
    def _():
        pl.semaphore_wait(near_ready, 4)

    @pl.when(inner_first)
    def _():
        packets_x[1].start()
        prec_faces.run(1, start)
        main_faces.run(1, start)

    @pl.when(first)
    def _():
        prec_faces.west_to_hold.start()

    @pl.when(down_source)
    def _():
        main_faces.run(0, start)
        prec_faces.run(0, start)

    def prec_rest(x, carry):
        prec_load(x).wait()
        prec_plane(x)
        return carry

    lax.fori_loop(1, prec_x - 1, prec_rest, 0)

    def pack(g, count, rows, out_y):
        for side in range(2):
            row = TOP + rows - 1 if side == 0 else TOP
            for a in range(3):
                for e in range(3):
                    i = 9 * a + (6 if side == 0 else 0) + e
                    for part in range(count * ztiles // ROWS):
                        out_y[side, 3 * a + e, pl.ds(part * ROWS, ROWS), :] = load_across(g, i, part, row)

    def y_copies(out_y, got_y, send, recv):
        return [
            remote(out_y.at[side], got_y.at[side], send.at[2 + side], recv.at[2 + side], (gx, (north, south)[side]))
            for side in range(2)
        ]

    pack(prec_g, prec_x, prec_y, prec_out_y)
    prec_y_copies = y_copies(prec_out_y, prec_got_y, prec_send, prec_recv)
    main_y_copies = y_copies(main_out_y, main_got_y, main_send, main_recv)
    for copy in prec_y_copies:
        copy.start()

    def main_rest(x, carry):
        main_load(x).wait()
        main_plane(x)
        return carry

    lax.fori_loop(1, main_x // 2, main_rest, 0)

    @pl.when(passing)
    def _():
        inlet_to_relay.wait_recv()
        inlet_from_relay.start()

    @pl.when(passing_face)
    def _():
        prec_faces.to_relay[0].wait_recv()
        prec_faces.from_relay[0].start()

    lax.fori_loop(main_x // 2, main_x - 1, main_rest, 0)
    pack(main_g, main_x, main_y, main_out_y)
    for copy in main_y_copies:
        copy.start()

    @pl.when(relaying)
    def _():
        main_faces.to_relay[0].wait_recv()

    @pl.when(up_relay)
    def _():
        main_faces.from_relay[0].start()

    @pl.when(down_relay)
    def _():
        main_faces.from_relay[1].start()

    @pl.when(jnp.logical_and(second, jnp.logical_not(beside_last)))
    def _():
        prec_faces.to_relay[0].wait_recv()

    @pl.when(jnp.logical_and(up_second, jnp.logical_not(beside_last)))
    def _():
        prec_faces.from_relay[0].start()

    @pl.when(down_second)
    def _():
        prec_faces.from_relay[1].start()

    packets_x[1].wait_recv()

    @pl.when(inner_first)
    def _():
        packets_x[0].wait_recv()
        for up in range(2):
            packets_y[up].start()

    @pl.when(first)
    def _():
        for up in range(2):
            west_packets_y[up].start()

    def unpack(g, count, rows, got_y):
        for side in range(2):
            row = TOP - 1 if side == 0 else TOP + rows
            for a in range(3):
                for e in range(3):
                    i = 9 * a + (6 if side == 0 else 0) + e
                    for part in range(count * ztiles // ROWS):
                        store_across(g, i, part, row, got_y[side, 3 * a + e, pl.ds(part * ROWS, ROWS), :])

    def unpack_corner(lattice, side, up, tile):
        g, count, rows = ((main_g, main_x, main_y), (prec_g, prec_x, prec_y))[lattice]
        a, x = (0, count + 1) if side else (2, 0)
        row = TOP + rows if up else TOP - 1
        for e in range(3):
            for z in range(ztiles):
                g[a, (0 if up else 6) + e, x, z, pl.ds(row, 1), :] = tile[pl.ds(e * ztiles + z, 1), :]

    for side in range(2):
        prec_y_copies[side].wait_recv()
    unpack(prec_g, prec_x, prec_y, prec_got_y)
    for side in range(2):
        main_y_copies[side].wait_recv()
    unpack(main_g, main_x, main_y, main_got_y)

    def main_middle(x, carry):
        stream_plane(main_g, main_mid, x - 1, main_x, x, None)
        return carry

    def prec_middle(x, carry):
        stream_plane(prec_g, prec_mid, x - 1, prec_x, x, None)
        return carry

    lax.fori_loop(1, main_x - 1, main_middle, 0)
    lax.fori_loop(1, prec_x - 1, prec_middle, 0)

    @pl.when(first)
    def _():
        pl.semaphore_wait(late_ready, 1)
        packets_x[1].start()

    @pl.when(holding)
    def _():
        prec_faces.west_to_hold.wait_recv()
        pl.semaphore_wait(late_ready, 1)
        prec_faces.west_from_hold.start()

    for up in range(2):

        @pl.when(inner_first)
        def _():
            packets_y[up].wait_recv()
            unpack_corner(0, 0, up, packet_y.at[up, 0, 0])

        @pl.when(first)
        def _():
            west_packets_y[up].wait_recv()
            wrap_corners[up].wait_recv()
            inlet_corners[up][0].wait_recv()
            unpack_corner(0, 0, up, inlet_c.at[up])

        unpack_corner(0, 1, up, packet_y.at[up, 1, 0])
        for side in range(2):
            unpack_corner(1, side, up, packet_y.at[up, side, 1])

    prec_faces.whole[0].wait_recv()
    prec_faces.whole[1].wait_recv()
    main_faces.whole[0].wait_recv()

    @pl.when(inner_last)
    def _():
        main_faces.whole[1].wait_recv()

    for copy in [*prec_y_copies, *main_y_copies, packets_x[1]]:
        copy.wait_send()

    @pl.when(first)
    def _():
        prec_faces.west_to_hold.wait_send()

    @pl.when(holding)
    def _():
        prec_faces.west_from_hold.wait_send()

    @pl.when(inner_last)
    def _():
        prec_faces.run(0, sent)
        packets_x[0].wait_send()
        main_faces.run(0, sent)

    @pl.when(inner_first)
    def _():
        for up in range(2):
            packets_y[up].wait_send()
        main_faces.run(1, sent)
        prec_faces.run(1, sent)

    @pl.when(first)
    def _():
        for up in range(2):
            west_packets_y[up].wait_send()

    @pl.when(relaying)
    def _():
        main_faces.from_relay[0].wait_send()

    @pl.when(jnp.logical_or(passing_face, jnp.logical_and(second, jnp.logical_not(beside_last))))
    def _():
        prec_faces.from_relay[0].wait_send()

    @pl.when(passing)
    def _():
        inlet_from_relay.wait_send()

    @pl.when(last)
    def _():
        inlet_run(sent)


def stream(nx, main_g, prec_g, main_mid, prec_mid, prec_next, main_next, prec_out, main_out, prec_sem, main_sem):
    last = lax.axis_index("gx") == nx - 1
    copies = []
    for mid, dest, sem in ((main_mid, main_next, main_sem), (prec_mid, prec_next, prec_sem)):
        for x in range(1, dest.shape[1] - 1):
            copies.append(pltpu.make_async_copy(mid.at[x - 1], dest.at[:, x], sem.at[x]))
            copies[-1].start()
    for g, out, dest, sem, clamp in (
        (main_g, main_out, main_next, main_sem, last),
        (prec_g, prec_out, prec_next, prec_sem, None),
    ):
        count = dest.shape[1]
        for slot, x in enumerate((0, count - 1)):
            stream_plane(g, out, slot, count, x, clamp)
            copies.append(pltpu.make_async_copy(out.at[slot], dest.at[:, x], sem.at[x]))
            copies[-1].start()
    for copy in copies:
        copy.wait()


def solution(mesh):
    nx, ny = mesh.shape["gx"], mesh.shape["gy"]

    def shards(prec_pops, main_pops, cell_type, rates):
        main_x, main_y, depth = main_pops.shape[1:]
        prec_x, prec_y = prec_pops.shape[1:3]
        ztiles = depth // LANES
        main_shape = (3, 9, main_x + 2, ztiles, main_y + 2 * TOP, LANES)
        prec_shape = (3, 9, prec_x + 2, ztiles, prec_y + 2 * TOP, LANES)
        in_hbm = pl.BlockSpec(memory_space=pltpu.HBM)
        on_chip = pl.BlockSpec(memory_space=pltpu.VMEM)
        main_g, prec_g, main_mid, prec_mid = pl.pallas_call(
            functools.partial(exchange, (nx, ny)),
            name="exchange",
            out_shape=(
                pltpu.VMEM(main_shape, F32),
                pltpu.VMEM(prec_shape, F32),
                pltpu.VMEM((main_x - 2, 27, main_y, depth), F32),
                pltpu.VMEM((prec_x - 2, 27, prec_y, depth), F32),
            ),
            in_specs=[in_hbm] * 4,
            out_specs=(on_chip,) * 4,
            scratch_shapes=[
                pltpu.VMEM(main_pops.shape, F32),
                pltpu.VMEM(prec_pops.shape, F32),
                pltpu.VMEM(cell_type.shape, jnp.int32),
                pltpu.VMEM((54, ROWS, LANES), F32),
                pltpu.VMEM((2, 9, main_x * ztiles, LANES), F32),
                pltpu.VMEM((2, 9, main_x * ztiles, LANES), F32),
                pltpu.VMEM((2, 9, prec_x * ztiles, LANES), F32),
                pltpu.VMEM((2, 9, prec_x * ztiles, LANES), F32),
                pltpu.VMEM((2, 2, 2, ROWS, LANES), F32),
                pltpu.VMEM((2, 2, 2, ROWS, LANES), F32),
                pltpu.VMEM((2, 2, 2, ROWS, LANES), F32),
                pltpu.VMEM((2, ROWS, LANES), F32),
                pltpu.VMEM((9, ztiles // 2, main_y, LANES), F32),
                pltpu.VMEM((9, ztiles, prec_y, LANES), F32),
                pltpu.VMEM((9, ztiles, prec_y, LANES), F32),
                pltpu.SemaphoreType.DMA((main_x + prec_x,)),
                pltpu.SemaphoreType.DMA,
                pltpu.SemaphoreType.DMA((6,)),
                pltpu.SemaphoreType.DMA((4,)),
                pltpu.SemaphoreType.DMA((6,)),
                pltpu.SemaphoreType.DMA((4,)),
                pltpu.SemaphoreType.DMA((4,)),
                pltpu.SemaphoreType.DMA((4,)),
                pltpu.SemaphoreType.DMA((6,)),
                pltpu.SemaphoreType.DMA((4,)),
                pltpu.SemaphoreType.DMA((3,)),
                pltpu.SemaphoreType.REGULAR,
                pltpu.SemaphoreType.REGULAR,
                pltpu.SMEM((27,), F32),
                pltpu.SemaphoreType.DMA,
            ],
            compiler_params=pltpu.CompilerParams(
                collective_id=0, has_side_effects=True, vmem_limit_bytes=24 * 1024 * 1024
            ),
        )(*(pltpu.with_memory_space_constraint(x, pltpu.HBM) for x in (rates, prec_pops, main_pops, cell_type)))
        prec_next, main_next = pl.pallas_call(
            functools.partial(stream, nx),
            name="stream",
            out_shape=(
                jax.ShapeDtypeStruct(prec_pops.shape, F32),
                jax.ShapeDtypeStruct(main_pops.shape, F32),
            ),
            in_specs=[on_chip] * 4,
            out_specs=(in_hbm, in_hbm),
            scratch_shapes=[
                pltpu.VMEM((2, 27, prec_y, depth), F32),
                pltpu.VMEM((2, 27, main_y, depth), F32),
                pltpu.SemaphoreType.DMA((prec_x,)),
                pltpu.SemaphoreType.DMA((main_x,)),
            ],
            compiler_params=pltpu.CompilerParams(vmem_limit_bytes=24 * 1024 * 1024),
        )(main_g, prec_g, main_mid, prec_mid)
        return prec_next, main_next

    placed = (P(None, "gx", "gy", None), P(None, "gx", "gy", None), P("gx", "gy", None), P())
    return jax.shard_map(
        shards,
        mesh=mesh,
        in_specs=placed,
        out_specs=(P(None, "gx", "gy", None), P(None, "gx", "gy", None)),
        check_vma=False,
    )
```
